256 devices in a mesh: fourier: 8 (over x, core), ex: 8 (over z), ey: 4 (over y).
Axes of the slice: x: 4, y: 4, z: 8, core: 2. Of those that a mesh axis runs over, the one named last changes fastest.
Arguments:
- forcing: float32 [128, 81, 4096], P('fourier', None, ('ex', 'ey')), may hold values from -6 to 6
- element_coef: float32 [4096], P(('ex', 'ey')), may hold values from 0.5 to 2
- schur: float32 [128, 32, 32], P('fourier'), may hold values from -12 to 20, as said below
- couple: float32 [128, 32, 49], P('fourier'), may hold values from -0.875 to 0.875
- inner_inv: float32 [128, 49, 49], P('fourier'), may hold values from -3 to 4.5, as said below
- element_cell: int32 [4096], P(('ex', 'ey')), may hold values from 0 to 127, as said below
Outputs:
- velocity: float32 [128, 81, 4096], P('fourier', None, ('ex', 'ey'))
The draws below stay inside these ranges and needn't reach their ends.
Inputs may be any that keep to these rules, and one draw needn't show every extreme that they name: `element_cell`: each aligned block of 128 entries is a permutation of 0 to 127. `schur`: each matrix is symmetric positive definite. `inner_inv`: each matrix is symmetric positive definite.
All inputs are finite; a program needn't handle non-finite values.
Results may differ from the reference program's by a relative error of at most 0.0001.
Values sent between devices are 32-bit elements; how exact they have to be, the bound alone decides.
No kernel may reach another device: no remote copies, remote signals or barrier semaphores. Data moves between devices by JAX's collectives and lax.ppermute only.
A program may use at most 64 MiB of HBM per device.

```python
import math
import jax
import jax.numpy as jnp
import numpy as np
from jax import lax

P_SIZE = 8
NZ = 128
ITERS = 3
ELX = 8
ELY = 16
NODES = 81
NB = 32
NI = 49
EL_DEV = 128
ELEMENTS = 4096
NXE = 64
NYE = 64
N_EY = 4


def draw_schur(key, part):
    first, second = jax.random.split(jax.random.fold_in(key, 11), 2)
    width = 4 * P_SIZE
    factor = jax.random.uniform(first, (NZ, width, width), jnp.float32, -math.sqrt(3.0), math.sqrt(3.0))
    shift = jnp.exp(jax.random.uniform(second, (NZ, 1, 1), jnp.float32, math.log(0.5), math.log(2.0)))
    matrix = jnp.einsum('mab,mcb->mac', factor, factor) / width + shift * jnp.eye(width, dtype=jnp.float32)
    return matrix


def draw_inner_inv(key, part):
    first, second = jax.random.split(jax.random.fold_in(key, 23), 2)
    width = (P_SIZE - 1) ** 2
    factor = jax.random.uniform(first, (NZ, width, width), jnp.float32, -math.sqrt(3.0), math.sqrt(3.0))
    shift = jax.random.uniform(second, (NZ, 1, 1), jnp.float32, 0.5, 1.5)
    return jnp.einsum('mab,mcb->mac', factor, factor) / width + shift * jnp.eye(width, dtype=jnp.float32)


def draw_element_cell(key, part):
    keys = jax.random.split(jax.random.fold_in(key, 37), ELEMENTS // EL_DEV)
    orders = jax.vmap(lambda single: jax.random.permutation(single, EL_DEV))(keys)
    return orders.reshape(-1).astype(jnp.int32)


def level_of(stream_key, extent, pieces, least, high):
    def one(position, shards_of):
        heights = jax.random.uniform(jax.random.fold_in(jax.random.fold_in(stream_key, 6), position), (shards_of,), jnp.float32, least / len(pieces), high / len(pieces))
        return jnp.repeat(jnp.exp(heights), extent[position] // shards_of).reshape((-1,) + (1,) * (len(extent) - position - 1))

    factor_of = one(*pieces[0])
    for cut in pieces[1:]:
        factor_of = factor_of * one(*cut)
    return factor_of


def normal_values(own_key, dims, scale, limit, pieces=(), kind=jnp.bfloat16):
    drawn = jax.random.normal(own_key, dims, jnp.float32) * scale
    if len(pieces) > 0:
        drawn = level_of(own_key, dims, pieces, -0.22, 0.18) * drawn
    return jnp.clip(drawn, min=-limit, max=limit).astype(kind)


def setup_inputs(seed: int = 0) -> dict:
    arg_keys = jax.random.split(jax.random.key(seed), 7)
    forcing = normal_values(arg_keys[0], (NZ, NODES, ELEMENTS), 1.0, 6.0, ((0, 8), (2, 32)), jnp.float32)
    element_coef = jnp.clip(jnp.exp(math.log(2.0) - 1.3862944 * jax.random.uniform(arg_keys[1], (ELEMENTS,), jnp.float32) ** level_of(arg_keys[1], (ELEMENTS,), ((0, 32),), -0.2, 0.2)), 0.5, 2.0)
    schur = draw_schur(jax.random.fold_in(arg_keys[6], 71), 0)
    couple = normal_values(arg_keys[3], (NZ, NB, NI), NI ** -0.5, 0.875, ((0, 8),), jnp.float32)
    inner_inv = draw_inner_inv(jax.random.fold_in(arg_keys[6], 71), 0)
    element_cell = draw_element_cell(jax.random.fold_in(arg_keys[6], 71), 0)
    return {"forcing": forcing, "element_coef": element_coef, "schur": schur, "couple": couple, "inner_inv": inner_inv, "element_cell": element_cell}


def dft_rows(length):
    row_index = jnp.arange(length)[:, None]
    plane_pos = jnp.arange(length, dtype=jnp.float32)[None, :]
    waves = ((row_index + 1) // 2).astype(jnp.float32)
    angles = 2.0 * math.pi * waves * plane_pos / length
    factor = math.sqrt(2.0 / length)
    result = jnp.where(row_index % 2 == 1, factor * jnp.cos(angles), factor * jnp.sin(angles))
    result = jnp.where(row_index == 0, 1.0 / math.sqrt(length), result)
    result = jnp.where(row_index == length - 1, jnp.cos(math.pi * plane_pos) / math.sqrt(length), result)
    return result.astype(jnp.float32)

def node_masks(row_ids, col_ids, rows_total, cols_total):
    slots = np.arange(4 * P_SIZE)
    on_left = jnp.asarray((slots == 0) | (slots >= 3 * P_SIZE))[:, None, None]
    on_right = jnp.asarray((slots >= P_SIZE) & (slots <= 2 * P_SIZE))[:, None, None]
    on_bottom = jnp.asarray(slots <= P_SIZE)[:, None, None]
    on_top = jnp.asarray((slots >= 2 * P_SIZE) & (slots <= 3 * P_SIZE))[:, None, None]
    dropped = on_left & (row_ids == 0)[None, :, None] | on_right & (row_ids == rows_total - 1)[None, :, None]
    dropped = dropped | on_bottom & (col_ids == 0)[None, None, :] | on_top & (col_ids == cols_total - 1)[None, None, :]
    keep = jnp.where(dropped, 0.0, 1.0).astype(jnp.float32)
    corner_weight = jnp.asarray(np.where(slots % P_SIZE == 0, 0.25, 0.5)).astype(jnp.float32)
    return (keep, keep * corner_weight[:, None, None])

def side_lines(values):
    return (jnp.concatenate([values[:, 0:1], values[:, 4 * P_SIZE - 1:3 * P_SIZE - 1:-1]], 1), values[:, P_SIZE:2 * P_SIZE + 1])

def add_sides(values, left_next, right_prev):
    blank = jnp.zeros((values.shape[0], P_SIZE - 1) + values.shape[2:], values.dtype)
    return values + jnp.concatenate([right_prev[:, 0:1], blank, left_next, blank, right_prev[:, P_SIZE:0:-1]], 1)

def end_lines(values):
    return (values[:, 0:P_SIZE + 1], values[:, 3 * P_SIZE:2 * P_SIZE - 1:-1])

def add_ends(values, bottom_next, top_prev):
    blank = jnp.zeros((values.shape[0], P_SIZE - 1) + values.shape[2:], values.dtype)
    return values + jnp.concatenate([top_prev, blank, bottom_next[:, ::-1], blank], 1)

def assemble(values):
    left_line, right_line = side_lines(values)
    left_next = jnp.pad(left_line[:, :, 1:], ((0, 0), (0, 0), (0, 1), (0, 0)))
    right_prev = jnp.pad(right_line[:, :, :-1], ((0, 0), (0, 0), (1, 0), (0, 0)))
    values = add_sides(values, left_next, right_prev)
    bottom_line, top_line = end_lines(values)
    bottom_next = jnp.pad(bottom_line[:, :, :, 1:], ((0, 0), (0, 0), (0, 0), (0, 1)))
    top_prev = jnp.pad(top_line[:, :, :, :-1], ((0, 0), (0, 0), (0, 0), (1, 0)))
    return add_ends(values, bottom_next, top_prev)

def reference(forcing, element_coef, schur, couple, inner_inv, element_cell):
    highest = lax.Precision.HIGHEST
    dft_table = dft_rows(NZ)
    spectral = jnp.einsum('jz,zne->jne', dft_table, forcing, precision=highest)
    block_ids = jnp.arange(ELEMENTS, dtype=jnp.int32) // EL_DEV
    grid_row = block_ids // N_EY * ELX + element_cell // ELY
    grid_col = block_ids % N_EY * ELY + element_cell % ELY
    location = (grid_row * NYE + grid_col).astype(jnp.int32)
    ordering = jnp.zeros((ELEMENTS,), jnp.int32).at[location].set(jnp.arange(ELEMENTS, dtype=jnp.int32))
    gridded = jnp.take(spectral, ordering, axis=2).reshape(NZ, NODES, NXE, NYE)
    scaling = jnp.take(element_coef, ordering).reshape(NXE, NYE)
    keep, weights = node_masks(jnp.arange(NXE), jnp.arange(NYE), NXE, NYE)

    def solve_mode(packed):
        fields, schur_mode, couple_mode, inner_mode = packed
        cycle_part = fields[:, :NB]
        inner_part = fields[:, NB:]
        condensed = cycle_part - jnp.einsum('mbi,mixy->mbxy', couple_mode, inner_part, precision=highest)
        residual = keep * assemble(condensed)

        def operator(search):
            return keep * assemble(scaling * jnp.einsum('mab,mbxy->maxy', schur_mode, search, precision=highest))

        def inner_sum(first, second):
            return lax.optimization_barrier(jnp.sum(weights * first * second, axis=(1, 2, 3)))[:, None, None, None]
        iterate = jnp.zeros_like(residual)
        search = residual
        norm_now = inner_sum(residual, residual)
        for sweep in range(ITERS):
            images = operator(search)
            step_size = norm_now / inner_sum(search, images)
            iterate = iterate + step_size * search
            residual = residual - step_size * images
            norm_next = inner_sum(residual, residual)
            search = residual + norm_next / norm_now * search
            norm_now = norm_next
        interior = jnp.einsum('mij,mjxy->mixy', inner_mode, inner_part, precision=highest) / scaling
        interior = interior - jnp.einsum('mbi,mbxy->mixy', couple_mode, iterate, precision=highest)
        return jnp.concatenate([iterate, interior], 1)
    modal = lax.map(solve_mode, (gridded[:, None], schur[:, None], couple[:, None], inner_inv[:, None]))
    modal = jnp.take(modal.reshape(NZ, NODES, ELEMENTS), location, axis=2)
    return jnp.einsum('jz,jne->zne', dft_table, modal, precision=highest)
```

```python
import math

import jax
import jax.numpy as jnp
import numpy as np
from jax import lax
from jax.experimental import pallas as pl
from jax.experimental.pallas import tpu as pltpu
from jax.sharding import PartitionSpec as P

P_SIZE = 8
NZ = 128
ELX = 8
ELY = 16
NODES = 81
NB = 32
NI = 49
EL = ELX * ELY
PADDED = 88
MODES = 16
DEEP = 3
PITCH = 24
XROWS = ELX + 2 * DEEP
XCOLS = ELY + 2 * DEEP
XL = 384
HIGHEST = lax.Precision.HIGHEST
F32 = jnp.float32


def real_transform():
    k = np.arange(NZ)[:, None]
    z = np.arange(NZ)[None, :]
    angle = 2.0 * math.pi * (((k + 1) // 2 * z) % NZ) / NZ
    w = np.where(k % 2 == 1, np.cos(angle), np.sin(angle)) * math.sqrt(2.0 / NZ)
    w[0] = 1.0 / math.sqrt(NZ)
    w[NZ - 1] = np.cos(math.pi * np.arange(NZ)) / math.sqrt(NZ)
    return w.astype(np.float32)


def column_tables():
    lane = np.arange(EL) % 64
    half = np.arange(EL) // 64 * 64
    row = lane // DEEP
    out = []
    for first in (0, ELY - DEEP):
        col = lane % DEEP + first
        out.append(np.clip((row - DEEP) * ELY + col, 0, EL - 1))
        out.append(np.where(row < DEEP, row * ELY + col + half, 0))
        out.append(np.where((row >= DEEP + ELX) & (row < XROWS), (row - DEEP - ELX) * ELY + col + half, 0))
    out.append(row)
    out.append(half)
    return np.stack(out).astype(np.int32)


OWN, LOW, HIGH, LEFT, RIGHT, NONE = range(6)


def extended_tables():
    lane = np.arange(XL)
    row, col = lane // PITCH, lane % PITCH
    middle = (col >= DEEP) & (col < DEEP + ELY)
    left = (col < DEEP) & (row < XROWS)
    right = (col >= DEEP + ELY) & (col < XCOLS) & (row < XROWS)
    own = middle & (row >= DEEP) & (row < DEEP + ELX)
    low = middle & (row < DEEP)
    high = middle & (row >= DEEP + ELX) & (row < XROWS)
    source = np.full(XL, NONE)
    tables = np.zeros((6, XL), np.int64)
    for number, mask, index in (
        (OWN, own, (row - DEEP) * ELY + col - DEEP),
        (LOW, low, row * ELY + col - DEEP),
        (HIGH, high, (row - DEEP - ELX) * ELY + col - DEEP),
        (LEFT, left, row * DEEP + col),
        (RIGHT, right, row * DEEP + col - DEEP - ELY),
    ):
        source[mask] = number
        tables[number][mask] = index[mask]
    tables[5] = source
    home = np.arange(EL) // ELY * PITCH + DEEP * PITCH + np.arange(EL) % ELY + DEEP
    tables = tables.reshape(6, XL // EL, EL).reshape(-1, EL)
    return np.concatenate([tables, (home % EL)[None], (home // EL)[None]]).astype(np.int32), source.reshape(-1, EL)


EXT_TABLE, EXT_SOURCE = extended_tables()
COL_TABLE = column_tables()


def pick(values, index):
    return jnp.take_along_axis(values, jnp.broadcast_to(index, values.shape), axis=1, mode="promise_in_bounds")


def dot(a, b):
    return lax.dot_general(a, b, (((1,), (0,)), ((), ())), precision=HIGHEST, preferred_element_type=F32)


def transform_kernel(table, planes, out):
    groups, nodes = planes.shape[0], planes.shape[1]
    for n in range(nodes):
        block = planes[:, n].reshape(NZ, EL)
        out[:, n] = dot(table[...], block).reshape(groups, NZ // groups, EL)


def condense_kernel(spectral, coef, cell, couple, inner, condensed, base, down, up, coef_grid):
    lane = lax.broadcasted_iota(jnp.int32, (EL, EL), 1)
    elem = lax.broadcasted_iota(jnp.int32, (EL, EL), 0)
    cells = jnp.transpose(jnp.broadcast_to(cell[...], (EL, EL)))
    order = jnp.sum(jnp.where(cells == lane, elem, 0), axis=0, keepdims=True)
    scale = pick(jnp.broadcast_to(coef[...], (16, EL)), order)
    coef_grid[...] = scale[0:8]
    inverse = 1.0 / scale[0:1]
    first = lax.broadcasted_iota(jnp.int32, (16, EL), 1) < 64

    def messages(top, bottom):
        return (
            jnp.where(first, top, pltpu.roll(bottom, 64, 1)),
            jnp.where(first, pltpu.roll(top, 48, 1), pltpu.roll(bottom, 112, 1)),
        )

    down[MODES], up[MODES] = messages(scale, scale)

    def mode(m, _):
        fields = pick(spectral[pl.ds(m, PADDED, stride=MODES), :], order)
        within = fields[NB:NODES]
        value = fields[0:NB] - dot(couple[m], within)
        condensed[m] = value
        base[m, 0:NI] = dot(inner[pl.ds(m, NI, stride=MODES), :], within) * inverse
        down[m], up[m] = messages(value[0:16], value[16:32])
        return 0

    lax.fori_loop(0, MODES, mode, 0, unroll=2)


def columns_kernel(condensed, coef_grid, low, high, table, left, right):
    row = table[6:7, :]
    first = jnp.broadcast_to(table[7:8, :], (16, EL)) == 0
    is_own = jnp.broadcast_to((row >= DEEP) & (row < DEEP + ELX), (16, EL))
    is_low = jnp.broadcast_to(row < DEEP, (16, EL))

    def message(top, bottom, lo, hi, at):
        own = jnp.where(first, pick(top, table[at : at + 1, :]), pick(bottom, table[at : at + 1, :]))
        other = jnp.where(is_low, pick(lo, table[at + 1 : at + 2, :]), pick(hi, table[at + 2 : at + 3, :]))
        return jnp.where(is_own, own, other)

    scale = jnp.concatenate([coef_grid[...], coef_grid[...]], 0)
    left[MODES] = message(scale, scale, low[MODES], high[MODES], 0)
    right[MODES] = message(scale, scale, low[MODES], high[MODES], 3)

    def mode(m, _):
        top, bottom = condensed[m, 0:16], condensed[m, 16:32]
        left[m] = message(top, bottom, low[m], high[m], 0)
        right[m] = message(top, bottom, low[m], high[m], 3)
        return 0

    lax.fori_loop(0, MODES, mode, 0, unroll=2)


def krylov_kernel(
    position, condensed, coef_grid, low, high, left, right, schur, table, basis, sums, keep_ref, weight_ref, parts
):
    sources = (condensed, low, high, left, right)

    def spread(own, others, half):
        pieces = []
        for j in range(XL // EL):
            source = jnp.broadcast_to(table[15 + j : 16 + j, :], own.shape)
            piece = jnp.zeros(own.shape, F32)
            for number, values in ((OWN, own), (LOW, others[0]), (HIGH, others[1]), (LEFT, others[2]), (RIGHT, others[3])):
                if not (EXT_SOURCE[j] == number).any():
                    continue
                index = table[3 * number + j : 3 * number + j + 1, :]
                if number != OWN and half:
                    index = index + 64
                piece = jnp.where(source == number, pick(values, index), piece)
            pieces.append(piece)
        return jnp.concatenate(pieces, 1)

    lane = lax.broadcasted_iota(jnp.int32, (NB, XL), 1)
    slot = lax.broadcasted_iota(jnp.int32, (NB, XL), 0)
    row, col = lane // PITCH, lane % PITCH
    grid_row = row - DEEP + position[0] * ELX
    grid_col = col - DEEP + position[1] * ELY
    last_row, last_col = position[2] * ELX - 1, position[3] * ELY - 1
    inside = (grid_row >= 0) & (grid_row <= last_row) & (grid_col >= 0) & (grid_col <= last_col)
    inside = inside & (row < XROWS) & (col < XCOLS)
    dropped = (grid_row == 0) & ((slot == 0) | (slot >= 24))
    dropped = dropped | (grid_row == last_row) & (slot >= 8) & (slot <= 16)
    dropped = dropped | (grid_col == 0) & (slot <= 8)
    dropped = dropped | (grid_col == last_col) & (slot >= 16) & (slot <= 24)
    own = (row >= DEEP) & (row < DEEP + ELX) & (col >= DEEP) & (col < DEEP + ELY)
    keep = jnp.where(inside & ~dropped, 1.0, 0.0).astype(F32)
    keep_ref[...] = keep
    weight_ref[0] = jnp.where(own, 1.0, 0.0).astype(F32)
    weight_ref[1] = jnp.where(own, keep * jnp.where(slot % P_SIZE == 0, 0.25, 0.5), 0.0).astype(F32)
    scale8 = spread(coef_grid[...], [s[MODES, 0:8] for s in sources[1:]], 0)
    scale = jnp.where(inside[0:1], scale8[0:1], 0.0)

    sub = lax.broadcasted_iota(jnp.int32, (8, XL), 0)
    zero = sub == 0
    back = (8 - sub) % 8

    def rev(tile):
        return jnp.take_along_axis(tile, back, axis=0, mode="promise_in_bounds")

    def assemble(values):
        t = [values[8 * i : 8 * i + 8] for i in range(4)]
        for axis, (a, b, c, d) in ((PITCH, (1, 2, 3, 0)), (1, (2, 3, 0, 1))):
            ahead, behind = axis, XL - axis
            if axis == PITCH:
                prev3 = pltpu.roll(jnp.where(zero, t[2], rev(t[1])), ahead, 1)
                prev0 = pltpu.roll(jnp.where(zero, t[1], 0.0), ahead, 1)
                next1 = pltpu.roll(jnp.where(zero, t[0], rev(t[3])), behind, 1)
                next2 = pltpu.roll(jnp.where(zero, t[3], 0.0), behind, 1)
                t = [t[0] + prev0, t[1] + next1, t[2] + next2, t[3] + prev3]
            else:
                prev0 = pltpu.roll(jnp.where(zero, t[3], rev(t[2])), ahead, 1)
                prev1 = pltpu.roll(jnp.where(zero, t[2], 0.0), ahead, 1)
                next2 = pltpu.roll(jnp.where(zero, t[1], rev(t[0])), behind, 1)
                next3 = pltpu.roll(jnp.where(zero, t[0], 0.0), behind, 1)
                t = [t[0] + prev0, t[1] + prev1, t[2] + next2, t[3] + next3]
        return keep_ref[...] * jnp.concatenate(t, 0)

    eye = lax.broadcasted_iota(jnp.int32, (NB, NB), 0) == lax.broadcasted_iota(jnp.int32, (NB, NB), 1)
    home = table[18:19, :]
    home_at = jnp.broadcast_to(table[19:20, :], (NB, EL))

    def mode(m, _):
        matrix = schur[m]
        trace = jnp.sum(jnp.sum(jnp.where(eye, matrix, 0.0), axis=0, keepdims=True), axis=1, keepdims=True)
        shift = (0.5 * NB) / trace
        others = [s[m] for s in sources[1:]]
        value = jnp.concatenate([spread(condensed[m, 16 * h : 16 * h + 16], others, h) for h in (0, 1)], 0)
        v = [assemble(jnp.where(inside, value, 0.0))]
        w = []
        for step in range(3):
            w.append(scale * dot(matrix, v[step]))
            if step < 2:
                v.append(assemble(w[step]) * shift - v[step])
        mine, weight = weight_ref[0], weight_ref[1]
        k = 0
        for first, second, mask in (
            (v[0], v[0], weight), (v[0], v[1], weight), (v[1], v[1], weight),
            (v[0], w[0], mine), (v[1], w[0], mine), (v[1], w[1], mine), (v[2], w[1], mine), (v[2], w[2], mine),
        ):
            whole = jnp.sum(first * second * mask, axis=0, keepdims=True)
            folded = whole[:, 0:EL] + whole[:, EL : 2 * EL] + whole[:, 2 * EL :]
            parts[pl.ds(MODES * k + m, 1), :] = folded
            k += 1
        for i in range(3):
            out = jnp.zeros((NB, EL), F32)
            for j in range(XL // EL):
                out = jnp.where(home_at == j, pick(v[i][:, EL * j : EL * j + EL], home), out)
            basis[i, m] = out
        return 0

    lax.fori_loop(0, MODES, mode, 0, unroll=2)
    ones = jnp.ones((8, EL), F32)
    total = lax.dot_general(ones, parts[...], (((1,), (1,)), ((), ())), precision=HIGHEST, preferred_element_type=F32)
    sums[...] = total[0:1]


def finish_kernel(gathered, basis, base, couple, cell, out, coefs):
    total = jnp.broadcast_to(jnp.sum(gathered[...].reshape(-1, EL), axis=0, keepdims=True), (8, EL))
    b0, b1, b2, h0, h1, h2, h3, h4 = [
        total if k == 0 else pltpu.roll(total, EL - MODES * k, 1) for k in range(8)
    ]
    tiny = 2e-7
    l1, l2 = h1 / h0, h2 / h0
    d1 = h2 - l1 * h1
    ok1 = d1 > tiny * h2
    d1 = jnp.where(ok1, d1, 1.0)
    l12 = jnp.where(ok1, (h3 - l1 * h2) / d1, 0.0)
    d2 = h4 - l2 * h2 - l12 * l12 * d1
    ok2 = d2 > tiny * h4
    y1 = b1 - l1 * b0
    y2 = b2 - l2 * b0 - l12 * y1
    c2 = jnp.where(ok2, y2 / jnp.where(ok2, d2, 1.0), 0.0)
    c1 = jnp.where(ok1, y1 / d1, 0.0) - l12 * c2
    c0 = b0 / h0 - l1 * c1 - l2 * c2
    coefs[0], coefs[1], coefs[2] = c0, c1, c2
    index = cell[...]

    for m in range(MODES):
        c = [coefs[i, 0:1, m : m + 1] for i in range(3)]
        x = c[0] * basis[0, m] + c[1] * basis[1, m] + c[2] * basis[2, m]
        within = base[m, 0:NI] - lax.dot_general(
            couple[m], x, (((0,), (0,)), ((), ())), precision=HIGHEST, preferred_element_type=F32
        )
        fields = jnp.concatenate([x, within, jnp.zeros((PADDED - NODES, EL), F32)], 0)
        out[pl.ds(m, PADDED, stride=MODES), :] = pick(fields, index)


def call(kernel, shapes, scratch=(), smem=0):
    def run(*operands):
        many = isinstance(shapes, list)
        outs = [jax.ShapeDtypeStruct(s, F32) for s in (shapes if many else [shapes])]
        whole = pl.BlockSpec(memory_space=pltpu.VMEM)
        specs = [pl.BlockSpec(memory_space=pltpu.SMEM)] * smem + [whole] * (len(operands) - smem)
        return pl.pallas_call(
            kernel,
            out_shape=outs if many else outs[0],
            in_specs=specs,
            out_specs=[whole] * len(outs) if many else whole,
            scratch_shapes=list(scratch),
            name=kernel.__name__,
        )(*operands)

    return run


def swap(array):
    return lax.all_to_all(array, "fourier", split_axis=0, concat_axis=0, tiled=True)


def ring(axis, step):
    count = lax.axis_size(axis)
    return [(i, (i + step) % count) for i in range(count)]


def neighbours(to_low, to_high, axis):
    return lax.ppermute(to_high, axis, ring(axis, 1)), lax.ppermute(to_low, axis, ring(axis, -1))


def on_device(forcing, element_coef, schur, couple, inner_inv, element_cell):
    parts = lax.axis_size("fourier")
    group = PADDED // parts
    table = jnp.asarray(real_transform())
    cell = element_cell.reshape(1, EL)
    exchanged = (parts, group, MODES, EL)

    planes = jnp.pad(jnp.transpose(forcing, (1, 0, 2)), ((0, PADDED - NODES), (0, 0), (0, 0)))
    planes = swap(planes).reshape(exchanged)
    spectral = swap(call(transform_kernel, exchanged)(table, planes).reshape(PADDED, MODES, EL))

    message = (MODES + 1, 16, EL)
    condensed, base, down, up, coef_grid = call(
        condense_kernel, [(MODES, NB, EL), (MODES, 56, EL), message, message, (8, EL)]
    )(
        spectral.reshape(PADDED * MODES, EL),
        element_coef.reshape(1, EL),
        cell,
        couple,
        jnp.transpose(inner_inv, (1, 0, 2)).reshape(NI * MODES, NI),
    )
    low, high = neighbours(down, up, "ex")
    left, right = call(columns_kernel, [message, message])(condensed, coef_grid, low, high, jnp.asarray(COL_TABLE))
    left, right = neighbours(left, right, "ey")
    position = jnp.stack(
        [lax.axis_index("ex"), lax.axis_index("ey"), lax.axis_size("ex"), lax.axis_size("ey")]
    ).astype(jnp.int32)
    basis, sums = call(
        krylov_kernel,
        [(3, MODES, NB, EL), (1, EL)],
        [pltpu.VMEM((NB, XL), F32), pltpu.VMEM((2, NB, XL), F32), pltpu.VMEM((EL, EL), F32)],
        smem=1,
    )(position, condensed, coef_grid, low, high, left, right, schur, jnp.asarray(EXT_TABLE))
    copies = lax.axis_size("ex") * lax.axis_size("ey")
    gathered = lax.all_to_all(
        jnp.broadcast_to(sums[None], (copies, 1, EL)), ("ex", "ey"), split_axis=0, concat_axis=0, tiled=True
    )
    modal = call(finish_kernel, (PADDED * MODES, EL), [pltpu.VMEM((3, 8, EL), F32)])(
        gathered, basis, base, couple, cell
    )
    modal = swap(modal.reshape(PADDED, MODES, EL)).reshape(exchanged)
    velocity = swap(call(transform_kernel, exchanged)(table.T, modal).reshape(PADDED, MODES, EL))
    return jnp.transpose(velocity[:NODES], (1, 0, 2))


def solution(mesh):
    placed = (
        P("fourier", None, ("ex", "ey")),
        P(("ex", "ey")),
        P("fourier", None, None),
        P("fourier", None, None),
        P("fourier", None, None),
        P(("ex", "ey")),
    )
    return jax.shard_map(
        on_device,
        mesh=mesh,
        in_specs=placed,
        out_specs=P("fourier", None, ("ex", "ey")),
        check_vma=False,
    )
```

```python
import math

import jax
import jax.numpy as jnp
import numpy as np
from jax import lax
from jax.experimental import pallas as pl
from jax.experimental.pallas import tpu as pltpu
from jax.sharding import PartitionSpec as P

P_SIZE = 8
NZ = 128
ELX = 8
ELY = 16
NODES = 81
NB = 32
NI = 49
EL = ELX * ELY
PADDED = 88
MODES = 16
DEEP = 3
PITCH = 24
XROWS = ELX + 2 * DEEP
XCOLS = ELY + 2 * DEEP
XL = 384
UNROLL = 8
HIGHEST = lax.Precision.HIGHEST
F32 = jnp.float32


def real_transform():
    k = np.arange(NZ)[:, None]
    z = np.arange(NZ)[None, :]
    angle = 2.0 * math.pi * (((k + 1) // 2 * z) % NZ) / NZ
    w = np.where(k % 2 == 1, np.cos(angle), np.sin(angle)) * math.sqrt(2.0 / NZ)
    w[0] = 1.0 / math.sqrt(NZ)
    w[NZ - 1] = np.cos(math.pi * np.arange(NZ)) / math.sqrt(NZ)
    return w.astype(np.float32)


def column_tables():
    lane = np.arange(EL) % 64
    half = np.arange(EL) // 64 * 64
    row = lane // DEEP
    out = []
    for first in (0, ELY - DEEP):
        col = lane % DEEP + first
        out.append(np.clip((row - DEEP) * ELY + col, 0, EL - 1))
        out.append(np.where(row < DEEP, row * ELY + col + half, 0))
        out.append(np.where((row >= DEEP + ELX) & (row < XROWS), (row - DEEP - ELX) * ELY + col + half, 0))
    out.append(row)
    out.append(half)
    return np.stack(out).astype(np.int32)


OWN, LOW, HIGH, LEFT, RIGHT, NONE = range(6)
BLOCKS = XL // EL


def extended_tables():
    lane = np.arange(XL)
    row, col = (lane // PITCH + DEEP) % (XL // PITCH), lane % PITCH
    middle = (col >= DEEP) & (col < DEEP + ELY)
    left = (col < DEEP) & (row < XROWS)
    right = (col >= DEEP + ELY) & (col < XCOLS) & (row < XROWS)
    own = middle & (row >= DEEP) & (row < DEEP + ELX)
    low = middle & (row < DEEP)
    high = middle & (row >= DEEP + ELX) & (row < XROWS)
    source = np.full(XL, NONE)
    tables = np.zeros((6, XL), np.int64)
    for number, mask, index in (
        (OWN, own, (row - DEEP) * ELY + col - DEEP),
        (LOW, low, row * ELY + col - DEEP),
        (HIGH, high, (row - DEEP - ELX) * ELY + col - DEEP),
        (LEFT, left, row * DEEP + col),
        (RIGHT, right, row * DEEP + col - DEEP - ELY),
    ):
        source[mask] = number
        tables[number][mask] = index[mask]
    tables[5] = source
    home = np.arange(EL) // ELY * PITCH + np.arange(EL) % ELY + DEEP
    tables = tables.reshape(6, BLOCKS, EL).reshape(-1, EL)
    tables = np.concatenate([tables, (home % EL)[None], (home // EL)[None]])
    place = np.stack([row, col]).repeat(8, 0).reshape(2, 8, XL)
    return np.repeat(tables[:, None], 8, 1).astype(np.int32), source.reshape(-1, EL), place.astype(np.int32)


EXT_TABLE, EXT_SOURCE, EXT_PLACE = extended_tables()
COL_TABLE = column_tables()


def pick(values, index):
    return jnp.take_along_axis(values, jnp.broadcast_to(index, values.shape), axis=1, mode="promise_in_bounds")


def dot(a, b):
    return lax.dot_general(a, b, (((1,), (0,)), ((), ())), precision=HIGHEST, preferred_element_type=F32)


def transform_kernel(table, planes, out):
    groups, nodes = planes.shape[0], planes.shape[1]
    for n in range(nodes):
        block = planes[:, n].reshape(NZ, EL)
        out[:, n] = dot(table[...], block).reshape(groups, NZ // groups, EL)


def enter_kernel(forcing, coef, cell, planes, order, index, scale, done):
    nodes = forcing.shape[0]
    copy = pltpu.make_async_copy(forcing, planes.at[pl.ds(0, nodes)], done)
    copy.start()
    planes[nodes:PADDED] = jnp.zeros((PADDED - nodes, planes.shape[1], EL), F32)
    lane = lax.broadcasted_iota(jnp.int32, (EL, EL), 1)
    elem = lax.broadcasted_iota(jnp.int32, (EL, EL), 0)
    cells = jnp.transpose(jnp.broadcast_to(cell[...], (EL, EL)))
    found = jnp.sum(jnp.where(cells == lane, elem, 0), axis=0, keepdims=True)
    order[...] = jnp.broadcast_to(found, (8, EL))
    index[...] = jnp.broadcast_to(cell[...], (8, EL))
    scale[...] = pick(jnp.broadcast_to(coef[...], (8, EL)), found)
    copy.wait()


def leave_kernel(planes, velocity, done):
    copy = pltpu.make_async_copy(planes.at[pl.ds(0, velocity.shape[0])], velocity, done)
    copy.start()
    copy.wait()


def condense_kernel(spectral, order, scale, couple, condensed, down, up):
    first = lax.broadcasted_iota(jnp.int32, (16, EL), 1) < 64

    def messages(top, bottom):
        return (
            jnp.where(first, top, pltpu.roll(bottom, 64, 1)),
            jnp.where(first, pltpu.roll(top, 48, 1), pltpu.roll(bottom, 112, 1)),
        )

    wide = jnp.concatenate([scale[...], scale[...]], 0)
    down[MODES], up[MODES] = messages(wide, wide)

    def mode(m, _):
        fields = pick(spectral[pl.ds(m, PADDED, stride=MODES), :], order[0:1])
        value = fields[0:NB] - dot(couple[m], fields[NB:NODES])
        condensed[m] = value
        down[m], up[m] = messages(value[0:16], value[16:32])
        return 0

    lax.fori_loop(0, MODES, mode, 0, unroll=UNROLL)


def interior_kernel(spectral, order, scale, inner, base):
    inverse = 1.0 / scale[0:1]

    def mode(m, _):
        within = pick(spectral[pl.ds(NB * MODES + m, PADDED - NB, stride=MODES), :], order[0:1])[0:NI]
        base[m, 0:NI] = dot(inner[pl.ds(m, NI, stride=MODES), :], within) * inverse
        return 0

    lax.fori_loop(0, MODES, mode, 0, unroll=UNROLL)


def columns_kernel(condensed, coef_grid, low, high, table, left, right):
    row = table[6:7, :]
    first = jnp.broadcast_to(table[7:8, :], (16, EL)) == 0
    is_own = jnp.broadcast_to((row >= DEEP) & (row < DEEP + ELX), (16, EL))
    is_low = jnp.broadcast_to(row < DEEP, (16, EL))

    def message(top, bottom, lo, hi, at):
        own = jnp.where(first, pick(top, table[at : at + 1, :]), pick(bottom, table[at : at + 1, :]))
        other = jnp.where(is_low, pick(lo, table[at + 1 : at + 2, :]), pick(hi, table[at + 2 : at + 3, :]))
        return jnp.where(is_own, own, other)

    wide = jnp.concatenate([coef_grid[...], coef_grid[...]], 0)
    left[MODES] = message(wide, wide, low[MODES], high[MODES], 0)
    right[MODES] = message(wide, wide, low[MODES], high[MODES], 3)

    def mode(m, _):
        top, bottom = condensed[m, 0:16], condensed[m, 16:32]
        left[m] = message(top, bottom, low[m], high[m], 0)
        right[m] = message(top, bottom, low[m], high[m], 3)
        return 0

    lax.fori_loop(0, MODES, mode, 0, unroll=UNROLL)


def spread(tile, sources, table):
    pieces = []
    for j in range(BLOCKS):
        source = table[5 * BLOCKS + j]
        piece = tile[j]
        for number, values, half in sources:
            if (EXT_SOURCE[j] == number).any():
                index = table[BLOCKS * number + j]
                piece = jnp.where(source == number, pick(values, index + 64 if half else index), piece)
        pieces.append(piece)
    return pieces


def middle_kernel(condensed, scale, low, high, table, block):
    blank = [jnp.zeros((8, EL), F32)] * BLOCKS

    def put(m, tile, pieces):
        for j in range(BLOCKS):
            block[m, 8 * tile : 8 * tile + 8, EL * j : EL * j + EL] = pieces[j]

    put(MODES, 0, spread(blank, ((OWN, scale[...], 0), (LOW, low[MODES, 0:8], 0), (HIGH, high[MODES, 0:8], 0)), table))

    def mode(m, _):
        for tile in range(4):
            half, at = tile // 2, tile % 2 * 8
            sources = (
                (OWN, condensed[m, 8 * tile : 8 * tile + 8], 0),
                (LOW, low[m, at : at + 8], half),
                (HIGH, high[m, at : at + 8], half),
            )
            put(m, tile, spread(blank, sources, table))
        return 0

    lax.fori_loop(0, MODES, mode, 0, unroll=UNROLL)


def krylov_kernel(block, coef_grid, left, right, schur, table, place, basis, sums, keep_ref, weight_ref, parts, state):
    def sides(m, tile):
        half, at = tile // 2, tile % 2 * 8
        held = [block[m, 8 * tile : 8 * tile + 8, EL * j : EL * j + EL] for j in range(BLOCKS)]
        sources = ((LEFT, left[m, at : at + 8], half), (RIGHT, right[m, at : at + 8], half))
        return jnp.concatenate(spread(held, sources, table), 1)

    row, col = place[0], place[1]
    grid_row = row - DEEP + lax.axis_index("ex") * ELX
    grid_col = col - DEEP + lax.axis_index("ey") * ELY
    last_row, last_col = lax.axis_size("ex") * ELX - 1, lax.axis_size("ey") * ELY - 1
    inside = (grid_row >= 0) & (grid_row <= last_row) & (grid_col >= 0) & (grid_col <= last_col)
    inside = inside & (row < XROWS) & (col < XCOLS)
    own = (row >= DEEP) & (row < DEEP + ELX) & (col >= DEEP) & (col < DEEP + ELY)
    corner = lax.broadcasted_iota(jnp.int32, (8, XL), 0) == 0
    low_row, high_row, low_col, high_col = grid_row == 0, grid_row == last_row, grid_col == 0, grid_col == last_col
    for tile, (edge, other) in enumerate(((low_col, low_row), (high_row, low_col), (high_col, high_row), (low_row, high_col))):
        keep = jnp.where(inside & ~(edge | (corner & other)), 1.0, 0.0).astype(F32)
        keep_ref[8 * tile : 8 * tile + 8] = keep
        weight_ref[8 * tile : 8 * tile + 8] = jnp.where(own, keep * jnp.where(corner, 0.25, 0.5), 0.0).astype(F32)
    scale = jnp.where(inside, sides(MODES, 0), 0.0)[0:1]

    sub = lax.broadcasted_iota(jnp.int32, (8, XL), 0)
    zero = sub == 0
    back = (8 - sub) % 8

    def rev(tile):
        return jnp.take_along_axis(tile, back, axis=0, mode="promise_in_bounds")

    def assemble(values):
        t = [values[8 * i : 8 * i + 8] for i in range(4)]
        for axis, (a, b, c, d) in ((PITCH, (1, 2, 3, 0)), (1, (2, 3, 0, 1))):
            ahead, behind = axis, XL - axis
            if axis == PITCH:
                prev3 = pltpu.roll(jnp.where(zero, t[2], rev(t[1])), ahead, 1)
                prev0 = pltpu.roll(jnp.where(zero, t[1], 0.0), ahead, 1)
                next1 = pltpu.roll(jnp.where(zero, t[0], rev(t[3])), behind, 1)
                next2 = pltpu.roll(jnp.where(zero, t[3], 0.0), behind, 1)
                t = [t[0] + prev0, t[1] + next1, t[2] + next2, t[3] + prev3]
            else:
                prev0 = pltpu.roll(jnp.where(zero, t[3], rev(t[2])), ahead, 1)
                prev1 = pltpu.roll(jnp.where(zero, t[2], 0.0), ahead, 1)
                next2 = pltpu.roll(jnp.where(zero, t[1], rev(t[0])), behind, 1)
                next3 = pltpu.roll(jnp.where(zero, t[0], 0.0), behind, 1)
                t = [t[0] + prev0, t[1] + prev1, t[2] + next2, t[3] + next3]
        return keep_ref[...] * jnp.concatenate(t, 0)

    eye = lax.broadcasted_iota(jnp.int32, (NB, NB), 0) == lax.broadcasted_iota(jnp.int32, (NB, NB), 1)
    home, home_at = table[6 * BLOCKS], table[6 * BLOCKS + 1]
    own_scale = coef_grid[0:1]

    def at_home(ref):
        tiles = []
        for tile in range(4):
            one, two = (pick(ref[8 * tile : 8 * tile + 8, EL * j : EL * j + EL], home) for j in (0, 1))
            tiles.append(jnp.where(home_at == 0, one, two))
        return jnp.concatenate(tiles, 0)

    weight_ref[:, 0:EL] = at_home(weight_ref)

    def gather_mode(m):
        state[0, m] = assemble(jnp.concatenate([sides(m, tile) for tile in range(4)], 0))

    def apply_mode(i):
        def run(m):
            state[3, m] = scale * dot(schur[m], state[i, m])

        return run

    def extend_mode(i):
        def run(m):
            trace = jnp.sum(jnp.sum(jnp.where(eye, schur[m], 0.0), axis=0, keepdims=True), axis=1, keepdims=True)
            state[i + 1, m] = assemble(state[3, m]) * ((0.5 * NB) / trace) - state[i, m]

        return run

    def sum_mode(m):
        v = [at_home(state.at[i, m]) for i in range(3)]
        w = [own_scale * dot(schur[m], v[i]) for i in range(3)]
        weight = weight_ref[:, 0:EL]
        weighted = v[0] * weight
        k = 0
        for first, second in (
            (v[0], weighted), (v[1], weighted), (v[1], v[1] * weight),
            (v[0], w[0]), (v[1], w[0]), (v[1], w[1]), (v[2], w[1]), (v[2], w[2]),
        ):
            parts[pl.ds(MODES * k + m, 1), :] = jnp.sum(first * second, axis=0, keepdims=True)
            k += 1
        for i in range(3):
            basis[i, m] = v[i]

    def every(body):
        def step(m, _):
            body(m)
            return 0

        lax.fori_loop(0, MODES, step, 0, unroll=UNROLL)

    every(gather_mode)
    for i in range(2):
        every(apply_mode(i))
        every(extend_mode(i))
    every(sum_mode)
    ones = jnp.ones((8, EL), F32)
    total = lax.dot_general(ones, parts[...], (((1,), (1,)), ((), ())), precision=HIGHEST, preferred_element_type=F32)
    sums[...] = total[0:1]


def finish_kernel(gathered, basis, base, couple, cell, out, coefs):
    total = jnp.broadcast_to(jnp.sum(gathered[...].reshape(-1, EL), axis=0, keepdims=True), (8, EL))
    b0, b1, b2, h0, h1, h2, h3, h4 = [
        total if k == 0 else pltpu.roll(total, EL - MODES * k, 1) for k in range(8)
    ]
    tiny = 2e-7
    l1, l2 = h1 / h0, h2 / h0
    d1 = h2 - l1 * h1
    ok1 = d1 > tiny * h2
    d1 = jnp.where(ok1, d1, 1.0)
    l12 = jnp.where(ok1, (h3 - l1 * h2) / d1, 0.0)
    d2 = h4 - l2 * h2 - l12 * l12 * d1
    ok2 = d2 > tiny * h4
    y1 = b1 - l1 * b0
    y2 = b2 - l2 * b0 - l12 * y1
    c2 = jnp.where(ok2, y2 / jnp.where(ok2, d2, 1.0), 0.0)
    c1 = jnp.where(ok1, y1 / d1, 0.0) - l12 * c2
    c0 = b0 / h0 - l1 * c1 - l2 * c2
    coefs[0], coefs[1], coefs[2] = c0, c1, c2
    index = cell[0:1]

    for m in range(MODES):
        c = [coefs[i, 0:1, m : m + 1] for i in range(3)]
        x = c[0] * basis[0, m] + c[1] * basis[1, m] + c[2] * basis[2, m]
        within = base[m, 0:NI] - lax.dot_general(
            couple[m], x, (((0,), (0,)), ((), ())), precision=HIGHEST, preferred_element_type=F32
        )
        fields = jnp.concatenate([x, within, jnp.zeros((PADDED - NODES, EL), F32)], 0)
        out[pl.ds(m, PADDED, stride=MODES), :] = pick(fields, index)


def call(kernel, shapes=(), scratch=(), far=0, far_out=None):
    def run(*operands):
        many = isinstance(shapes, list)
        outs = [s if isinstance(s, pl.MemoryRef) else pltpu.VMEM(s, F32) for s in (shapes if many else [shapes])]
        whole, away = pl.BlockSpec(memory_space=pltpu.VMEM), pl.BlockSpec(memory_space=pl.ANY)
        near = tuple(pltpu.with_memory_space_constraint(o, pltpu.VMEM) for o in operands[far:])
        if far_out:
            outs = [jax.ShapeDtypeStruct(far_out, F32)]
        specs = [away if far_out else whole] * len(outs)
        return pl.pallas_call(
            kernel,
            out_shape=outs if many else outs[0],
            in_specs=[away] * far + [whole] * len(near),
            out_specs=specs if many else specs[0],
            scratch_shapes=list(scratch),
            compiler_params=pltpu.CompilerParams(vmem_limit_bytes=16 << 20),
            name=kernel.__name__,
        )(*operands[:far], *near)

    return run


def swap(array):
    return lax.all_to_all(array, "fourier", split_axis=0, concat_axis=0, tiled=True)


def ring(axis, step):
    count = lax.axis_size(axis)
    return [(i, (i + step) % count) for i in range(count)]


def neighbours(to_low, to_high, axis):
    return lax.ppermute(to_high, axis, ring(axis, 1)), lax.ppermute(to_low, axis, ring(axis, -1))


def on_device(forcing, element_coef, schur, couple, inner_inv, element_cell):
    parts = lax.axis_size("fourier")
    group = PADDED // parts
    table = jnp.asarray(real_transform())
    exchanged = (parts, group, MODES, EL)
    lanes = (8, EL)
    ints = pltpu.VMEM(lanes, jnp.int32)

    planes, order, index, scale = call(
        enter_kernel, [(PADDED, MODES, EL), ints, ints, lanes], [pltpu.SemaphoreType.DMA], far=1
    )(jnp.transpose(forcing, (1, 0, 2)), element_coef.reshape(1, EL), element_cell.reshape(1, EL))
    planes = swap(planes).reshape(exchanged)
    spectral = swap(call(transform_kernel, exchanged)(table, planes).reshape(PADDED, MODES, EL))
    spectral = spectral.reshape(PADDED * MODES, EL)

    message = (MODES + 1, 16, EL)
    condensed, down, up = call(condense_kernel, [(MODES, NB, EL), message, message])(spectral, order, scale, couple)
    low, high = neighbours(down, up, "ex")
    base = call(interior_kernel, (MODES, 56, EL))(
        spectral, order, scale, jnp.transpose(inner_inv, (1, 0, 2)).reshape(NI * MODES, NI)
    )
    left, right = call(columns_kernel, [message, message])(condensed, scale, low, high, jnp.asarray(COL_TABLE))
    left, right = neighbours(left, right, "ey")
    extended = jnp.asarray(EXT_TABLE)
    block = call(middle_kernel, (MODES + 1, NB, XL))(condensed, scale, low, high, extended)
    basis, sums = call(
        krylov_kernel,
        [(3, MODES, NB, EL), (1, EL)],
        [pltpu.VMEM((NB, XL), F32), pltpu.VMEM((NB, XL), F32), pltpu.VMEM((EL, EL), F32), pltpu.VMEM((4, MODES, NB, XL), F32)],
    )(block, scale, left, right, schur, extended, jnp.asarray(EXT_PLACE))
    copies = lax.axis_size("ex") * lax.axis_size("ey")
    gathered = lax.all_to_all(
        jnp.broadcast_to(sums[None], (copies, 1, EL)), ("ex", "ey"), split_axis=0, concat_axis=0, tiled=True
    )
    modal = call(finish_kernel, (PADDED * MODES, EL), [pltpu.VMEM((3, 8, EL), F32)])(
        gathered, basis, base, couple, index
    )
    modal = swap(modal.reshape(PADDED, MODES, EL)).reshape(exchanged)
    velocity = swap(call(transform_kernel, exchanged)(table.T, modal).reshape(PADDED, MODES, EL))
    velocity = call(leave_kernel, far_out=(NODES, MODES, EL), scratch=[pltpu.SemaphoreType.DMA])(velocity)
    return jnp.transpose(velocity, (1, 0, 2))


def solution(mesh):
    placed = (
        P("fourier", None, ("ex", "ey")),
        P(("ex", "ey")),
        P("fourier", None, None),
        P("fourier", None, None),
        P("fourier", None, None),
        P(("ex", "ey")),
    )
    return jax.shard_map(
        on_device,
        mesh=mesh,
        in_specs=placed,
        out_specs=P("fourier", None, ("ex", "ey")),
        check_vma=False,
    )
```

```python
import math

import jax
import jax.numpy as jnp
import numpy as np
from jax import lax
from jax.experimental import pallas as pl
from jax.experimental.pallas import tpu as pltpu
from jax.sharding import PartitionSpec as P

P_SIZE = 8
NZ = 128
ELX = 8
ELY = 16
NODES = 81
NB = 32
NI = 49
EL = ELX * ELY
PADDED = 88
MODES = 16
DEEP = 3
PITCH = 24
XROWS = ELX + 2 * DEEP
XCOLS = ELY + 2 * DEEP
XL = 384
NEAR = 256
UNROLL = 8
CHUNKS = 3
HIGHEST = lax.Precision.HIGHEST
F32 = jnp.float32


def real_transform():
    k = np.arange(NZ)[:, None]
    z = np.arange(NZ)[None, :]
    angle = 2.0 * math.pi * (((k + 1) // 2 * z) % NZ) / NZ
    w = np.where(k % 2 == 1, np.cos(angle), np.sin(angle)) * math.sqrt(2.0 / NZ)
    w[0] = 1.0 / math.sqrt(NZ)
    w[NZ - 1] = np.cos(math.pi * np.arange(NZ)) / math.sqrt(NZ)
    return w.astype(np.float32)


def column_tables():
    lane = np.arange(EL) % 64
    half = np.arange(EL) // 64 * 64
    row = lane // DEEP
    out = []
    for first in (0, ELY - DEEP):
        col = lane % DEEP + first
        out.append(np.clip((row - DEEP) * ELY + col, 0, EL - 1))
        out.append(np.where(row < DEEP, row * ELY + col + half, 0))
        out.append(np.where((row >= DEEP + ELX) & (row < XROWS), (row - DEEP - ELX) * ELY + col + half, 0))
    out.append(row)
    out.append(half)
    return np.stack(out).astype(np.int32)


OWN, LOW, HIGH, SIDE, NONE = range(5)
BLOCKS = XL // EL


def extended_tables():
    lane = np.arange(XL)
    row, col = (lane // PITCH + DEEP) % (XL // PITCH), lane % PITCH
    middle = (col >= DEEP) & (col < DEEP + ELY)
    left = (col < DEEP) & (row < XROWS)
    right = (col >= DEEP + ELY) & (col < XCOLS) & (row < XROWS)
    own = middle & (row >= DEEP) & (row < DEEP + ELX)
    low = middle & (row < DEEP)
    high = middle & (row >= DEEP + ELX) & (row < XROWS)
    source = np.full(XL, NONE)
    tables = np.zeros((5, XL), np.int64)
    for number, mask, index in (
        (OWN, own, (row - DEEP) * ELY + col - DEEP),
        (LOW, low, row * ELY + col - DEEP),
        (HIGH, high, (row - DEEP - ELX) * ELY + col - DEEP),
        (SIDE, left | right, np.where(left, row * DEEP + col, 64 + row * DEEP + col - DEEP - ELY)),
    ):
        source[mask] = number
        tables[number][mask] = index[mask]
    tables[4] = source
    tables = tables.reshape(5, BLOCKS, EL).reshape(-1, EL)
    place = np.stack([row, col]).repeat(8, 0).reshape(2, 8, XL)
    return np.repeat(tables[:, None], 8, 1).astype(np.int32), source.reshape(-1, EL), place.astype(np.int32)


EXT_TABLE, EXT_SOURCE, EXT_PLACE = extended_tables()
COL_TABLE = column_tables()


def pick(values, index):
    return jnp.take_along_axis(values, jnp.broadcast_to(index, values.shape), axis=1, mode="promise_in_bounds")


def dot(a, b):
    return lax.dot_general(a, b, (((1,), (0,)), ((), ())), precision=HIGHEST, preferred_element_type=F32)


def transform_kernel(table, planes, out):
    groups, nodes = planes.shape[0], planes.shape[1]
    for n in range(nodes):
        block = planes[:, n].reshape(NZ, EL)
        out[:, n] = dot(table[...], block).reshape(groups, NZ // groups, EL)


def copies(source, target, nodes, done):
    step = -(-nodes // CHUNKS)
    cuts = [(at, min(step, nodes - at)) for at in range(0, nodes, step)]
    return [
        pltpu.make_async_copy(source.at[pl.ds(at, size)], target.at[pl.ds(at, size)], done.at[i])
        for i, (at, size) in enumerate(cuts)
    ]


def enter_kernel(forcing, coef_far, cell_far, planes, order, index, scale, stored, done, small, coef, cell):
    nodes = forcing.shape[0]
    fetched = [pltpu.make_async_copy(coef_far, coef, small.at[0]), pltpu.make_async_copy(cell_far, cell, small.at[1])]
    moved = copies(forcing, planes, nodes, done)
    for copy in fetched + moved:
        copy.start()
    planes[nodes:PADDED] = jnp.zeros((PADDED - nodes, planes.shape[1], EL), F32)
    for copy in fetched:
        copy.wait()
    lane = lax.broadcasted_iota(jnp.int32, (EL, EL), 1)
    elem = lax.broadcasted_iota(jnp.int32, (EL, EL), 0)
    cells = jnp.transpose(jnp.broadcast_to(cell[...], (EL, EL)))
    found = jnp.sum(jnp.where(cells == lane, elem, 0), axis=0, keepdims=True)
    order[...] = jnp.broadcast_to(found, (8, EL))
    index[...] = jnp.broadcast_to(cell[...], (8, EL))
    stored[...] = jnp.broadcast_to(coef[...], (8, EL))
    scale[...] = pick(jnp.broadcast_to(coef[...], (8, EL)), found)
    for copy in moved:
        copy.wait()


def leave_kernel(planes, velocity, done):
    moved = copies(planes, velocity, velocity.shape[0], done)
    for copy in moved:
        copy.start()
    for copy in moved:
        copy.wait()


def flipped(tile):
    back = (8 - lax.broadcasted_iota(jnp.int32, tile.shape, 0)) % 8
    return jnp.take_along_axis(tile, back, axis=0, mode="promise_in_bounds")


def both_ascending(values):
    return jnp.concatenate([values[0:16], flipped(values[16:24]), flipped(values[24:32])], 0)


def condense_kernel(spectral, order, scale, couple, condensed, down, up):
    first = lax.broadcasted_iota(jnp.int32, (16, EL), 1) < 64

    def messages(top, bottom):
        return (
            jnp.where(first, top, pltpu.roll(bottom, 64, 1)),
            jnp.where(first, pltpu.roll(top, 48, 1), pltpu.roll(bottom, 112, 1)),
        )

    wide = jnp.concatenate([scale[...], scale[...]], 0)
    down[MODES], up[MODES] = messages(wide, wide)

    def mode(m, _):
        fields = pick(spectral[pl.ds(m, PADDED, stride=MODES), :], order[0:1])
        value = both_ascending(fields[0:NB] - dot(couple[m], fields[NB:NODES]))
        condensed[m] = value
        down[m], up[m] = messages(value[0:16], value[16:32])
        return 0

    lax.fori_loop(0, MODES, mode, 0, unroll=UNROLL)


def interior_kernel(spectral, stored, inner, base):
    inverse = 1.0 / stored[0:1]

    def mode(m, _):
        within = spectral[pl.ds(NB * MODES + m, PADDED - NB, stride=MODES), :][0:NI]
        base[m, 0:NI] = dot(inner[pl.ds(m, NI, stride=MODES), :], within) * inverse
        return 0

    lax.fori_loop(0, MODES, mode, 0, unroll=UNROLL)


def columns_kernel(condensed, coef_grid, low, high, table, left, right):
    row = table[6:7, :]
    first = jnp.broadcast_to(table[7:8, :], (16, EL)) == 0
    is_own = jnp.broadcast_to((row >= DEEP) & (row < DEEP + ELX), (16, EL))
    is_low = jnp.broadcast_to(row < DEEP, (16, EL))

    def message(top, bottom, lo, hi, at):
        own = jnp.where(first, pick(top, table[at : at + 1, :]), pick(bottom, table[at : at + 1, :]))
        other = jnp.where(is_low, pick(lo, table[at + 1 : at + 2, :]), pick(hi, table[at + 2 : at + 3, :]))
        return jnp.where(is_own, own, other)

    wide = jnp.concatenate([coef_grid[...], coef_grid[...]], 0)
    left[MODES] = message(wide, wide, low[MODES], high[MODES], 0)
    right[MODES] = message(wide, wide, low[MODES], high[MODES], 3)

    def mode(m, _):
        top, bottom = condensed[m, 0:16], condensed[m, 16:32]
        left[m] = message(top, bottom, low[m], high[m], 0)
        right[m] = message(top, bottom, low[m], high[m], 3)
        return 0

    lax.fori_loop(0, MODES, mode, 0, unroll=UNROLL)


def spread(tile, sources, table):
    pieces = []
    for j in range(BLOCKS):
        source = table[4 * BLOCKS + j]
        piece = tile[j]
        for number, values, half in sources:
            if (EXT_SOURCE[j] == number).any():
                index = table[BLOCKS * number + j]
                piece = jnp.where(source == number, pick(values, index + 64 if half else index), piece)
        pieces.append(piece)
    return pieces


def middle_kernel(condensed, scale, low, high, schur, table, block, matrix):
    blank = [jnp.zeros((8, EL), F32)] * BLOCKS

    def put(m, tile, pieces):
        for j in range(BLOCKS):
            block[m, 8 * tile : 8 * tile + 8, EL * j : EL * j + EL] = pieces[j]

    put(MODES, 0, spread(blank, ((OWN, scale[...], 0), (LOW, low[MODES, 0:8], 0), (HIGH, high[MODES, 0:8], 0)), table))

    lane = lax.broadcasted_iota(jnp.int32, (NB, NB), 1)
    across = jnp.where((lane >= 16) & (lane % 8 > 0), lane // 8 * 8 + 8 - lane % 8, lane)

    def mode(m, _):
        rows = both_ascending(schur[m])
        matrix[m] = jnp.take_along_axis(rows, across, axis=1, mode="promise_in_bounds")
        for tile in range(4):
            half, at = tile // 2, tile % 2 * 8
            sources = (
                (OWN, condensed[m, 8 * tile : 8 * tile + 8], 0),
                (LOW, low[m, at : at + 8], half),
                (HIGH, high[m, at : at + 8], half),
            )
            put(m, tile, spread(blank, sources, table))
        return 0

    lax.fori_loop(0, MODES, mode, 0, unroll=UNROLL)


def krylov_kernel(
    block, coef_grid, left, right, schur, table, place, basis, sums, keep_ref, weight_ref, mine_ref, parts, state, applied, pairs, spreadout
):
    first = lax.broadcasted_iota(jnp.int32, (8, EL), 1) < 64

    def pair_up(m):
        for at in (0, 1):
            low, high = left[m, 8 * at : 8 * at + 8], right[m, 8 * at : 8 * at + 8]
            base = m * NB + 8 * at
            pairs[pl.ds(base, 8), :] = jnp.where(first, low, pltpu.roll(high, 64, 1))
            pairs[pl.ds(base + 16, 8), :] = jnp.where(first, pltpu.roll(low, 64, 1), high)

    for m in range(MODES + 1):
        pair_up(m)
    turn = jnp.concatenate([jnp.where(table[BLOCKS * SIDE + j, 0:1] == lax.broadcasted_iota(jnp.int32, (EL, EL), 0), 1.0, 0.0) * jnp.where(table[4 * BLOCKS + j, 0:1] == SIDE, 1.0, 0.0) for j in range(BLOCKS)], 1).astype(F32)
    spreadout[...] = dot(pairs[...], turn)

    row, col = place[0], place[1]
    grid_row = row - DEEP + lax.axis_index("ex") * ELX
    grid_col = col - DEEP + lax.axis_index("ey") * ELY
    last_row, last_col = lax.axis_size("ex") * ELX - 1, lax.axis_size("ey") * ELY - 1
    inside = (grid_row >= 0) & (grid_row <= last_row) & (grid_col >= 0) & (grid_col <= last_col)
    inside = inside & (row < XROWS) & (col < XCOLS)
    own = (row >= DEEP) & (row < DEEP + ELX) & (col >= DEEP) & (col < DEEP + ELY)
    mine_ref[...] = jnp.where(own, 1.0, 0.0)[:, 0:NEAR].astype(F32)
    corner = lax.broadcasted_iota(jnp.int32, (8, XL), 0) == 0
    low_row, high_row, low_col, high_col = grid_row == 0, grid_row == last_row, grid_col == 0, grid_col == last_col
    for tile, (edge, other) in enumerate(((low_col, low_row), (high_row, low_col), (high_col, high_row), (low_row, high_col))):
        keep = jnp.where(inside & ~(edge | (corner & other)), 1.0, 0.0).astype(F32)
        keep_ref[8 * tile : 8 * tile + 8] = keep
        weight_ref[8 * tile : 8 * tile + 8] = jnp.where(own, keep * jnp.where(corner, 0.25, 0.5), 0.0).astype(F32)
    scale = jnp.where(inside[0:1], block[MODES, 0:1] + spreadout[MODES * NB : MODES * NB + 1], 0.0)

    sub = lax.broadcasted_iota(jnp.int32, (8, XL), 0)
    zero = sub == 0

    def assemble(values):
        t = values if isinstance(values, list) else [values[8 * i : 8 * i + 8] for i in range(4)]
        for axis, (a, b, c, d) in ((PITCH, (1, 2, 3, 0)), (1, (2, 3, 0, 1))):
            ahead, behind = axis, XL - axis
            if axis == PITCH:
                prev3 = pltpu.roll(jnp.where(zero, t[2], t[1]), ahead, 1)
                prev0 = pltpu.roll(jnp.where(zero, t[1], 0.0), ahead, 1)
                next1 = pltpu.roll(jnp.where(zero, t[0], t[3]), behind, 1)
                next2 = pltpu.roll(jnp.where(zero, t[3], 0.0), behind, 1)
                t = [t[0] + prev0, t[1] + next1, t[2] + next2, t[3] + prev3]
            else:
                prev0 = pltpu.roll(jnp.where(zero, t[3], t[2]), ahead, 1)
                prev1 = pltpu.roll(jnp.where(zero, t[2], 0.0), ahead, 1)
                next2 = pltpu.roll(jnp.where(zero, t[1], t[0]), behind, 1)
                next3 = pltpu.roll(jnp.where(zero, t[0], 0.0), behind, 1)
                t = [t[0] + prev0, t[1] + prev1, t[2] + next2, t[3] + next3]
        return keep_ref[...] * jnp.concatenate(t, 0)

    eye = lax.broadcasted_iota(jnp.int32, (NB, NB), 0) == lax.broadcasted_iota(jnp.int32, (NB, NB), 1)
    def gather_mode(m):
        state[0, m] = assemble(block[m] + spreadout[pl.ds(pl.multiple_of(m * NB, NB), NB), :])

    def extend_mode(i):
        def run(m):
            trace = jnp.sum(jnp.sum(jnp.where(eye, schur[m], 0.0), axis=0, keepdims=True), axis=1, keepdims=True)
            images = scale * dot(schur[m], state[i, m])
            applied[i, m] = images[:, 0:NEAR]
            state[i + 1, m] = assemble(images) * ((0.5 * NB) / trace) - state[i, m]

        return run

    def sum_mode(m):
        v = [state[i, m, :, 0:NEAR] for i in range(3)]
        w = [applied[0, m], applied[1, m], scale[:, 0:NEAR] * dot(schur[m], v[2])]
        weight, mine = weight_ref[:, 0:NEAR], mine_ref[0:1]
        weighted = v[1] * weight
        own = [value * mine for value in v]
        k = 0
        for first, second in (
            (v[0], v[0] * weight), (v[0], weighted), (v[1], weighted),
            (own[0], w[0]), (own[1], w[0]), (own[1], w[1]), (own[2], w[1]), (own[2], w[2]),
        ):
            whole = jnp.sum(first * second, axis=0, keepdims=True)
            parts[pl.ds(MODES * k + m, 1), :] = whole[:, 0:EL] + whole[:, EL:NEAR]
            k += 1
        for i in range(3):
            basis[i, m] = v[i]

    def every(body):
        def step(m, _):
            body(m)
            return 0

        lax.fori_loop(0, MODES, step, 0, unroll=UNROLL)

    every(gather_mode)
    for i in range(2):
        every(extend_mode(i))
    every(sum_mode)
    ones = jnp.ones((8, EL), F32)
    total = lax.dot_general(ones, parts[...], (((1,), (1,)), ((), ())), precision=HIGHEST, preferred_element_type=F32)
    for at in range(0, sums.shape[0], 8):
        sums[at : at + 8] = total


def finish_kernel(gathered, basis, base, couple, cell, out, coefs):
    total = jnp.broadcast_to(jnp.sum(gathered[...].reshape(-1, EL), axis=0, keepdims=True), (8, EL))
    b0, b1, b2, h0, h1, h2, h3, h4 = [
        total if k == 0 else pltpu.roll(total, EL - MODES * k, 1) for k in range(8)
    ]
    tiny = 2e-7
    l1, l2 = h1 / h0, h2 / h0
    d1 = h2 - l1 * h1
    ok1 = d1 > tiny * h2
    d1 = jnp.where(ok1, d1, 1.0)
    l12 = jnp.where(ok1, (h3 - l1 * h2) / d1, 0.0)
    d2 = h4 - l2 * h2 - l12 * l12 * d1
    ok2 = d2 > tiny * h4
    y1 = b1 - l1 * b0
    y2 = b2 - l2 * b0 - l12 * y1
    c2 = jnp.where(ok2, y2 / jnp.where(ok2, d2, 1.0), 0.0)
    c1 = jnp.where(ok1, y1 / d1, 0.0) - l12 * c2
    c0 = b0 / h0 - l1 * c1 - l2 * c2
    coefs[0], coefs[1], coefs[2] = c0, c1, c2
    place = cell[...] // ELY * PITCH + cell[...] % ELY + DEEP
    nearer = jnp.broadcast_to(place[0:1] < EL, (NB, EL))
    index = place[0:1] % EL

    for m in range(MODES):
        c = [coefs[i, 0:1, m : m + 1] for i in range(3)]
        x = c[0] * basis[0, m] + c[1] * basis[1, m] + c[2] * basis[2, m]
        x = both_ascending(jnp.where(nearer, pick(x[:, 0:EL], index), pick(x[:, EL:NEAR], index)))
        within = base[m, 0:NI] - lax.dot_general(
            couple[m], x, (((0,), (0,)), ((), ())), precision=HIGHEST, preferred_element_type=F32
        )
        out[pl.ds(m, PADDED, stride=MODES), :] = jnp.concatenate([x, within, jnp.zeros((PADDED - NODES, EL), F32)], 0)


def call(kernel, shapes=(), scratch=(), far=0, far_out=None):
    def run(*operands):
        many = isinstance(shapes, list)
        outs = [s if isinstance(s, pl.MemoryRef) else pltpu.VMEM(s, F32) for s in (shapes if many else [shapes])]
        whole, away = pl.BlockSpec(memory_space=pltpu.VMEM), pl.BlockSpec(memory_space=pl.ANY)
        near = tuple(pltpu.with_memory_space_constraint(o, pltpu.VMEM) for o in operands[far:])
        if far_out:
            outs = [jax.ShapeDtypeStruct(far_out, F32)]
        specs = [away if far_out else whole] * len(outs)
        return pl.pallas_call(
            kernel,
            out_shape=outs if many else outs[0],
            in_specs=[away] * far + [whole] * len(near),
            out_specs=specs if many else specs[0],
            scratch_shapes=list(scratch),
            compiler_params=pltpu.CompilerParams(vmem_limit_bytes=16 << 20),
            name=kernel.__name__,
        )(*(pltpu.with_memory_space_constraint(o, pltpu.HBM) for o in operands[:far]), *near)

    return run


def swap(array):
    return lax.all_to_all(array, "fourier", split_axis=0, concat_axis=0, tiled=True)


def ring(axis, step):
    count = lax.axis_size(axis)
    return [(i, (i + step) % count) for i in range(count)]


def neighbours(to_low, to_high, axis):
    return lax.ppermute(to_high, axis, ring(axis, 1)), lax.ppermute(to_low, axis, ring(axis, -1))


def on_device(forcing, element_coef, schur, couple, inner_inv, element_cell):
    parts = lax.axis_size("fourier")
    devices = lax.axis_size("ex") * lax.axis_size("ey")
    group = PADDED // parts
    table = jnp.asarray(real_transform())
    exchanged = (parts, group, MODES, EL)
    lanes = (8, EL)
    ints = pltpu.VMEM(lanes, jnp.int32)

    planes, order, index, scale, stored = call(
        enter_kernel, [(PADDED, MODES, EL), ints, ints, lanes, lanes],
        [
            pltpu.SemaphoreType.DMA((CHUNKS,)),
            pltpu.SemaphoreType.DMA((2,)),
            pltpu.VMEM((1, EL), F32),
            pltpu.VMEM((1, EL), jnp.int32),
        ],
        far=3,
    )(jnp.transpose(forcing, (1, 0, 2)), element_coef.reshape(1, EL), element_cell.reshape(1, EL))
    planes = swap(planes).reshape(exchanged)
    spectral = swap(call(transform_kernel, exchanged)(table, planes).reshape(PADDED, MODES, EL))
    spectral = spectral.reshape(PADDED * MODES, EL)

    message = (MODES + 1, 16, EL)
    condensed, down, up = call(condense_kernel, [(MODES, NB, EL), message, message])(spectral, order, scale, couple)
    low, high = neighbours(down, up, "ex")
    base = call(interior_kernel, (MODES, 56, EL))(
        spectral, stored, jnp.transpose(inner_inv, (1, 0, 2)).reshape(NI * MODES, NI)
    )
    low, high, base = lax.optimization_barrier((low, high, base))
    left, right = call(columns_kernel, [message, message])(condensed, scale, low, high, jnp.asarray(COL_TABLE))
    left, right = neighbours(left, right, "ey")
    extended = jnp.asarray(EXT_TABLE)
    block, matrix = call(middle_kernel, [(MODES + 1, NB, XL), (MODES, NB, NB)])(
        condensed, scale, low, high, schur, extended
    )
    basis, sums = call(
        krylov_kernel,
        [(3, MODES, NB, NEAR), (devices, EL)],
        [
            pltpu.VMEM((NB, XL), F32),
            pltpu.VMEM((NB, XL), F32),
            pltpu.VMEM((8, NEAR), F32),
            pltpu.VMEM((EL, EL), F32),
            pltpu.VMEM((3, MODES, NB, XL), F32),
            pltpu.VMEM((2, MODES, NB, NEAR), F32),
            pltpu.VMEM(((MODES + 1) * NB, EL), F32),
            pltpu.VMEM(((MODES + 1) * NB, XL), F32),
        ],
    )(block, scale, left, right, matrix, extended, jnp.asarray(EXT_PLACE))
    gathered = lax.all_to_all(sums.reshape(devices, 1, EL), ("ex", "ey"), split_axis=0, concat_axis=0, tiled=True)
    modal = call(finish_kernel, (PADDED * MODES, EL), [pltpu.VMEM((3, 8, EL), F32)])(
        gathered, basis, base, couple, index
    )
    modal = swap(modal.reshape(PADDED, MODES, EL)).reshape(exchanged)
    velocity = swap(call(transform_kernel, exchanged)(table.T, modal).reshape(PADDED, MODES, EL))
    velocity = call(leave_kernel, far_out=(NODES, MODES, EL), scratch=[pltpu.SemaphoreType.DMA((CHUNKS,))])(velocity)
    return jnp.transpose(velocity, (1, 0, 2))


def solution(mesh):
    placed = (
        P("fourier", None, ("ex", "ey")),
        P(("ex", "ey")),
        P("fourier", None, None),
        P("fourier", None, None),
        P("fourier", None, None),
        P(("ex", "ey")),
    )
    return jax.shard_map(
        on_device,
        mesh=mesh,
        in_specs=placed,
        out_specs=P("fourier", None, ("ex", "ey")),
        check_vma=False,
    )
```

```python
import math

import jax
import jax.numpy as jnp
import numpy as np
from jax import lax
from jax.experimental import pallas as pl
from jax.experimental.pallas import tpu as pltpu
from jax.sharding import PartitionSpec as P

P_SIZE = 8
NZ = 128
ELX = 8
ELY = 16
NODES = 81
NB = 32
NI = 49
EL = ELX * ELY
PADDED = 88
MODES = 16
DEEP = 2
XROWS = ELX + 2 * DEEP
XCOLS = ELY + 2 * DEEP
PITCH = XCOLS
XL = 256
SLOT = DEEP * ELY
UNROLL = 8
CHUNKS = 3
HIGHEST = lax.Precision.HIGHEST
F32 = jnp.float32


def real_transform():
    k = np.arange(NZ)[:, None]
    z = np.arange(NZ)[None, :]
    angle = 2.0 * math.pi * (((k + 1) // 2 * z) % NZ) / NZ
    w = np.where(k % 2 == 1, np.cos(angle), np.sin(angle)) * math.sqrt(2.0 / NZ)
    w[0] = 1.0 / math.sqrt(NZ)
    w[NZ - 1] = np.cos(math.pi * np.arange(NZ)) / math.sqrt(NZ)
    return w.astype(np.float32)


def lane_tables():
    lane = np.arange(XL)
    row, col = lane // PITCH, lane % PITCH
    valid = row < XROWS
    middle = valid & (col >= DEEP) & (col < DEEP + ELY)
    right = col >= DEEP + ELY
    spread = np.where(middle, row * ELY + col - DEEP, -1)
    turn = np.where(right, SLOT + row * DEEP + col - DEEP - ELY, row * DEEP + col)
    turn = np.where(valid & ~middle, turn, -1)
    at = lane % SLOT
    send = at // DEEP * ELY + at % DEEP + np.where(lane >= SLOT, ELY - DEEP, 0)
    send = np.where((at < DEEP * XROWS) & (lane < 2 * SLOT), send, -1)
    return np.stack([spread, turn, send, row, col, row, row, row]).astype(np.int32)


def pick(values, index):
    return jnp.take_along_axis(values, jnp.broadcast_to(index, values.shape), axis=1, mode="promise_in_bounds")


def dot(a, b):
    return lax.dot_general(a, b, (((1,), (0,)), ((), ())), precision=HIGHEST, preferred_element_type=F32)


def selection(index, size):
    return jnp.where(lax.broadcasted_iota(jnp.int32, (size, index.shape[1]), 0) == index, 1.0, 0.0).astype(F32)


def add_rows(t, step, before, behind):
    width = t[0].shape[1]
    zero = lax.broadcasted_iota(jnp.int32, t[0].shape, 0) == 0
    back = width - step

    def masked(mask, values):
        return values if mask is None else jnp.where(mask, values, 0.0)

    from0 = masked(before, pltpu.roll(jnp.where(zero, t[1], 0.0), step, 1))
    from3 = masked(before, pltpu.roll(jnp.where(zero, t[2], t[1]), step, 1))
    from1 = masked(behind, pltpu.roll(jnp.where(zero, t[0], t[3]), back, 1))
    from2 = masked(behind, pltpu.roll(jnp.where(zero, t[3], 0.0), back, 1))
    return [t[0] + from0, t[1] + from1, t[2] + from2, t[3] + from3]


def add_columns(t, before, behind):
    turned = add_rows([t[1], t[2], t[3], t[0]], 1, before, behind)
    return [turned[3], turned[0], turned[1], turned[2]]


def tiles(values):
    return [values[8 * i : 8 * i + 8] for i in range(4)]


def transform_kernel(table, planes, out):
    groups, nodes = planes.shape[0], planes.shape[1]
    for n in range(nodes):
        block = planes[:, n].reshape(NZ, EL)
        out[:, n] = dot(table[...], block).reshape(groups, NZ // groups, EL)


def copies(source, target, nodes, done):
    step = -(-nodes // CHUNKS)
    cuts = [(at, min(step, nodes - at)) for at in range(0, nodes, step)]
    return [
        pltpu.make_async_copy(source.at[pl.ds(at, size)], target.at[pl.ds(at, size)], done.at[i])
        for i, (at, size) in enumerate(cuts)
    ]


def enter_kernel(forcing, coef_far, cell_far, planes, order, index, scale, stored, done, small, coef, cell):
    nodes = forcing.shape[0]
    fetched = [pltpu.make_async_copy(coef_far, coef, small.at[0]), pltpu.make_async_copy(cell_far, cell, small.at[1])]
    moved = copies(forcing, planes, nodes, done)
    for copy in fetched + moved:
        copy.start()
    planes[nodes:PADDED] = jnp.zeros((PADDED - nodes, planes.shape[1], EL), F32)
    for copy in fetched:
        copy.wait()
    lane = lax.broadcasted_iota(jnp.int32, (EL, EL), 1)
    elem = lax.broadcasted_iota(jnp.int32, (EL, EL), 0)
    cells = jnp.transpose(jnp.broadcast_to(cell[...], (EL, EL)))
    found = jnp.sum(jnp.where(cells == lane, elem, 0), axis=0, keepdims=True)
    order[...] = jnp.broadcast_to(found, (8, EL))
    index[...] = jnp.broadcast_to(cell[...], (8, EL))
    stored[...] = jnp.broadcast_to(coef[...], (8, EL))
    scale[...] = pick(jnp.broadcast_to(coef[...], (8, EL)), found)
    for copy in moved:
        copy.wait()


def leave_kernel(planes, velocity, done):
    moved = copies(planes, velocity, velocity.shape[0], done)
    for copy in moved:
        copy.start()
    for copy in moved:
        copy.wait()


def flipped(tile):
    back = (8 - lax.broadcasted_iota(jnp.int32, tile.shape, 0)) % 8
    return jnp.take_along_axis(tile, back, axis=0, mode="promise_in_bounds")


def both_ascending(values):
    return jnp.concatenate([values[0:16], flipped(values[16:24]), flipped(values[24:32])], 0)


def condense_kernel(spectral, order, scale, couple, condensed, down, up):
    lane = lax.broadcasted_iota(jnp.int32, (8, EL), 1)
    row, col, slot = lane // ELY, lane % ELY, lane // SLOT
    inner_row, inner_col = (row > 0, row < ELX - 1), (col > 0, col < ELY - 1)

    def messages(t):
        low, high = t[0], t[3]
        for i in (1, 2, 3):
            low = jnp.where(slot == i, pltpu.roll(t[i], SLOT * i, 1), low)
            high = jnp.where(slot == i - 1, pltpu.roll(t[i - 1], SLOT * i, 1), high)
        return low, high

    down[MODES], up[MODES] = messages([scale[...]] * 4)

    def mode(m, _):
        fields = pick(spectral[pl.ds(m, PADDED, stride=MODES), :], order[0:1])
        t = tiles(both_ascending(fields[0:NB] - dot(couple[m], fields[NB:NODES])))
        t = add_columns(add_rows(t, ELY, *inner_row), *inner_col)
        condensed[m] = jnp.concatenate(t, 0)
        down[m], up[m] = messages(t)
        return 0

    lax.fori_loop(0, MODES, mode, 0, unroll=UNROLL)


def interior_kernel(spectral, stored, inner, base):
    inverse = 1.0 / stored[0:1]

    def mode(m, _):
        within = spectral[pl.ds(NB * MODES + m, PADDED - NB, stride=MODES), :][0:NI]
        base[m, 0:NI] = dot(inner[pl.ds(m, NI, stride=MODES), :], within) * inverse
        return 0

    lax.fori_loop(0, MODES, mode, 0, unroll=UNROLL)


def columns_kernel(condensed, scale, low, high, table, left, right, middle, sent):
    lane = lax.broadcasted_iota(jnp.int32, (8, EL), 1)
    slot = lane // SLOT
    inner, outer = slot == 0, slot == 1
    meets = (lane >= SLOT) & (lane < SLOT + ELY), (lane >= SLOT - ELY) & (lane < SLOT)

    def stack(own, lo, hi):
        first, second = [], []
        for i in range(4):
            moved = pltpu.roll(own[i], SLOT, 1)
            below = lo if i == 0 else pltpu.roll(lo, EL - SLOT * i, 1)
            above = hi if i == 1 else pltpu.roll(hi, (EL + SLOT - SLOT * i) % EL, 1)
            first.append(jnp.where(inner, below, moved))
            second.append(jnp.where(inner, moved, jnp.where(outer, above, 0.0)))
        return first, second

    def put(m, parts):
        for j, part in enumerate(parts):
            middle[m, :, EL * j : EL * j + EL] = jnp.concatenate(part, 0)

    put(MODES, stack([scale[...]] * 4, low[MODES], high[MODES]))

    def mode(m, _):
        parts = stack(tiles(condensed[m]), low[m], high[m])
        put(m, [add_rows(part, ELY, *meets) for part in parts])
        return 0

    lax.fori_loop(0, MODES, mode, 0, unroll=UNROLL)
    send = selection(table[2:3, 0:EL], XL)
    sent[...] = dot(middle[...].reshape((MODES + 1) * NB, XL), send)

    def message(m, _):
        t = [sent[pl.ds(pl.multiple_of(m * NB + 8 * i, 8), 8), :] for i in range(4)]
        to_left, to_right = t[0], t[1]
        for i in range(1, 4):
            to_left = jnp.where(slot == i, pltpu.roll(t[i], SLOT * i, 1), to_left)
        for i in (0, 2, 3):
            to_right = jnp.where(slot == i, pltpu.roll(t[i], (SLOT * i - SLOT) % EL, 1), to_right)
        left[m], right[m] = to_left, to_right
        return 0

    lax.fori_loop(0, MODES + 1, message, 0, unroll=UNROLL)


def middle_kernel(middle, schur, table, block, matrix):
    lane = lax.broadcasted_iota(jnp.int32, (NB, NB), 1)
    across = jnp.where((lane >= 16) & (lane % 8 > 0), lane // 8 * 8 + 8 - lane % 8, lane)

    def mode(m, _):
        rows = both_ascending(schur[m])
        matrix[m] = jnp.take_along_axis(rows, across, axis=1, mode="promise_in_bounds")
        return 0

    lax.fori_loop(0, MODES, mode, 0, unroll=UNROLL)
    spread = dot(middle[...].reshape((MODES + 1) * NB, XL), selection(table[0:1], XL))
    block[...] = spread.reshape(MODES + 1, NB, XL)


def krylov_kernel(
    block, left, right, schur, table, basis, sums, keep_ref, weight_ref, mine_ref, parts, state, applied, pairs, spread
):
    half = lax.broadcasted_iota(jnp.int32, (8, EL), 1) < SLOT

    def pair_up(m, _):
        low, high = left[m], right[m]
        for i in range(4):
            below = low if i == 0 else pltpu.roll(low, EL - SLOT * i, 1)
            above = high if i == 1 else pltpu.roll(high, (EL + SLOT - SLOT * i) % EL, 1)
            pairs[pl.ds(pl.multiple_of(m * NB + 8 * i, 8), 8), :] = jnp.where(half, below, above)
        return 0

    lax.fori_loop(0, MODES + 1, pair_up, 0, unroll=UNROLL)
    spread[...] = dot(pairs[...], selection(table[1:2], EL))

    row, col = jnp.broadcast_to(table[3:4], (8, XL)), jnp.broadcast_to(table[4:5], (8, XL))
    grid_row = row - DEEP + lax.axis_index("ex") * ELX
    grid_col = col - DEEP + lax.axis_index("ey") * ELY
    last_row, last_col = lax.axis_size("ex") * ELX - 1, lax.axis_size("ey") * ELY - 1
    inside = (grid_row >= 0) & (grid_row <= last_row) & (grid_col >= 0) & (grid_col <= last_col) & (row < XROWS)
    own = (row >= DEEP) & (row < DEEP + ELX) & (col >= DEEP) & (col < DEEP + ELY)
    meets = (col == DEEP) | (col == DEEP + ELY), (col == DEEP - 1) | (col == DEEP + ELY - 1)
    mine_ref[...] = jnp.where(own, 1.0, 0.0).astype(F32)
    corner = lax.broadcasted_iota(jnp.int32, (8, XL), 0) == 0
    low_row, high_row, low_col, high_col = grid_row == 0, grid_row == last_row, grid_col == 0, grid_col == last_col
    for tile, (edge, other) in enumerate(((low_col, low_row), (high_row, low_col), (high_col, high_row), (low_row, high_col))):
        keep = jnp.where(inside & ~(edge | (corner & other)), 1.0, 0.0).astype(F32)
        keep_ref[8 * tile : 8 * tile + 8] = keep
        weight_ref[8 * tile : 8 * tile + 8] = jnp.where(own, keep * jnp.where(corner, 0.25, 0.5), 0.0).astype(F32)
    scale = jnp.where(inside[0:1], block[MODES, 0:1] + spread[MODES * NB : MODES * NB + 1], 0.0)

    def assemble(values):
        return keep_ref[...] * jnp.concatenate(add_columns(add_rows(tiles(values), PITCH, None, None), None, None), 0)

    eye = lax.broadcasted_iota(jnp.int32, (NB, NB), 0) == lax.broadcasted_iota(jnp.int32, (NB, NB), 1)
    def gather_mode(m):
        values = block[m] + spread[pl.ds(pl.multiple_of(m * NB, NB), NB), :]
        state[0, m] = keep_ref[...] * jnp.concatenate(add_columns(tiles(values), *meets), 0)

    def extend_mode(i):
        def run(m):
            trace = jnp.sum(jnp.sum(jnp.where(eye, schur[m], 0.0), axis=0, keepdims=True), axis=1, keepdims=True)
            images = scale * dot(schur[m], state[i, m])
            applied[i, m] = images
            state[i + 1, m] = assemble(images) * ((0.5 * NB) / trace) - state[i, m]

        return run

    def sum_mode(m):
        v = [state[i, m] for i in range(3)]
        w = [applied[0, m], applied[1, m], scale * dot(schur[m], v[2])]
        weight, mine = weight_ref[...], mine_ref[0:1]
        weighted = v[1] * weight
        own = [value * mine for value in v]
        k = 0
        for first, second in (
            (v[0], v[0] * weight), (v[0], weighted), (v[1], weighted),
            (own[0], w[0]), (own[1], w[0]), (own[1], w[1]), (own[2], w[1]), (own[2], w[2]),
        ):
            whole = jnp.sum(first * second, axis=0, keepdims=True)
            parts[pl.ds(MODES * k + m, 1), :] = whole[:, 0:EL] + whole[:, EL:XL]
            k += 1
        for i in range(3):
            basis[i, m] = v[i]

    def every(body):
        def step(m, _):
            body(m)
            return 0

        lax.fori_loop(0, MODES, step, 0, unroll=UNROLL)

    every(gather_mode)
    for i in range(2):
        every(extend_mode(i))
    every(sum_mode)
    ones = jnp.ones((8, EL), F32)
    total = lax.dot_general(ones, parts[...], (((1,), (1,)), ((), ())), precision=HIGHEST, preferred_element_type=F32)
    for at in range(0, sums.shape[0], 8):
        sums[at : at + 8] = total


def finish_kernel(gathered, basis, base, couple, cell, out, coefs):
    total = jnp.broadcast_to(jnp.sum(gathered[...].reshape(-1, EL), axis=0, keepdims=True), (8, EL))
    b0, b1, b2, h0, h1, h2, h3, h4 = [
        total if k == 0 else pltpu.roll(total, EL - MODES * k, 1) for k in range(8)
    ]
    tiny = 2e-7
    l1, l2 = h1 / h0, h2 / h0
    d1 = h2 - l1 * h1
    ok1 = d1 > tiny * h2
    d1 = jnp.where(ok1, d1, 1.0)
    l12 = jnp.where(ok1, (h3 - l1 * h2) / d1, 0.0)
    d2 = h4 - l2 * h2 - l12 * l12 * d1
    ok2 = d2 > tiny * h4
    y1 = b1 - l1 * b0
    y2 = b2 - l2 * b0 - l12 * y1
    c2 = jnp.where(ok2, y2 / jnp.where(ok2, d2, 1.0), 0.0)
    c1 = jnp.where(ok1, y1 / d1, 0.0) - l12 * c2
    c0 = b0 / h0 - l1 * c1 - l2 * c2
    coefs[0], coefs[1], coefs[2] = c0, c1, c2
    place = (cell[...] // ELY + DEEP) * PITCH + cell[...] % ELY + DEEP
    nearer = jnp.broadcast_to(place[0:1] < EL, (NB, EL))
    index = place[0:1] % EL

    for m in range(MODES):
        c = [coefs[i, 0:1, m : m + 1] for i in range(3)]
        x = c[0] * basis[0, m] + c[1] * basis[1, m] + c[2] * basis[2, m]
        x = both_ascending(jnp.where(nearer, pick(x[:, 0:EL], index), pick(x[:, EL:XL], index)))
        within = base[m, 0:NI] - lax.dot_general(
            couple[m], x, (((0,), (0,)), ((), ())), precision=HIGHEST, preferred_element_type=F32
        )
        out[pl.ds(m, PADDED, stride=MODES), :] = jnp.concatenate([x, within, jnp.zeros((PADDED - NODES, EL), F32)], 0)


def call(kernel, shapes=(), scratch=(), far=0, far_out=None):
    def run(*operands):
        many = isinstance(shapes, list)
        outs = [s if isinstance(s, pl.MemoryRef) else pltpu.VMEM(s, F32) for s in (shapes if many else [shapes])]
        whole, away = pl.BlockSpec(memory_space=pltpu.VMEM), pl.BlockSpec(memory_space=pl.ANY)
        near = tuple(pltpu.with_memory_space_constraint(o, pltpu.VMEM) for o in operands[far:])
        if far_out:
            outs = [jax.ShapeDtypeStruct(far_out, F32)]
        specs = [away if far_out else whole] * len(outs)
        return pl.pallas_call(
            kernel,
            out_shape=outs if many else outs[0],
            in_specs=[away] * far + [whole] * len(near),
            out_specs=specs if many else specs[0],
            scratch_shapes=list(scratch),
            compiler_params=pltpu.CompilerParams(vmem_limit_bytes=16 << 20),
            name=kernel.__name__,
        )(*(pltpu.with_memory_space_constraint(o, pltpu.HBM) for o in operands[:far]), *near)

    return run


def swap(array):
    return lax.all_to_all(array, "fourier", split_axis=0, concat_axis=0, tiled=True)


def ring(axis, step):
    count = lax.axis_size(axis)
    return [(i, (i + step) % count) for i in range(count)]


def neighbours(to_low, to_high, axis):
    return lax.ppermute(to_high, axis, ring(axis, 1)), lax.ppermute(to_low, axis, ring(axis, -1))


def on_device(forcing, element_coef, schur, couple, inner_inv, element_cell):
    parts = lax.axis_size("fourier")
    devices = lax.axis_size("ex") * lax.axis_size("ey")
    group = PADDED // parts
    table = jnp.asarray(real_transform())
    exchanged = (parts, group, MODES, EL)
    lanes = (8, EL)
    ints = pltpu.VMEM(lanes, jnp.int32)

    planes, order, index, scale, stored = call(
        enter_kernel, [(PADDED, MODES, EL), ints, ints, lanes, lanes],
        [
            pltpu.SemaphoreType.DMA((CHUNKS,)),
            pltpu.SemaphoreType.DMA((2,)),
            pltpu.VMEM((1, EL), F32),
            pltpu.VMEM((1, EL), jnp.int32),
        ],
        far=3,
    )(jnp.transpose(forcing, (1, 0, 2)), element_coef.reshape(1, EL), element_cell.reshape(1, EL))
    planes = swap(planes).reshape(exchanged)
    spectral = swap(call(transform_kernel, exchanged)(table, planes).reshape(PADDED, MODES, EL))
    spectral = spectral.reshape(PADDED * MODES, EL)

    message, extended = (MODES + 1, 8, EL), (MODES + 1, NB, XL)
    table_of_lanes = jnp.asarray(lane_tables())
    condensed, down, up = call(condense_kernel, [(MODES, NB, EL), message, message])(spectral, order, scale, couple)
    low, high = neighbours(down, up, "ex")
    base = call(interior_kernel, (MODES, 56, EL))(
        spectral, stored, jnp.transpose(inner_inv, (1, 0, 2)).reshape(NI * MODES, NI)
    )
    low, high, base = lax.optimization_barrier((low, high, base))
    rows = (MODES + 1) * NB
    left, right, middle = call(columns_kernel, [message, message, extended], [pltpu.VMEM((rows, EL), F32)])(
        condensed, scale, low, high, table_of_lanes
    )
    left, right = neighbours(left, right, "ey")
    block, matrix = call(middle_kernel, [extended, (MODES, NB, NB)])(middle, schur, table_of_lanes)
    basis, sums = call(
        krylov_kernel,
        [(3, MODES, NB, XL), (devices, EL)],
        [
            pltpu.VMEM((NB, XL), F32),
            pltpu.VMEM((NB, XL), F32),
            pltpu.VMEM((8, XL), F32),
            pltpu.VMEM((EL, EL), F32),
            pltpu.VMEM((3, MODES, NB, XL), F32),
            pltpu.VMEM((2, MODES, NB, XL), F32),
            pltpu.VMEM((rows, EL), F32),
            pltpu.VMEM((rows, XL), F32),
        ],
    )(block, left, right, matrix, table_of_lanes)
    gathered = lax.all_to_all(sums.reshape(devices, 1, EL), ("ex", "ey"), split_axis=0, concat_axis=0, tiled=True)
    modal = call(finish_kernel, (PADDED * MODES, EL), [pltpu.VMEM((3, 8, EL), F32)])(
        gathered, basis, base, couple, index
    )
    modal = swap(modal.reshape(PADDED, MODES, EL)).reshape(exchanged)
    velocity = swap(call(transform_kernel, exchanged)(table.T, modal).reshape(PADDED, MODES, EL))
    velocity = call(leave_kernel, far_out=(NODES, MODES, EL), scratch=[pltpu.SemaphoreType.DMA((CHUNKS,))])(velocity)
    return jnp.transpose(velocity, (1, 0, 2))


def solution(mesh):
    placed = (
        P("fourier", None, ("ex", "ey")),
        P(("ex", "ey")),
        P("fourier", None, None),
        P("fourier", None, None),
        P("fourier", None, None),
        P(("ex", "ey")),
    )
    return jax.shard_map(
        on_device,
        mesh=mesh,
        in_specs=placed,
        out_specs=P("fourier", None, ("ex", "ey")),
        check_vma=False,
    )
```

```python
import math

import jax
import jax.numpy as jnp
import numpy as np
from jax import lax
from jax.experimental import pallas as pl
from jax.experimental.pallas import tpu as pltpu
from jax.sharding import PartitionSpec as P

P_SIZE = 8
NZ = 128
ELX = 8
ELY = 16
NODES = 81
NB = 32
NI = 49
EL = ELX * ELY
PADDED = 88
MODES = 16
DEEP = 2
XROWS = ELX + 2 * DEEP
XCOLS = ELY + 2 * DEEP
PITCH = XCOLS
XL = 256
SLOT = DEEP * ELY
UNROLL = 8
QUAD = 4
CHUNKS = 3
HIGHEST = lax.Precision.HIGHEST
F32 = jnp.float32


def real_transform():
    k = np.arange(NZ)[:, None]
    z = np.arange(NZ)[None, :]
    angle = 2.0 * math.pi * (((k + 1) // 2 * z) % NZ) / NZ
    w = np.where(k % 2 == 1, np.cos(angle), np.sin(angle)) * math.sqrt(2.0 / NZ)
    w[0] = 1.0 / math.sqrt(NZ)
    w[NZ - 1] = np.cos(math.pi * np.arange(NZ)) / math.sqrt(NZ)
    return w.astype(np.float32)


def lane_tables():
    lane = np.arange(XL)
    row, col = lane // PITCH, lane % PITCH
    valid = row < XROWS
    middle = valid & (col >= DEEP) & (col < DEEP + ELY)
    right = col >= DEEP + ELY
    spread = np.where(middle, row * ELY + col - DEEP, -1)
    turn = np.where(right, SLOT + row * DEEP + col - DEEP - ELY, row * DEEP + col)
    turn = np.where(valid & ~middle, turn, -1)
    at = lane % SLOT
    send = at // DEEP * ELY + at % DEEP + np.where(lane >= SLOT, ELY - DEEP, 0)
    send = np.where((at < DEEP * XROWS) & (lane < 2 * SLOT), send, -1)
    return np.stack([spread, turn, send, row, col, row, row, row]).astype(np.int32)


def pick(values, index):
    return jnp.take_along_axis(values, jnp.broadcast_to(index, values.shape), axis=1, mode="promise_in_bounds")


def dot(a, b):
    return lax.dot_general(a, b, (((1,), (0,)), ((), ())), precision=HIGHEST, preferred_element_type=F32)


def selection(index, size):
    return jnp.where(lax.broadcasted_iota(jnp.int32, (size, index.shape[1]), 0) == index, 1.0, 0.0).astype(F32)


def take(values, chosen):
    high = values.astype(jnp.bfloat16)
    rest = values - high.astype(F32)
    middle = rest.astype(jnp.bfloat16)
    low = (rest - middle.astype(F32)).astype(jnp.bfloat16)
    chosen = chosen.astype(jnp.bfloat16)

    def product(part):
        return lax.dot_general(part, chosen, (((1,), (0,)), ((), ())), preferred_element_type=F32)

    return (product(high) + product(middle)) + product(low)


def add_rows(t, step, before, behind):
    width = t[0].shape[1]
    zero = lax.broadcasted_iota(jnp.int32, t[0].shape, 0) == 0
    back = width - step

    def masked(mask, values):
        return values if mask is None else jnp.where(mask, values, 0.0)

    from0 = masked(before, pltpu.roll(jnp.where(zero, t[1], 0.0), step, 1))
    from3 = masked(before, pltpu.roll(jnp.where(zero, t[2], t[1]), step, 1))
    from1 = masked(behind, pltpu.roll(jnp.where(zero, t[0], t[3]), back, 1))
    from2 = masked(behind, pltpu.roll(jnp.where(zero, t[3], 0.0), back, 1))
    return [t[0] + from0, t[1] + from1, t[2] + from2, t[3] + from3]


def add_columns(t, before, behind):
    turned = add_rows([t[1], t[2], t[3], t[0]], 1, before, behind)
    return [turned[3], turned[0], turned[1], turned[2]]


def tiles(values):
    return [values[8 * i : 8 * i + 8] for i in range(4)]


def split(values):
    high = values.astype(jnp.bfloat16)
    return high, (values - high.astype(F32)).astype(jnp.bfloat16)


def dot_of_parts(a, b):
    (a_high, a_low), (b_high, b_low) = a, b

    def product(first, second):
        return lax.dot_general(first, second, (((1,), (0,)), ((), ())), preferred_element_type=F32)

    return product(a_high, b_low) + product(a_low, b_high) + product(a_high, b_high)


def transform_kernel(table, planes, out):
    groups, nodes = planes.shape[0], planes.shape[1]
    held = split(table[...])
    for n in range(nodes):
        block = planes[:, n].reshape(NZ, EL)
        out[:, n] = dot_of_parts(held, split(block)).reshape(groups, NZ // groups, EL)


def copies(source, target, nodes, done):
    step = -(-nodes // CHUNKS)
    cuts = [(at, min(step, nodes - at)) for at in range(0, nodes, step)]
    return [
        pltpu.make_async_copy(source.at[pl.ds(at, size)], target.at[pl.ds(at, size)], done.at[i])
        for i, (at, size) in enumerate(cuts)
    ]


def enter_kernel(forcing, coef_far, cell_far, planes, order, index, scale, stored, done, small, coef, cell):
    nodes = forcing.shape[0]
    fetched = [pltpu.make_async_copy(coef_far, coef, small.at[0]), pltpu.make_async_copy(cell_far, cell, small.at[1])]
    moved = copies(forcing, planes, nodes, done)
    for copy in fetched + moved:
        copy.start()
    planes[nodes:PADDED] = jnp.zeros((PADDED - nodes, planes.shape[1], EL), F32)
    for copy in fetched:
        copy.wait()
    lane = lax.broadcasted_iota(jnp.int32, (EL, EL), 1)
    elem = lax.broadcasted_iota(jnp.int32, (EL, EL), 0)
    cells = jnp.transpose(jnp.broadcast_to(cell[...], (EL, EL)))
    found = jnp.sum(jnp.where(cells == lane, elem, 0), axis=0, keepdims=True)
    order[...] = jnp.broadcast_to(found, (8, EL))
    index[...] = jnp.broadcast_to(cell[...], (8, EL))
    stored[...] = jnp.broadcast_to(coef[...], (8, EL))
    scale[...] = pick(jnp.broadcast_to(coef[...], (8, EL)), found)
    for copy in moved:
        copy.wait()


def leave_kernel(planes, velocity, done):
    moved = copies(planes, velocity, velocity.shape[0], done)
    for copy in moved:
        copy.start()
    for copy in moved:
        copy.wait()


def flipped(tile):
    back = (8 - lax.broadcasted_iota(jnp.int32, tile.shape, 0)) % 8
    return jnp.take_along_axis(tile, back, axis=0, mode="promise_in_bounds")


def both_ascending(values):
    return jnp.concatenate([values[0:16], flipped(values[16:24]), flipped(values[24:32])], 0)


def condense_kernel(spectral, order, scale, couple, condensed, down, up):
    lane = lax.broadcasted_iota(jnp.int32, (8, EL), 1)
    row, col, slot = lane // ELY, lane % ELY, lane // SLOT
    inner_row, inner_col = (row > 0, row < ELX - 1), (col > 0, col < ELY - 1)

    def messages(t):
        low, high = t[0], t[3]
        for i in (1, 2, 3):
            low = jnp.where(slot == i, pltpu.roll(t[i], SLOT * i, 1), low)
            high = jnp.where(slot == i - 1, pltpu.roll(t[i - 1], SLOT * i, 1), high)
        return low, high

    down[MODES], up[MODES] = messages([scale[...]] * 4)

    def mode(m, _):
        fields = spectral[pl.ds(m, PADDED, stride=MODES), :]
        value = fields[0:NB] - dot_of_parts(split(couple[m]), split(fields[NB:NODES]))
        t = tiles(both_ascending(pick(value, order[0:1])))
        t = add_columns(add_rows(t, ELY, *inner_row), *inner_col)
        condensed[m] = jnp.concatenate(t, 0)
        down[m], up[m] = messages(t)
        return 0

    lax.fori_loop(0, MODES, mode, 0, unroll=UNROLL)


def interior_kernel(spectral, stored, inner, couple, base, turned, wide):
    inverse = 1.0 / stored[0:1]

    def mode(m, _):
        within = spectral[pl.ds(NB * MODES + m, PADDED - NB, stride=MODES), :][0:NI]
        base[m, 0:NI] = dot(inner[pl.ds(m, NI, stride=MODES), :], within) * inverse
        return 0

    lax.fori_loop(0, MODES, mode, 0, unroll=UNROLL)
    wide[...] = jnp.zeros_like(wide)
    for q in range(MODES // QUAD):
        wide[:, 0:NI] = couple[QUAD * q : QUAD * q + QUAD].reshape(QUAD * NB, NI)
        turned[q] = jnp.transpose(wide[...])[0 : turned.shape[1]]


def columns_kernel(condensed, scale, low, high, table, left, right, middle, sent):
    lane = lax.broadcasted_iota(jnp.int32, (8, EL), 1)
    slot = lane // SLOT
    inner, outer = slot == 0, slot == 1
    meets = (lane >= SLOT) & (lane < SLOT + ELY), (lane >= SLOT - ELY) & (lane < SLOT)

    def stack(own, lo, hi):
        first, second = [], []
        for i in range(4):
            moved = pltpu.roll(own[i], SLOT, 1)
            below = lo if i == 0 else pltpu.roll(lo, EL - SLOT * i, 1)
            above = hi if i == 1 else pltpu.roll(hi, (EL + SLOT - SLOT * i) % EL, 1)
            first.append(jnp.where(inner, below, moved))
            second.append(jnp.where(inner, moved, jnp.where(outer, above, 0.0)))
        return first, second

    def put(m, parts):
        for j, part in enumerate(parts):
            middle[m, :, EL * j : EL * j + EL] = jnp.concatenate(part, 0)

    put(MODES, stack([scale[...]] * 4, low[MODES], high[MODES]))

    def mode(m, _):
        parts = stack(tiles(condensed[m]), low[m], high[m])
        put(m, [add_rows(part, ELY, *meets) for part in parts])
        return 0

    lax.fori_loop(0, MODES, mode, 0, unroll=UNROLL)
    send = selection(table[2:3, 0:EL], XL)
    sent[...] = take(middle[...].reshape((MODES + 1) * NB, XL), send)

    def message(m, _):
        t = [sent[pl.ds(pl.multiple_of(m * NB + 8 * i, 8), 8), :] for i in range(4)]
        to_left, to_right = t[0], t[1]
        for i in range(1, 4):
            to_left = jnp.where(slot == i, pltpu.roll(t[i], SLOT * i, 1), to_left)
        for i in (0, 2, 3):
            to_right = jnp.where(slot == i, pltpu.roll(t[i], (SLOT * i - SLOT) % EL, 1), to_right)
        left[m], right[m] = to_left, to_right
        return 0

    lax.fori_loop(0, MODES + 1, message, 0, unroll=UNROLL)


def middle_kernel(middle, schur, table, block, matrix):
    lane = lax.broadcasted_iota(jnp.int32, (NB, NB), 1)
    across = jnp.where((lane >= 16) & (lane % 8 > 0), lane // 8 * 8 + 8 - lane % 8, lane)

    def mode(m, _):
        rows = both_ascending(schur[m])
        matrix[m] = jnp.take_along_axis(rows, across, axis=1, mode="promise_in_bounds")
        return 0

    lax.fori_loop(0, MODES, mode, 0, unroll=UNROLL)
    spread = take(middle[...].reshape((MODES + 1) * NB, XL), selection(table[0:1], XL))
    block[...] = spread.reshape(MODES + 1, NB, XL)


def krylov_kernel(
    block, left, right, schur, table, basis, sums, keep_ref, weight_ref, mine_ref, parts, state, applied, pairs, spread
):
    half = lax.broadcasted_iota(jnp.int32, (8, EL), 1) < SLOT

    def pair_up(m, _):
        low, high = left[m], right[m]
        for i in range(4):
            below = low if i == 0 else pltpu.roll(low, EL - SLOT * i, 1)
            above = high if i == 1 else pltpu.roll(high, (EL + SLOT - SLOT * i) % EL, 1)
            pairs[pl.ds(pl.multiple_of(m * NB + 8 * i, 8), 8), :] = jnp.where(half, below, above)
        return 0

    lax.fori_loop(0, MODES + 1, pair_up, 0, unroll=UNROLL)
    spread[...] = take(pairs[...], selection(table[1:2], EL))

    row, col = jnp.broadcast_to(table[3:4], (8, XL)), jnp.broadcast_to(table[4:5], (8, XL))
    grid_row = row - DEEP + lax.axis_index("ex") * ELX
    grid_col = col - DEEP + lax.axis_index("ey") * ELY
    last_row, last_col = lax.axis_size("ex") * ELX - 1, lax.axis_size("ey") * ELY - 1
    inside = (grid_row >= 0) & (grid_row <= last_row) & (grid_col >= 0) & (grid_col <= last_col) & (row < XROWS)
    own = (row >= DEEP) & (row < DEEP + ELX) & (col >= DEEP) & (col < DEEP + ELY)
    meets = (col == DEEP) | (col == DEEP + ELY), (col == DEEP - 1) | (col == DEEP + ELY - 1)
    mine_ref[...] = jnp.where(own, 1.0, 0.0).astype(F32)
    corner = lax.broadcasted_iota(jnp.int32, (8, XL), 0) == 0
    low_row, high_row, low_col, high_col = grid_row == 0, grid_row == last_row, grid_col == 0, grid_col == last_col
    for tile, (edge, other) in enumerate(((low_col, low_row), (high_row, low_col), (high_col, high_row), (low_row, high_col))):
        keep = jnp.where(inside & ~(edge | (corner & other)), 1.0, 0.0).astype(F32)
        keep_ref[8 * tile : 8 * tile + 8] = keep
        weight_ref[8 * tile : 8 * tile + 8] = jnp.where(own, keep * jnp.where(corner, 0.25, 0.5), 0.0).astype(F32)
    scale = jnp.where(inside[0:1], block[MODES, 0:1] + spread[MODES * NB : MODES * NB + 1], 0.0)

    def assemble(values):
        return keep_ref[...] * jnp.concatenate(add_columns(add_rows(tiles(values), PITCH, None, None), None, None), 0)

    eye = lax.broadcasted_iota(jnp.int32, (NB, NB), 0) == lax.broadcasted_iota(jnp.int32, (NB, NB), 1)
    def gather_mode(m):
        values = block[m] + spread[pl.ds(pl.multiple_of(m * NB, NB), NB), :]
        state[0, m] = keep_ref[...] * jnp.concatenate(add_columns(tiles(values), *meets), 0)

    def extend_mode(i):
        def run(m):
            trace = jnp.sum(jnp.sum(jnp.where(eye, schur[m], 0.0), axis=0, keepdims=True), axis=1, keepdims=True)
            images = scale * dot(schur[m], state[i, m])
            applied[i, m] = images
            state[i + 1, m] = assemble(images) * ((0.5 * NB) / trace) - state[i, m]

        return run

    def sum_mode(m):
        v = [state[i, m] for i in range(3)]
        w = [applied[0, m], applied[1, m], scale * dot(schur[m], v[2])]
        weight, mine = weight_ref[...], mine_ref[0:1]
        weighted = v[1] * weight
        own = [value * mine for value in v]
        k = 0
        for first, second in (
            (v[0], v[0] * weight), (v[0], weighted), (v[1], weighted),
            (own[0], w[0]), (own[1], w[0]), (own[1], w[1]), (own[2], w[1]), (own[2], w[2]),
        ):
            whole = jnp.sum(first * second, axis=0, keepdims=True)
            parts[pl.ds(MODES * k + m, 1), :] = whole[:, 0:EL] + whole[:, EL:XL]
            k += 1
        for i in range(3):
            basis[i, m] = v[i]

    def every(body):
        def step(m, _):
            body(m)
            return 0

        lax.fori_loop(0, MODES, step, 0, unroll=UNROLL)

    every(gather_mode)
    for i in range(2):
        every(extend_mode(i))
    every(sum_mode)
    ones = jnp.ones((8, EL), F32)
    total = lax.dot_general(ones, parts[...], (((1,), (1,)), ((), ())), precision=HIGHEST, preferred_element_type=F32)
    for at in range(0, sums.shape[0], 8):
        sums[at : at + 8] = total


def finish_kernel(gathered, basis, base, couple, cell, out, coefs, mixed, blocks):
    total = jnp.broadcast_to(jnp.sum(gathered[...].reshape(-1, EL), axis=0, keepdims=True), (8, EL))
    b0, b1, b2, h0, h1, h2, h3, h4 = [
        total if k == 0 else pltpu.roll(total, EL - MODES * k, 1) for k in range(8)
    ]
    tiny = 2e-7
    l1, l2 = h1 / h0, h2 / h0
    d1 = h2 - l1 * h1
    ok1 = d1 > tiny * h2
    d1 = jnp.where(ok1, d1, 1.0)
    l12 = jnp.where(ok1, (h3 - l1 * h2) / d1, 0.0)
    d2 = h4 - l2 * h2 - l12 * l12 * d1
    ok2 = d2 > tiny * h4
    y1 = b1 - l1 * b0
    y2 = b2 - l2 * b0 - l12 * y1
    c2 = jnp.where(ok2, y2 / jnp.where(ok2, d2, 1.0), 0.0)
    c1 = jnp.where(ok1, y1 / d1, 0.0) - l12 * c2
    c0 = b0 / h0 - l1 * c1 - l2 * c2
    for i, c in enumerate((c0, c1, c2)):
        coefs[i] = jnp.transpose(jnp.broadcast_to(c[0:1], (EL, EL)))[0:MODES]
    place = (cell[0:1] // ELY + DEEP) * PITCH + cell[0:1] % ELY + DEEP

    def combine(m, _):
        c = [jnp.concatenate([coefs[i, pl.ds(m, 1), :]] * 2, 1) for i in range(3)]
        x = c[0] * basis[0, m] + c[1] * basis[1, m] + c[2] * basis[2, m]
        mixed[pl.ds(pl.multiple_of(m * NB, NB), NB), :] = both_ascending(x)
        return 0

    lax.fori_loop(0, MODES, combine, 0, unroll=UNROLL)
    solved = take(mixed[...], selection(place, XL))
    blocks[...] = jnp.zeros_like(blocks)
    for m in range(MODES):
        x = solved[m * NB : m * NB + NB]
        q, r = m // QUAD, m % QUAD
        blocks[q, NB * r : NB * r + NB, EL * r : EL * r + EL] = x
        for tile in range(4):
            out[pl.ds(8 * tile * MODES + m, 8, stride=MODES), :] = x[8 * tile : 8 * tile + 8]
    for q in range(MODES // QUAD):
        lifted = dot_of_parts(split(couple[q]), split(blocks[q]))
        for r in range(QUAD):
            m = QUAD * q + r
            within = base[m, 0:NI] - lifted[0:NI, EL * r : EL * r + EL]
            within = jnp.concatenate([within, jnp.zeros((PADDED - NODES, EL), F32)], 0)
            out[pl.ds(NB * MODES + m, PADDED - NB, stride=MODES), :] = within


def call(kernel, shapes=(), scratch=(), far=0, far_out=None):
    def run(*operands):
        many = isinstance(shapes, list)
        outs = [s if isinstance(s, pl.MemoryRef) else pltpu.VMEM(s, F32) for s in (shapes if many else [shapes])]
        whole, away = pl.BlockSpec(memory_space=pltpu.VMEM), pl.BlockSpec(memory_space=pl.ANY)
        near = tuple(pltpu.with_memory_space_constraint(o, pltpu.VMEM) for o in operands[far:])
        if far_out:
            outs = [jax.ShapeDtypeStruct(far_out, F32)]
        specs = [away if far_out else whole] * len(outs)
        return pl.pallas_call(
            kernel,
            out_shape=outs if many else outs[0],
            in_specs=[away] * far + [whole] * len(near),
            out_specs=specs if many else specs[0],
            scratch_shapes=list(scratch),
            compiler_params=pltpu.CompilerParams(vmem_limit_bytes=16 << 20),
            name=kernel.__name__,
        )(*(pltpu.with_memory_space_constraint(o, pltpu.HBM) for o in operands[:far]), *near)

    return run


def swap(array):
    return lax.all_to_all(array, "fourier", split_axis=0, concat_axis=0, tiled=True)


def ring(axis, step):
    count = lax.axis_size(axis)
    return [(i, (i + step) % count) for i in range(count)]


def neighbours(to_low, to_high, axis):
    return lax.ppermute(to_high, axis, ring(axis, 1)), lax.ppermute(to_low, axis, ring(axis, -1))


def on_device(forcing, element_coef, schur, couple, inner_inv, element_cell):
    parts = lax.axis_size("fourier")
    devices = lax.axis_size("ex") * lax.axis_size("ey")
    group = PADDED // parts
    table = jnp.asarray(real_transform())
    exchanged = (parts, group, MODES, EL)
    lanes = (8, EL)
    ints = pltpu.VMEM(lanes, jnp.int32)

    planes, order, index, scale, stored = call(
        enter_kernel, [(PADDED, MODES, EL), ints, ints, lanes, lanes],
        [
            pltpu.SemaphoreType.DMA((CHUNKS,)),
            pltpu.SemaphoreType.DMA((2,)),
            pltpu.VMEM((1, EL), F32),
            pltpu.VMEM((1, EL), jnp.int32),
        ],
        far=3,
    )(jnp.transpose(forcing, (1, 0, 2)), element_coef.reshape(1, EL), element_cell.reshape(1, EL))
    planes = swap(planes).reshape(exchanged)
    spectral = swap(call(transform_kernel, exchanged)(table, planes).reshape(PADDED, MODES, EL))
    spectral = spectral.reshape(PADDED * MODES, EL)

    message, extended = (MODES + 1, 8, EL), (MODES + 1, NB, XL)
    table_of_lanes = jnp.asarray(lane_tables())
    condensed, down, up = call(condense_kernel, [(MODES, NB, EL), message, message])(spectral, order, scale, couple)
    low, high = neighbours(down, up, "ex")
    base, turned = call(
        interior_kernel, [(MODES, 56, EL), (MODES // QUAD, 56, QUAD * NB)], [pltpu.VMEM((QUAD * NB, EL), F32)]
    )(spectral, stored, jnp.transpose(inner_inv, (1, 0, 2)).reshape(NI * MODES, NI), couple)
    low, high, base, turned = lax.optimization_barrier((low, high, base, turned))
    rows = (MODES + 1) * NB
    left, right, middle = call(columns_kernel, [message, message, extended], [pltpu.VMEM((rows, EL), F32)])(
        condensed, scale, low, high, table_of_lanes
    )
    left, right = neighbours(left, right, "ey")
    block, matrix = call(middle_kernel, [extended, (MODES, NB, NB)])(middle, schur, table_of_lanes)
    basis, sums = call(
        krylov_kernel,
        [(3, MODES, NB, XL), (devices, EL)],
        [
            pltpu.VMEM((NB, XL), F32),
            pltpu.VMEM((NB, XL), F32),
            pltpu.VMEM((8, XL), F32),
            pltpu.VMEM((EL, EL), F32),
            pltpu.VMEM((3, MODES, NB, XL), F32),
            pltpu.VMEM((2, MODES, NB, XL), F32),
            pltpu.VMEM((rows, EL), F32),
            pltpu.VMEM((rows, XL), F32),
        ],
    )(block, left, right, matrix, table_of_lanes)
    gathered = lax.all_to_all(sums.reshape(devices, 1, EL), ("ex", "ey"), split_axis=0, concat_axis=0, tiled=True)
    modal = call(finish_kernel, (PADDED * MODES, EL), [pltpu.VMEM((3, MODES, EL), F32), pltpu.VMEM((MODES * NB, XL), F32), pltpu.VMEM((MODES // QUAD, QUAD * NB, QUAD * EL), F32)])(
        gathered, basis, base, turned, index
    )
    modal = swap(modal.reshape(PADDED, MODES, EL)).reshape(exchanged)
    velocity = swap(call(transform_kernel, exchanged)(table.T, modal).reshape(PADDED, MODES, EL))
    velocity = call(leave_kernel, far_out=(NODES, MODES, EL), scratch=[pltpu.SemaphoreType.DMA((CHUNKS,))])(velocity)
    return jnp.transpose(velocity, (1, 0, 2))


def solution(mesh):
    placed = (
        P("fourier", None, ("ex", "ey")),
        P(("ex", "ey")),
        P("fourier", None, None),
        P("fourier", None, None),
        P("fourier", None, None),
        P(("ex", "ey")),
    )
    return jax.shard_map(
        on_device,
        mesh=mesh,
        in_specs=placed,
        out_specs=P("fourier", None, ("ex", "ey")),
        check_vma=False,
    )
```

```python
import math

import jax
import jax.numpy as jnp
import numpy as np
from jax import lax
from jax.experimental import pallas as pl
from jax.experimental.pallas import tpu as pltpu
from jax.sharding import PartitionSpec as P

P_SIZE = 8
NZ = 128
ELX = 8
ELY = 16
NODES = 81
NB = 32
NI = 49
EL = ELX * ELY
PADDED = 88
MODES = 16
DEEP = 2
XROWS = ELX + 2 * DEEP
XCOLS = ELY + 2 * DEEP
PITCH = XCOLS
XL = 256
SLOT = DEEP * ELY
UNROLL = 8
TERMS = ((0, 0), (0, 1), (1, 0), (1, 1), (0, 2), (2, 0))
QUAD = 4
CHUNKS = 3
HIGHEST = lax.Precision.HIGHEST
F32 = jnp.float32


def real_transform():
    k = np.arange(NZ)[:, None]
    z = np.arange(NZ)[None, :]
    angle = 2.0 * math.pi * (((k + 1) // 2 * z) % NZ) / NZ
    w = np.where(k % 2 == 1, np.cos(angle), np.sin(angle)) * math.sqrt(2.0 / NZ)
    w[0] = 1.0 / math.sqrt(NZ)
    w[NZ - 1] = np.cos(math.pi * np.arange(NZ)) / math.sqrt(NZ)
    return w.astype(np.float32)


def lane_tables():
    lane = np.arange(XL)
    row, col = lane // PITCH, lane % PITCH
    valid = row < XROWS
    middle = valid & (col >= DEEP) & (col < DEEP + ELY)
    spread = np.where(middle, row * ELY + col - DEEP, -1)
    turn = row * DEEP + np.where(col < DEEP, col, EL + col - DEEP - ELY)
    turn = np.where(valid & ~middle, turn, -1)
    at = lane % SLOT
    send = at // DEEP * ELY + at % DEEP + np.where(lane >= EL, ELY - DEEP, 0)
    send = np.where(at < DEEP * XROWS, send, -1)
    return np.stack([spread, turn, send, row, col, lane % EL // SLOT, row, row]).astype(np.int32)


def pick(values, index):
    return jnp.take_along_axis(values, jnp.broadcast_to(index, values.shape), axis=1, mode="promise_in_bounds")


def dot(a, b):
    return lax.dot_general(a, b, (((1,), (0,)), ((), ())), precision=HIGHEST, preferred_element_type=F32)


def selection(index, size):
    return jnp.where(lax.broadcasted_iota(jnp.int32, (size, index.shape[1]), 0) == index, 1.0, 0.0).astype(F32)


def three_parts(values):
    high = values.astype(jnp.bfloat16)
    rest = values - high.astype(F32)
    middle = rest.astype(jnp.bfloat16)
    return high, middle, (rest - middle.astype(F32)).astype(jnp.bfloat16)


def take(values, chosen):
    high, middle, low = three_parts(values)
    chosen = chosen.astype(jnp.bfloat16)

    def product(part):
        return lax.dot_general(part, chosen, (((1,), (0,)), ((), ())), preferred_element_type=F32)

    return (product(high) + product(middle)) + product(low)


def add_rows(t, step, before, behind):
    width = t[0].shape[1]
    zero = lax.broadcasted_iota(jnp.int32, t[0].shape, 0) == 0
    back = width - step

    def masked(mask, values):
        return values if mask is None else jnp.where(mask, values, 0.0)

    from0 = masked(before, pltpu.roll(jnp.where(zero, t[1], 0.0), step, 1))
    from3 = masked(before, pltpu.roll(jnp.where(zero, t[2], t[1]), step, 1))
    from1 = masked(behind, pltpu.roll(jnp.where(zero, t[0], t[3]), back, 1))
    from2 = masked(behind, pltpu.roll(jnp.where(zero, t[3], 0.0), back, 1))
    return [t[0] + from0, t[1] + from1, t[2] + from2, t[3] + from3]


def add_columns(t, before, behind):
    turned = add_rows([t[1], t[2], t[3], t[0]], 1, before, behind)
    return [turned[3], turned[0], turned[1], turned[2]]


def tiles(values):
    return [values[8 * i : 8 * i + 8] for i in range(4)]


def split(values):
    high = values.astype(jnp.bfloat16)
    return high, (values - high.astype(F32)).astype(jnp.bfloat16)


def dot_of_parts(a, b):
    (a_high, a_low), (b_high, b_low) = a, b

    def product(first, second):
        return lax.dot_general(first, second, (((1,), (0,)), ((), ())), preferred_element_type=F32)

    return product(a_high, b_low) + product(a_low, b_high) + product(a_high, b_high)


def transform_kernel(table, planes, out):
    groups, nodes = planes.shape[0], planes.shape[1]
    held = split(table[...])
    for n in range(nodes):
        block = planes[:, n].reshape(NZ, EL)
        out[:, n] = dot_of_parts(held, split(block)).reshape(groups, NZ // groups, EL)


def copies(source, target, nodes, done):
    step = -(-nodes // CHUNKS)
    cuts = [(at, min(step, nodes - at)) for at in range(0, nodes, step)]
    return [
        pltpu.make_async_copy(source.at[pl.ds(at, size)], target.at[pl.ds(at, size)], done.at[i])
        for i, (at, size) in enumerate(cuts)
    ]


def enter_kernel(forcing, coef_far, cell_far, planes, order, index, scale, stored, done, small, coef, cell):
    nodes = forcing.shape[0]
    fetched = [pltpu.make_async_copy(coef_far, coef, small.at[0]), pltpu.make_async_copy(cell_far, cell, small.at[1])]
    moved = copies(forcing, planes, nodes, done)
    for copy in fetched + moved:
        copy.start()
    planes[nodes:PADDED] = jnp.zeros((PADDED - nodes, planes.shape[1], EL), F32)
    for copy in fetched:
        copy.wait()
    lane = lax.broadcasted_iota(jnp.int32, (EL, EL), 1)
    elem = lax.broadcasted_iota(jnp.int32, (EL, EL), 0)
    cells = jnp.transpose(jnp.broadcast_to(cell[...], (EL, EL)))
    found = jnp.sum(jnp.where(cells == lane, elem, 0), axis=0, keepdims=True)
    order[...] = jnp.broadcast_to(found, (8, EL))
    index[...] = jnp.broadcast_to(cell[...], (8, EL))
    stored[...] = jnp.broadcast_to(coef[...], (8, EL))
    scale[...] = pick(jnp.broadcast_to(coef[...], (8, EL)), found)
    for copy in moved:
        copy.wait()


def leave_kernel(planes, velocity, done):
    moved = copies(planes, velocity, velocity.shape[0], done)
    for copy in moved:
        copy.start()
    for copy in moved:
        copy.wait()


def flipped(tile):
    back = (8 - lax.broadcasted_iota(jnp.int32, tile.shape, 0)) % 8
    return jnp.take_along_axis(tile, back, axis=0, mode="promise_in_bounds")


def both_ascending(values):
    return jnp.concatenate([values[0:16], flipped(values[16:24]), flipped(values[24:32])], 0)


def condense_kernel(spectral, order, scale, couple, condensed, down, up):
    lane = lax.broadcasted_iota(jnp.int32, (8, EL), 1)
    row, col, slot = lane // ELY, lane % ELY, lane // SLOT
    inner_row, inner_col = (row > 0, row < ELX - 1), (col > 0, col < ELY - 1)

    def messages(t):
        low, high = t[0], t[3]
        for i in (1, 2, 3):
            low = jnp.where(slot == i, pltpu.roll(t[i], SLOT * i, 1), low)
            high = jnp.where(slot == i - 1, pltpu.roll(t[i - 1], SLOT * i, 1), high)
        return low, high

    down[MODES], up[MODES] = messages([scale[...]] * 4)

    def mode(m, _):
        fields = spectral[pl.ds(m, PADDED, stride=MODES), :]
        value = fields[0:NB] - dot_of_parts(split(couple[m]), split(fields[NB:NODES]))
        t = tiles(both_ascending(pick(value, order[0:1])))
        t = add_columns(add_rows(t, ELY, *inner_row), *inner_col)
        condensed[m] = jnp.concatenate(t, 0)
        down[m], up[m] = messages(t)
        return 0

    lax.fori_loop(0, MODES, mode, 0, unroll=UNROLL)


def interior_kernel(spectral, stored, inner, couple, base, turned, wide):
    inverse = 1.0 / stored[0:1]

    def mode(m, _):
        within = spectral[pl.ds(NB * MODES + m, PADDED - NB, stride=MODES), :][0:NI]
        base[m, 0:NI] = dot(inner[pl.ds(m, NI, stride=MODES), :], within) * inverse
        return 0

    lax.fori_loop(0, MODES, mode, 0, unroll=UNROLL)
    wide[...] = jnp.zeros_like(wide)
    for q in range(MODES // QUAD):
        wide[:, 0:NI] = couple[QUAD * q : QUAD * q + QUAD].reshape(QUAD * NB, NI)
        turned[q] = jnp.transpose(wide[...])[0 : turned.shape[1]]


def columns_kernel(condensed, scale, low, high, table, left, right, middle):
    lane = lax.broadcasted_iota(jnp.int32, (8, EL), 1)
    slot = lane // SLOT
    inner, outer = slot == 0, slot == 1
    meets = (lane >= SLOT) & (lane < SLOT + ELY), (lane >= SLOT - ELY) & (lane < SLOT)

    def stack(own, lo, hi):
        first, second = [], []
        for i in range(4):
            moved = pltpu.roll(own[i], SLOT, 1)
            below = lo if i == 0 else pltpu.roll(lo, EL - SLOT * i, 1)
            above = hi if i == 1 else pltpu.roll(hi, (EL + SLOT - SLOT * i) % EL, 1)
            first.append(jnp.where(inner, below, moved))
            second.append(jnp.where(inner, moved, jnp.where(outer, above, 0.0)))
        return first, second

    def put(m, parts):
        for j, part in enumerate(parts):
            middle[m, :, EL * j : EL * j + EL] = jnp.concatenate(part, 0)

    put(MODES, stack([scale[...]] * 4, low[MODES], high[MODES]))

    def mode(m, _):
        parts = stack(tiles(condensed[m]), low[m], high[m])
        put(m, [add_rows(part, ELY, *meets) for part in parts])
        return 0

    lax.fori_loop(0, MODES, mode, 0, unroll=UNROLL)
    total = 0.0
    for i in range(4):
        send = selection(jnp.where(table[5:6] == i, table[2:3], -1), XL)
        total = total + take(middle[:, 8 * i : 8 * i + 8, :].reshape((MODES + 1) * 8, XL), send)
    left[...] = total[:, 0:EL].reshape(MODES + 1, 8, EL)
    right[...] = total[:, EL:XL].reshape(MODES + 1, 8, EL)


def middle_kernel(middle, table, block):
    spread = take(middle[...].reshape((MODES + 1) * NB, XL), selection(table[0:1], XL))
    block[...] = spread.reshape(MODES + 1, NB, XL)


def matrices_kernel(schur, matrix, shift):
    lane = lax.broadcasted_iota(jnp.int32, (NB, NB), 1)
    eye = lax.broadcasted_iota(jnp.int32, (NB, NB), 0) == lane
    across = jnp.where((lane >= 16) & (lane % 8 > 0), lane // 8 * 8 + 8 - lane % 8, lane)

    def mode(m, _):
        trace = jnp.sum(jnp.sum(jnp.where(eye, schur[m], 0.0), axis=0, keepdims=True), axis=1, keepdims=True)
        shift[m] = jnp.broadcast_to((0.5 * NB) / trace, (8, XL))
        rows = both_ascending(schur[m])
        parts = three_parts(jnp.take_along_axis(rows, across, axis=1, mode="promise_in_bounds"))
        for k, (part, _) in enumerate(TERMS):
            matrix[m, :, NB * k : NB * k + NB] = parts[part]
        return 0

    lax.fori_loop(0, MODES, mode, 0, unroll=UNROLL)


def krylov_kernel(
    block, left, right, schur, shift, table, basis, sums, keep_ref, weight_ref, mine_ref, parts, state, applied, spread
):
    sides = jnp.concatenate([left[...].reshape((MODES + 1) * 8, EL), right[...].reshape((MODES + 1) * 8, EL)], 1)
    for i in range(4):
        turn = selection(jnp.where(table[1:2] < 0, -1, table[1:2] + SLOT * i), XL)
        spread[:, 8 * i : 8 * i + 8, :] = take(sides, turn).reshape(MODES + 1, 8, XL)

    row, col = jnp.broadcast_to(table[3:4], (8, XL)), jnp.broadcast_to(table[4:5], (8, XL))
    grid_row = row - DEEP + lax.axis_index("ex") * ELX
    grid_col = col - DEEP + lax.axis_index("ey") * ELY
    last_row, last_col = lax.axis_size("ex") * ELX - 1, lax.axis_size("ey") * ELY - 1
    inside = (grid_row >= 0) & (grid_row <= last_row) & (grid_col >= 0) & (grid_col <= last_col) & (row < XROWS)
    own = (row >= DEEP) & (row < DEEP + ELX) & (col >= DEEP) & (col < DEEP + ELY)
    meets = (col == DEEP) | (col == DEEP + ELY), (col == DEEP - 1) | (col == DEEP + ELY - 1)
    mine_ref[...] = jnp.where(own, 1.0, 0.0).astype(F32)
    corner = lax.broadcasted_iota(jnp.int32, (8, XL), 0) == 0
    low_row, high_row, low_col, high_col = grid_row == 0, grid_row == last_row, grid_col == 0, grid_col == last_col
    for tile, (edge, other) in enumerate(((low_col, low_row), (high_row, low_col), (high_col, high_row), (low_row, high_col))):
        keep = jnp.where(inside & ~(edge | (corner & other)), 1.0, 0.0).astype(F32)
        keep_ref[8 * tile : 8 * tile + 8] = keep
        weight_ref[8 * tile : 8 * tile + 8] = jnp.where(own, keep * jnp.where(corner, 0.25, 0.5), 0.0).astype(F32)
    scale = jnp.where(inside[0:1], block[MODES, 0:1] + spread[MODES, 0:1], 0.0)

    def assemble(values):
        return keep_ref[...] * jnp.concatenate(add_columns(add_rows(tiles(values), PITCH, None, None), None, None), 0)

    def image(m, values):
        parts_of = three_parts(values)
        stacked = jnp.concatenate([parts_of[part] for _, part in TERMS], 0)
        return scale * lax.dot_general(schur[m], stacked, (((1,), (0,)), ((), ())), preferred_element_type=F32)

    def gather_mode(m):
        values = block[m] + spread[m]
        state[0, m] = keep_ref[...] * jnp.concatenate(add_columns(tiles(values), *meets), 0)

    def extend_mode(i):
        def run(m):
            images = image(m, state[i, m])
            applied[i, m] = images
            state[i + 1, m] = assemble(images) * shift[m, 0:1] - state[i, m]

        return run

    def sum_mode(m):
        v = [state[i, m] for i in range(3)]
        w = [applied[0, m], applied[1, m], image(m, v[2])]
        weight, mine = weight_ref[...], mine_ref[0:1]
        weighted = v[1] * weight
        own = [value * mine for value in v]
        k = 0
        for first, second in (
            (v[0], v[0] * weight), (v[0], weighted), (v[1], weighted),
            (own[0], w[0]), (own[1], w[0]), (own[1], w[1]), (own[2], w[1]), (own[2], w[2]),
        ):
            whole = jnp.sum(first * second, axis=0, keepdims=True)
            parts[pl.ds(MODES * k + m, 1), :] = whole[:, 0:EL] + whole[:, EL:XL]
            k += 1
        for i in range(3):
            basis[i, m] = v[i]

    def every(body):
        def step(m, _):
            body(m)
            return 0

        lax.fori_loop(0, MODES, step, 0, unroll=UNROLL)

    every(gather_mode)
    for i in range(2):
        every(extend_mode(i))
    every(sum_mode)
    ones = jnp.ones((8, EL), F32)
    total = lax.dot_general(ones, parts[...], (((1,), (1,)), ((), ())), precision=HIGHEST, preferred_element_type=F32)
    for at in range(0, sums.shape[0], 8):
        sums[at : at + 8] = total


def finish_kernel(gathered, basis, base, couple, cell, out, coefs, mixed, blocks):
    total = jnp.broadcast_to(jnp.sum(gathered[...].reshape(-1, EL), axis=0, keepdims=True), (8, EL))
    b0, b1, b2, h0, h1, h2, h3, h4 = [
        total if k == 0 else pltpu.roll(total, EL - MODES * k, 1) for k in range(8)
    ]
    tiny = 2e-7
    l1, l2 = h1 / h0, h2 / h0
    d1 = h2 - l1 * h1
    ok1 = d1 > tiny * h2
    d1 = jnp.where(ok1, d1, 1.0)
    l12 = jnp.where(ok1, (h3 - l1 * h2) / d1, 0.0)
    d2 = h4 - l2 * h2 - l12 * l12 * d1
    ok2 = d2 > tiny * h4
    y1 = b1 - l1 * b0
    y2 = b2 - l2 * b0 - l12 * y1
    c2 = jnp.where(ok2, y2 / jnp.where(ok2, d2, 1.0), 0.0)
    c1 = jnp.where(ok1, y1 / d1, 0.0) - l12 * c2
    c0 = b0 / h0 - l1 * c1 - l2 * c2
    for i, c in enumerate((c0, c1, c2)):
        coefs[i] = jnp.transpose(jnp.broadcast_to(c[0:1], (EL, EL)))[0:MODES]
    place = (cell[0:1] // ELY + DEEP) * PITCH + cell[0:1] % ELY + DEEP

    def combine(m, _):
        c = [jnp.concatenate([coefs[i, pl.ds(m, 1), :]] * 2, 1) for i in range(3)]
        x = c[0] * basis[0, m] + c[1] * basis[1, m] + c[2] * basis[2, m]
        mixed[pl.ds(pl.multiple_of(m * NB, NB), NB), :] = both_ascending(x)
        return 0

    lax.fori_loop(0, MODES, combine, 0, unroll=UNROLL)
    solved = take(mixed[...], selection(place, XL))
    blocks[...] = jnp.zeros_like(blocks)
    for m in range(MODES):
        x = solved[m * NB : m * NB + NB]
        q, r = m // QUAD, m % QUAD
        blocks[q, NB * r : NB * r + NB, EL * r : EL * r + EL] = x
        for tile in range(4):
            out[pl.ds(8 * tile * MODES + m, 8, stride=MODES), :] = x[8 * tile : 8 * tile + 8]
    for q in range(MODES // QUAD):
        lifted = dot_of_parts(split(couple[q]), split(blocks[q]))
        for r in range(QUAD):
            m = QUAD * q + r
            within = base[m, 0:NI] - lifted[0:NI, EL * r : EL * r + EL]
            within = jnp.concatenate([within, jnp.zeros((PADDED - NODES, EL), F32)], 0)
            out[pl.ds(NB * MODES + m, PADDED - NB, stride=MODES), :] = within


def call(kernel, shapes=(), scratch=(), far=0, far_out=None):
    def run(*operands):
        many = isinstance(shapes, list)
        outs = [s if isinstance(s, pl.MemoryRef) else pltpu.VMEM(s, F32) for s in (shapes if many else [shapes])]
        whole, away = pl.BlockSpec(memory_space=pltpu.VMEM), pl.BlockSpec(memory_space=pl.ANY)
        near = tuple(pltpu.with_memory_space_constraint(o, pltpu.VMEM) for o in operands[far:])
        if far_out:
            outs = [jax.ShapeDtypeStruct(far_out, F32)]
        specs = [away if far_out else whole] * len(outs)
        return pl.pallas_call(
            kernel,
            out_shape=outs if many else outs[0],
            in_specs=[away] * far + [whole] * len(near),
            out_specs=specs if many else specs[0],
            scratch_shapes=list(scratch),
            compiler_params=pltpu.CompilerParams(vmem_limit_bytes=16 << 20),
            name=kernel.__name__,
        )(*(pltpu.with_memory_space_constraint(o, pltpu.HBM) for o in operands[:far]), *near)

    return run


def swap(array):
    return lax.all_to_all(array, "fourier", split_axis=0, concat_axis=0, tiled=True)


def ring(axis, step):
    count = lax.axis_size(axis)
    return [(i, (i + step) % count) for i in range(count)]


def neighbours(to_low, to_high, axis):
    return lax.ppermute(to_high, axis, ring(axis, 1)), lax.ppermute(to_low, axis, ring(axis, -1))


def on_device(forcing, element_coef, schur, couple, inner_inv, element_cell):
    parts = lax.axis_size("fourier")
    devices = lax.axis_size("ex") * lax.axis_size("ey")
    group = PADDED // parts
    table = jnp.asarray(real_transform())
    exchanged = (parts, group, MODES, EL)
    lanes = (8, EL)
    ints = pltpu.VMEM(lanes, jnp.int32)

    planes, order, index, scale, stored = call(
        enter_kernel, [(PADDED, MODES, EL), ints, ints, lanes, lanes],
        [
            pltpu.SemaphoreType.DMA((CHUNKS,)),
            pltpu.SemaphoreType.DMA((2,)),
            pltpu.VMEM((1, EL), F32),
            pltpu.VMEM((1, EL), jnp.int32),
        ],
        far=3,
    )(jnp.transpose(forcing, (1, 0, 2)), element_coef.reshape(1, EL), element_cell.reshape(1, EL))
    planes = swap(planes).reshape(exchanged)
    spectral = swap(call(transform_kernel, exchanged)(table, planes).reshape(PADDED, MODES, EL))
    spectral = spectral.reshape(PADDED * MODES, EL)

    message, extended = (MODES + 1, 8, EL), (MODES + 1, NB, XL)
    table_of_lanes = jnp.asarray(lane_tables())
    condensed, down, up = call(condense_kernel, [(MODES, NB, EL), message, message])(spectral, order, scale, couple)
    low, high = neighbours(down, up, "ex")
    base, turned = call(
        interior_kernel, [(MODES, 56, EL), (MODES // QUAD, 56, QUAD * NB)], [pltpu.VMEM((QUAD * NB, EL), F32)]
    )(spectral, stored, jnp.transpose(inner_inv, (1, 0, 2)).reshape(NI * MODES, NI), couple)
    low, high, base, turned, schur = lax.optimization_barrier((low, high, base, turned, schur))
    left, right, middle = call(columns_kernel, [message, message, extended])(
        condensed, scale, low, high, table_of_lanes
    )
    left, right = neighbours(left, right, "ey")
    matrix, shift = call(
        matrices_kernel, [pltpu.VMEM((MODES, NB, len(TERMS) * NB), jnp.bfloat16), (MODES, 8, XL)]
    )(schur)
    block = call(middle_kernel, extended)(middle, table_of_lanes)
    basis, sums = call(
        krylov_kernel,
        [(3, MODES, NB, XL), (devices, EL)],
        [
            pltpu.VMEM((NB, XL), F32),
            pltpu.VMEM((NB, XL), F32),
            pltpu.VMEM((8, XL), F32),
            pltpu.VMEM((EL, EL), F32),
            pltpu.VMEM((3, MODES, NB, XL), F32),
            pltpu.VMEM((2, MODES, NB, XL), F32),
            pltpu.VMEM(extended, F32),
        ],
    )(block, left, right, matrix, shift, table_of_lanes)
    gathered = lax.all_to_all(sums.reshape(devices, 1, EL), ("ex", "ey"), split_axis=0, concat_axis=0, tiled=True)
    modal = call(finish_kernel, (PADDED * MODES, EL), [pltpu.VMEM((3, MODES, EL), F32), pltpu.VMEM((MODES * NB, XL), F32), pltpu.VMEM((MODES // QUAD, QUAD * NB, QUAD * EL), F32)])(
        gathered, basis, base, turned, index
    )
    modal = swap(modal.reshape(PADDED, MODES, EL)).reshape(exchanged)
    velocity = swap(call(transform_kernel, exchanged)(table.T, modal).reshape(PADDED, MODES, EL))
    velocity = call(leave_kernel, far_out=(NODES, MODES, EL), scratch=[pltpu.SemaphoreType.DMA((CHUNKS,))])(velocity)
    return jnp.transpose(velocity, (1, 0, 2))


def solution(mesh):
    placed = (
        P("fourier", None, ("ex", "ey")),
        P(("ex", "ey")),
        P("fourier", None, None),
        P("fourier", None, None),
        P("fourier", None, None),
        P(("ex", "ey")),
    )
    return jax.shard_map(
        on_device,
        mesh=mesh,
        in_specs=placed,
        out_specs=P("fourier", None, ("ex", "ey")),
        check_vma=False,
    )
```

```python
import math

import jax
import jax.numpy as jnp
import numpy as np
from jax import lax
from jax.experimental import pallas as pl
from jax.experimental.pallas import tpu as pltpu
from jax.sharding import PartitionSpec as P

P_SIZE = 8
NZ = 128
ELX = 8
ELY = 16
NODES = 81
NB = 32
NI = 49
EL = ELX * ELY
PADDED = 88
MODES = 16
DEEP = 2
XROWS = ELX + 2 * DEEP
XCOLS = ELY + 2 * DEEP
PITCH = XCOLS
XL = 256
SLOT = DEEP * ELY
UNROLL = 16
TERMS = ((0, 0), (0, 1), (1, 0), (1, 1), (0, 2), (2, 0))
QUAD = 4
CHUNKS = 3
HIGHEST = lax.Precision.HIGHEST
F32 = jnp.float32


def real_transform():
    k = np.arange(NZ)[:, None]
    z = np.arange(NZ)[None, :]
    angle = 2.0 * math.pi * (((k + 1) // 2 * z) % NZ) / NZ
    w = np.where(k % 2 == 1, np.cos(angle), np.sin(angle)) * math.sqrt(2.0 / NZ)
    w[0] = 1.0 / math.sqrt(NZ)
    w[NZ - 1] = np.cos(math.pi * np.arange(NZ)) / math.sqrt(NZ)
    return w.astype(np.float32)


def lane_tables():
    lane = np.arange(XL)
    row, col = lane // PITCH, lane % PITCH
    valid = row < XROWS
    middle = valid & (col >= DEEP) & (col < DEEP + ELY)
    spread = np.where(middle, row * ELY + col - DEEP, -1)
    turn = row * DEEP + np.where(col < DEEP, col, EL + col - DEEP - ELY)
    turn = np.where(valid & ~middle, turn, -1)
    at = lane % SLOT
    send = at // DEEP * ELY + at % DEEP + np.where(lane >= EL, ELY - DEEP, 0)
    send = np.where(at < DEEP * XROWS, send, -1)
    return np.stack([spread, turn, send, row, col, lane % EL // SLOT, row, row]).astype(np.int32)


def pick(values, index):
    return jnp.take_along_axis(values, jnp.broadcast_to(index, values.shape), axis=1, mode="promise_in_bounds")


def dot(a, b):
    return lax.dot_general(a, b, (((1,), (0,)), ((), ())), precision=HIGHEST, preferred_element_type=F32)


def selection(index, size):
    return jnp.where(lax.broadcasted_iota(jnp.int32, (size, index.shape[1]), 0) == index, 1.0, 0.0).astype(F32)


def three_parts(values):
    high = values.astype(jnp.bfloat16)
    rest = values - high.astype(F32)
    middle = rest.astype(jnp.bfloat16)
    return high, middle, (rest - middle.astype(F32)).astype(jnp.bfloat16)


def take(values, chosen):
    high, middle, low = three_parts(values)
    chosen = chosen.astype(jnp.bfloat16)

    def product(part):
        return lax.dot_general(part, chosen, (((1,), (0,)), ((), ())), preferred_element_type=F32)

    return (product(high) + product(middle)) + product(low)


def add_rows(t, step, before, behind):
    width = t[0].shape[1]
    zero = lax.broadcasted_iota(jnp.int32, t[0].shape, 0) == 0
    back = width - step

    def masked(mask, values):
        return values if mask is None else jnp.where(mask, values, 0.0)

    from0 = masked(before, pltpu.roll(jnp.where(zero, t[1], 0.0), step, 1))
    from3 = masked(before, pltpu.roll(jnp.where(zero, t[2], t[1]), step, 1))
    from1 = masked(behind, pltpu.roll(jnp.where(zero, t[0], t[3]), back, 1))
    from2 = masked(behind, pltpu.roll(jnp.where(zero, t[3], 0.0), back, 1))
    return [t[0] + from0, t[1] + from1, t[2] + from2, t[3] + from3]


def add_columns(t, before, behind):
    turned = add_rows([t[1], t[2], t[3], t[0]], 1, before, behind)
    return [turned[3], turned[0], turned[1], turned[2]]


def tiles(values):
    return [values[8 * i : 8 * i + 8] for i in range(4)]


def split(values):
    high = values.astype(jnp.bfloat16)
    return high, (values - high.astype(F32)).astype(jnp.bfloat16)


def dot_of_parts(a, b):
    (a_high, a_low), (b_high, b_low) = a, b

    def product(first, second):
        return lax.dot_general(first, second, (((1,), (0,)), ((), ())), preferred_element_type=F32)

    return product(a_high, b_low) + product(a_low, b_high) + product(a_high, b_high)


def transform_kernel(table, planes, out):
    groups, nodes = planes.shape[0], planes.shape[1]
    held = split(table[...])
    for n in range(nodes):
        block = planes[:, n].reshape(NZ, EL)
        out[:, n] = dot_of_parts(held, split(block)).reshape(groups, NZ // groups, EL)


def copies(source, target, nodes, done):
    step = -(-nodes // CHUNKS)
    cuts = [(at, min(step, nodes - at)) for at in range(0, nodes, step)]
    return [
        pltpu.make_async_copy(source.at[pl.ds(at, size)], target.at[pl.ds(at, size)], done.at[i])
        for i, (at, size) in enumerate(cuts)
    ]


def enter_kernel(forcing, coef_far, cell_far, planes, order, index, scale, stored, done, small, coef, cell):
    nodes = forcing.shape[0]
    fetched = [pltpu.make_async_copy(coef_far, coef, small.at[0]), pltpu.make_async_copy(cell_far, cell, small.at[1])]
    moved = copies(forcing, planes, nodes, done)
    for copy in fetched + moved:
        copy.start()
    planes[nodes:PADDED] = jnp.zeros((PADDED - nodes, planes.shape[1], EL), F32)
    for copy in fetched:
        copy.wait()
    lane = lax.broadcasted_iota(jnp.int32, (EL, EL), 1)
    elem = lax.broadcasted_iota(jnp.int32, (EL, EL), 0)
    cells = jnp.transpose(jnp.broadcast_to(cell[...], (EL, EL)))
    found = jnp.sum(jnp.where(cells == lane, elem, 0), axis=0, keepdims=True)
    order[...] = jnp.broadcast_to(found, (8, EL))
    index[...] = jnp.broadcast_to(cell[...], (8, EL))
    stored[...] = jnp.broadcast_to(coef[...], (8, EL))
    scale[...] = pick(jnp.broadcast_to(coef[...], (8, EL)), found)
    for copy in moved:
        copy.wait()


def leave_kernel(planes, velocity, done):
    moved = copies(planes, velocity, velocity.shape[0], done)
    for copy in moved:
        copy.start()
    for copy in moved:
        copy.wait()


def flipped(tile):
    back = (8 - lax.broadcasted_iota(jnp.int32, tile.shape, 0)) % 8
    return jnp.take_along_axis(tile, back, axis=0, mode="promise_in_bounds")


def both_ascending(values):
    return jnp.concatenate([values[0:16], flipped(values[16:24]), flipped(values[24:32])], 0)


def condense_kernel(spectral, order, scale, couple, condensed, down, up):
    lane = lax.broadcasted_iota(jnp.int32, (8, EL), 1)
    row, col, slot = lane // ELY, lane % ELY, lane // SLOT
    inner_row, inner_col = (row > 0, row < ELX - 1), (col > 0, col < ELY - 1)

    def messages(t):
        low, high = t[0], t[3]
        for i in (1, 2, 3):
            low = jnp.where(slot == i, pltpu.roll(t[i], SLOT * i, 1), low)
            high = jnp.where(slot == i - 1, pltpu.roll(t[i - 1], SLOT * i, 1), high)
        return low, high

    down[MODES], up[MODES] = messages([scale[...]] * 4)

    def mode(m, _):
        fields = spectral[pl.ds(m, PADDED, stride=MODES), :]
        value = fields[0:NB] - dot_of_parts(split(couple[m]), split(fields[NB:NODES]))
        t = tiles(both_ascending(pick(value, order[0:1])))
        t = add_columns(add_rows(t, ELY, *inner_row), *inner_col)
        condensed[m] = jnp.concatenate(t, 0)
        down[m], up[m] = messages(t)
        return 0

    lax.fori_loop(0, MODES, mode, 0, unroll=UNROLL)


def interior_kernel(spectral, stored, inner, couple, base, turned, wide):
    inverse = 1.0 / stored[0:1]

    def mode(m, _):
        within = spectral[pl.ds(NB * MODES + m, PADDED - NB, stride=MODES), :][0:NI]
        base[m, 0:NI] = dot(inner[pl.ds(m, NI, stride=MODES), :], within) * inverse
        return 0

    lax.fori_loop(0, MODES, mode, 0, unroll=UNROLL)
    wide[...] = jnp.zeros_like(wide)
    for q in range(MODES // QUAD):
        wide[:, 0:NI] = couple[QUAD * q : QUAD * q + QUAD].reshape(QUAD * NB, NI)
        turned[q] = jnp.transpose(wide[...])[0 : turned.shape[1]]


def columns_kernel(condensed, scale, low, high, table, left, right, middle):
    lane = lax.broadcasted_iota(jnp.int32, (8, EL), 1)
    slot = lane // SLOT
    inner, outer = slot == 0, slot == 1
    meets = (lane >= SLOT) & (lane < SLOT + ELY), (lane >= SLOT - ELY) & (lane < SLOT)

    def stack(own, lo, hi):
        first, second = [], []
        for i in range(4):
            moved = pltpu.roll(own[i], SLOT, 1)
            below = lo if i == 0 else pltpu.roll(lo, EL - SLOT * i, 1)
            above = hi if i == 1 else pltpu.roll(hi, (EL + SLOT - SLOT * i) % EL, 1)
            first.append(jnp.where(inner, below, moved))
            second.append(jnp.where(inner, moved, jnp.where(outer, above, 0.0)))
        return first, second

    def put(m, parts):
        for j, part in enumerate(parts):
            middle[m, :, EL * j : EL * j + EL] = jnp.concatenate(part, 0)

    put(MODES, stack([scale[...]] * 4, low[MODES], high[MODES]))

    def mode(m, _):
        parts = stack(tiles(condensed[m]), low[m], high[m])
        put(m, [add_rows(part, ELY, *meets) for part in parts])
        return 0

    lax.fori_loop(0, MODES, mode, 0, unroll=UNROLL)
    total = 0.0
    for i in range(4):
        send = selection(jnp.where(table[5:6] == i, table[2:3], -1), XL)
        total = total + take(middle[:, 8 * i : 8 * i + 8, :].reshape((MODES + 1) * 8, XL), send)
    left[...] = total[:, 0:EL].reshape(MODES + 1, 8, EL)
    right[...] = total[:, EL:XL].reshape(MODES + 1, 8, EL)


def middle_kernel(middle, table, block):
    spread = take(middle[...].reshape((MODES + 1) * NB, XL), selection(table[0:1], XL))
    block[...] = spread.reshape(MODES + 1, NB, XL)


def matrices_kernel(schur, matrix, shift):
    lane = lax.broadcasted_iota(jnp.int32, (NB, NB), 1)
    eye = lax.broadcasted_iota(jnp.int32, (NB, NB), 0) == lane
    across = jnp.where((lane >= 16) & (lane % 8 > 0), lane // 8 * 8 + 8 - lane % 8, lane)

    def mode(m, _):
        trace = jnp.sum(jnp.sum(jnp.where(eye, schur[m], 0.0), axis=0, keepdims=True), axis=1, keepdims=True)
        shift[m] = jnp.broadcast_to((0.5 * NB) / trace, (8, XL))
        rows = both_ascending(schur[m])
        parts = three_parts(jnp.take_along_axis(rows, across, axis=1, mode="promise_in_bounds"))
        for k, (part, _) in enumerate(TERMS):
            matrix[m, :, NB * k : NB * k + NB] = parts[part]
        return 0

    lax.fori_loop(0, MODES, mode, 0, unroll=UNROLL)


def krylov_kernel(
    block, left, right, schur, shift, table, basis, sums, keep_ref, weight_ref, mine_ref, parts, state, applied, spread
):
    sides = jnp.concatenate([left[...].reshape((MODES + 1) * 8, EL), right[...].reshape((MODES + 1) * 8, EL)], 1)
    for i in range(4):
        turn = selection(jnp.where(table[1:2] < 0, -1, table[1:2] + SLOT * i), XL)
        spread[:, 8 * i : 8 * i + 8, :] = take(sides, turn).reshape(MODES + 1, 8, XL)

    row, col = jnp.broadcast_to(table[3:4], (8, XL)), jnp.broadcast_to(table[4:5], (8, XL))
    grid_row = row - DEEP + lax.axis_index("ex") * ELX
    grid_col = col - DEEP + lax.axis_index("ey") * ELY
    last_row, last_col = lax.axis_size("ex") * ELX - 1, lax.axis_size("ey") * ELY - 1
    inside = (grid_row >= 0) & (grid_row <= last_row) & (grid_col >= 0) & (grid_col <= last_col) & (row < XROWS)
    own = (row >= DEEP) & (row < DEEP + ELX) & (col >= DEEP) & (col < DEEP + ELY)
    meets = (col == DEEP) | (col == DEEP + ELY), (col == DEEP - 1) | (col == DEEP + ELY - 1)
    mine_ref[...] = jnp.where(own, 1.0, 0.0).astype(F32)
    corner = lax.broadcasted_iota(jnp.int32, (8, XL), 0) == 0
    low_row, high_row, low_col, high_col = grid_row == 0, grid_row == last_row, grid_col == 0, grid_col == last_col
    for tile, (edge, other) in enumerate(((low_col, low_row), (high_row, low_col), (high_col, high_row), (low_row, high_col))):
        keep = jnp.where(inside & ~(edge | (corner & other)), 1.0, 0.0).astype(F32)
        keep_ref[8 * tile : 8 * tile + 8] = keep
        weight_ref[8 * tile : 8 * tile + 8] = jnp.where(own, keep * jnp.where(corner, 0.25, 0.5), 0.0).astype(F32)
    scale = jnp.where(inside[0:1], block[MODES, 0:1] + spread[MODES, 0:1], 0.0)

    def assemble(values):
        return keep_ref[...] * jnp.concatenate(add_columns(add_rows(tiles(values), PITCH, None, None), None, None), 0)

    def image(m, values):
        parts_of = three_parts(values)
        stacked = jnp.concatenate([parts_of[part] for _, part in TERMS], 0)
        return scale * lax.dot_general(schur[m], stacked, (((1,), (0,)), ((), ())), preferred_element_type=F32)

    def gather_mode(m):
        values = block[m] + spread[m]
        state[0, m] = keep_ref[...] * jnp.concatenate(add_columns(tiles(values), *meets), 0)

    def extend_mode(i):
        def run(m):
            images = image(m, state[i, m])
            applied[i, m] = images
            state[i + 1, m] = assemble(images) * shift[m, 0:1] - state[i, m]

        return run

    def sum_mode(m):
        v = [state[i, m] for i in range(3)]
        w = [applied[0, m], applied[1, m], image(m, v[2])]
        weight, mine = weight_ref[...], mine_ref[0:1]
        weighted = v[1] * weight
        own = [value * mine for value in v]
        k = 0
        for first, second in (
            (v[0], v[0] * weight), (v[0], weighted), (v[1], weighted),
            (own[0], w[0]), (own[1], w[0]), (own[1], w[1]), (own[2], w[1]), (own[2], w[2]),
        ):
            whole = jnp.sum(first * second, axis=0, keepdims=True)
            parts[pl.ds(MODES * k + m, 1), :] = whole[:, 0:EL] + whole[:, EL:XL]
            k += 1
        for i in range(3):
            basis[i, m] = v[i]

    def every(body):
        def step(m, _):
            body(m)
            return 0

        lax.fori_loop(0, MODES, step, 0, unroll=UNROLL)

    every(gather_mode)
    for i in range(2):
        every(extend_mode(i))
    every(sum_mode)
    ones = jnp.ones((8, EL), F32)
    total = lax.dot_general(ones, parts[...], (((1,), (1,)), ((), ())), precision=HIGHEST, preferred_element_type=F32)
    for at in range(0, sums.shape[0], 8):
        sums[at : at + 8] = total


def finish_kernel(gathered, basis, base, couple, cell, out, coefs, mixed, blocks):
    total = jnp.broadcast_to(jnp.sum(gathered[...].reshape(-1, EL), axis=0, keepdims=True), (8, EL))
    b0, b1, b2, h0, h1, h2, h3, h4 = [
        total if k == 0 else pltpu.roll(total, EL - MODES * k, 1) for k in range(8)
    ]
    tiny = 2e-7
    l1, l2 = h1 / h0, h2 / h0
    d1 = h2 - l1 * h1
    ok1 = d1 > tiny * h2
    d1 = jnp.where(ok1, d1, 1.0)
    l12 = jnp.where(ok1, (h3 - l1 * h2) / d1, 0.0)
    d2 = h4 - l2 * h2 - l12 * l12 * d1
    ok2 = d2 > tiny * h4
    y1 = b1 - l1 * b0
    y2 = b2 - l2 * b0 - l12 * y1
    c2 = jnp.where(ok2, y2 / jnp.where(ok2, d2, 1.0), 0.0)
    c1 = jnp.where(ok1, y1 / d1, 0.0) - l12 * c2
    c0 = b0 / h0 - l1 * c1 - l2 * c2
    for i, c in enumerate((c0, c1, c2)):
        coefs[i] = jnp.transpose(jnp.broadcast_to(c[0:1], (EL, EL)))[0:MODES]
    place = (cell[0:1] // ELY + DEEP) * PITCH + cell[0:1] % ELY + DEEP

    def combine(m, _):
        c = [jnp.concatenate([coefs[i, pl.ds(m, 1), :]] * 2, 1) for i in range(3)]
        x = c[0] * basis[0, m] + c[1] * basis[1, m] + c[2] * basis[2, m]
        mixed[pl.ds(pl.multiple_of(m * NB, NB), NB), :] = both_ascending(x)
        return 0

    lax.fori_loop(0, MODES, combine, 0, unroll=UNROLL)
    solved = take(mixed[...], selection(place, XL))
    blocks[...] = jnp.zeros_like(blocks)
    for m in range(MODES):
        x = solved[m * NB : m * NB + NB]
        q, r = m // QUAD, m % QUAD
        blocks[q, NB * r : NB * r + NB, EL * r : EL * r + EL] = x
        for tile in range(4):
            out[pl.ds(8 * tile * MODES + m, 8, stride=MODES), :] = x[8 * tile : 8 * tile + 8]
    for q in range(MODES // QUAD):
        lifted = dot_of_parts(split(couple[q]), split(blocks[q]))
        for r in range(QUAD):
            m = QUAD * q + r
            within = base[m, 0:NI] - lifted[0:NI, EL * r : EL * r + EL]
            within = jnp.concatenate([within, jnp.zeros((PADDED - NODES, EL), F32)], 0)
            out[pl.ds(NB * MODES + m, PADDED - NB, stride=MODES), :] = within


def call(kernel, shapes=(), scratch=(), far=0, far_out=None):
    def run(*operands):
        many = isinstance(shapes, list)
        outs = [s if isinstance(s, pl.MemoryRef) else pltpu.VMEM(s, F32) for s in (shapes if many else [shapes])]
        whole, away = pl.BlockSpec(memory_space=pltpu.VMEM), pl.BlockSpec(memory_space=pl.ANY)
        near = tuple(pltpu.with_memory_space_constraint(o, pltpu.VMEM) for o in operands[far:])
        if far_out:
            outs = [jax.ShapeDtypeStruct(far_out, F32)]
        specs = [away if far_out else whole] * len(outs)
        return pl.pallas_call(
            kernel,
            out_shape=outs if many else outs[0],
            in_specs=[away] * far + [whole] * len(near),
            out_specs=specs if many else specs[0],
            scratch_shapes=list(scratch),
            compiler_params=pltpu.CompilerParams(vmem_limit_bytes=16 << 20),
            name=kernel.__name__,
        )(*(pltpu.with_memory_space_constraint(o, pltpu.HBM) for o in operands[:far]), *near)

    return run


def swap(array):
    return lax.all_to_all(array, "fourier", split_axis=0, concat_axis=0, tiled=True)


def ring(axis, step):
    count = lax.axis_size(axis)
    return [(i, (i + step) % count) for i in range(count)]


def neighbours(to_low, to_high, axis):
    return lax.ppermute(to_high, axis, ring(axis, 1)), lax.ppermute(to_low, axis, ring(axis, -1))


def on_device(forcing, element_coef, schur, couple, inner_inv, element_cell):
    parts = lax.axis_size("fourier")
    devices = lax.axis_size("ex") * lax.axis_size("ey")
    group = PADDED // parts
    table = jnp.asarray(real_transform())
    exchanged = (parts, group, MODES, EL)
    lanes = (8, EL)
    ints = pltpu.VMEM(lanes, jnp.int32)

    planes, order, index, scale, stored = call(
        enter_kernel, [(PADDED, MODES, EL), ints, ints, lanes, lanes],
        [
            pltpu.SemaphoreType.DMA((CHUNKS,)),
            pltpu.SemaphoreType.DMA((2,)),
            pltpu.VMEM((1, EL), F32),
            pltpu.VMEM((1, EL), jnp.int32),
        ],
        far=3,
    )(jnp.transpose(forcing, (1, 0, 2)), element_coef.reshape(1, EL), element_cell.reshape(1, EL))
    planes = swap(planes).reshape(exchanged)
    spectral = swap(call(transform_kernel, exchanged)(table, planes).reshape(PADDED, MODES, EL))
    spectral = spectral.reshape(PADDED * MODES, EL)

    message, extended = (MODES + 1, 8, EL), (MODES + 1, NB, XL)
    table_of_lanes = jnp.asarray(lane_tables())
    condensed, down, up = call(condense_kernel, [(MODES, NB, EL), message, message])(spectral, order, scale, couple)
    low, high = neighbours(down, up, "ex")
    base, turned = call(
        interior_kernel, [(MODES, 56, EL), (MODES // QUAD, 56, QUAD * NB)], [pltpu.VMEM((QUAD * NB, EL), F32)]
    )(spectral, stored, jnp.transpose(inner_inv, (1, 0, 2)).reshape(NI * MODES, NI), couple)
    low, high, base, turned, schur = lax.optimization_barrier((low, high, base, turned, schur))
    left, right, middle = call(columns_kernel, [message, message, extended])(
        condensed, scale, low, high, table_of_lanes
    )
    left, right = neighbours(left, right, "ey")
    matrix, shift = call(
        matrices_kernel, [pltpu.VMEM((MODES, NB, len(TERMS) * NB), jnp.bfloat16), (MODES, 8, XL)]
    )(schur)
    block = call(middle_kernel, extended)(middle, table_of_lanes)
    basis, sums = call(
        krylov_kernel,
        [(3, MODES, NB, XL), (devices, EL)],
        [
            pltpu.VMEM((NB, XL), F32),
            pltpu.VMEM((NB, XL), F32),
            pltpu.VMEM((8, XL), F32),
            pltpu.VMEM((EL, EL), F32),
            pltpu.VMEM((3, MODES, NB, XL), F32),
            pltpu.VMEM((2, MODES, NB, XL), F32),
            pltpu.VMEM(extended, F32),
        ],
    )(block, left, right, matrix, shift, table_of_lanes)
    gathered = lax.all_to_all(sums.reshape(devices, 1, EL), ("ex", "ey"), split_axis=0, concat_axis=0, tiled=True)
    modal = call(finish_kernel, (PADDED * MODES, EL), [pltpu.VMEM((3, MODES, EL), F32), pltpu.VMEM((MODES * NB, XL), F32), pltpu.VMEM((MODES // QUAD, QUAD * NB, QUAD * EL), F32)])(
        gathered, basis, base, turned, index
    )
    modal = swap(modal.reshape(PADDED, MODES, EL)).reshape(exchanged)
    velocity = swap(call(transform_kernel, exchanged)(table.T, modal).reshape(PADDED, MODES, EL))
    velocity = call(leave_kernel, far_out=(NODES, MODES, EL), scratch=[pltpu.SemaphoreType.DMA((CHUNKS,))])(velocity)
    return jnp.transpose(velocity, (1, 0, 2))


def solution(mesh):
    placed = (
        P("fourier", None, ("ex", "ey")),
        P(("ex", "ey")),
        P("fourier", None, None),
        P("fourier", None, None),
        P("fourier", None, None),
        P(("ex", "ey")),
    )
    return jax.shard_map(
        on_device,
        mesh=mesh,
        in_specs=placed,
        out_specs=P("fourier", None, ("ex", "ey")),
        check_vma=False,
    )
```

```python
import math

import jax
import jax.numpy as jnp
import numpy as np
from jax import lax
from jax.experimental import pallas as pl
from jax.experimental.pallas import tpu as pltpu
from jax.sharding import PartitionSpec as P

P_SIZE = 8
NZ = 128
ELX = 8
ELY = 16
NODES = 81
NB = 32
NI = 49
EL = ELX * ELY
PADDED = 88
MODES = 16
DEEP = 2
XROWS = ELX + 2 * DEEP
XCOLS = ELY + 2 * DEEP
PITCH = XCOLS
XL = 256
SLOT = DEEP * ELY
UNROLL = 16
TERMS = ((0, 0), (0, 1), (1, 0), (1, 1), (0, 2), (2, 0))
QUAD = 4
CHUNKS = 1
HIGHEST = lax.Precision.HIGHEST
F32 = jnp.float32


def real_transform():
    k = np.arange(NZ)[:, None]
    z = np.arange(NZ)[None, :]
    angle = 2.0 * math.pi * (((k + 1) // 2 * z) % NZ) / NZ
    w = np.where(k % 2 == 1, np.cos(angle), np.sin(angle)) * math.sqrt(2.0 / NZ)
    w[0] = 1.0 / math.sqrt(NZ)
    w[NZ - 1] = np.cos(math.pi * np.arange(NZ)) / math.sqrt(NZ)
    return w.astype(np.float32)


def lane_tables():
    lane = np.arange(XL)
    row, col = lane // PITCH, lane % PITCH
    valid = row < XROWS
    middle = valid & (col >= DEEP) & (col < DEEP + ELY)
    spread = np.where(middle, row * ELY + col - DEEP, -1)
    turn = row * DEEP + np.where(col < DEEP, col, EL + col - DEEP - ELY)
    turn = np.where(valid & ~middle, turn, -1)
    at = lane % SLOT
    send = at // DEEP * ELY + at % DEEP + np.where(lane >= EL, ELY - DEEP, 0)
    send = np.where(at < DEEP * XROWS, send, -1)
    return np.stack([spread, turn, send, row, col, lane % EL // SLOT, row, row]).astype(np.int32)


def pick(values, index):
    return jnp.take_along_axis(values, jnp.broadcast_to(index, values.shape), axis=1, mode="promise_in_bounds")


def dot(a, b):
    return lax.dot_general(a, b, (((1,), (0,)), ((), ())), precision=HIGHEST, preferred_element_type=F32)


def selection(index, size):
    return jnp.where(lax.broadcasted_iota(jnp.int32, (size, index.shape[1]), 0) == index, 1.0, 0.0).astype(F32)


def three_parts(values):
    high = values.astype(jnp.bfloat16)
    rest = values - high.astype(F32)
    middle = rest.astype(jnp.bfloat16)
    return high, middle, (rest - middle.astype(F32)).astype(jnp.bfloat16)


def take(values, chosen):
    high, middle, low = three_parts(values)
    chosen = chosen.astype(jnp.bfloat16)

    def product(part):
        return lax.dot_general(part, chosen, (((1,), (0,)), ((), ())), preferred_element_type=F32)

    return (product(high) + product(middle)) + product(low)


def add_rows(t, step, before, behind):
    width = t[0].shape[1]
    zero = lax.broadcasted_iota(jnp.int32, t[0].shape, 0) == 0
    back = width - step

    def masked(mask, values):
        return values if mask is None else jnp.where(mask, values, 0.0)

    from0 = masked(before, pltpu.roll(jnp.where(zero, t[1], 0.0), step, 1))
    from3 = masked(before, pltpu.roll(jnp.where(zero, t[2], t[1]), step, 1))
    from1 = masked(behind, pltpu.roll(jnp.where(zero, t[0], t[3]), back, 1))
    from2 = masked(behind, pltpu.roll(jnp.where(zero, t[3], 0.0), back, 1))
    return [t[0] + from0, t[1] + from1, t[2] + from2, t[3] + from3]


def add_columns(t, before, behind):
    turned = add_rows([t[1], t[2], t[3], t[0]], 1, before, behind)
    return [turned[3], turned[0], turned[1], turned[2]]


def tiles(values):
    return [values[8 * i : 8 * i + 8] for i in range(4)]


def split(values):
    high = values.astype(jnp.bfloat16)
    return high, (values - high.astype(F32)).astype(jnp.bfloat16)


def dot_of_parts(a, b):
    (a_high, a_low), (b_high, b_low) = a, b

    def product(first, second):
        return lax.dot_general(first, second, (((1,), (0,)), ((), ())), preferred_element_type=F32)

    return product(a_high, b_low) + product(a_low, b_high) + product(a_high, b_high)


def transform_kernel(table, planes, out):
    groups, nodes = planes.shape[0], planes.shape[1]
    held = split(table[...])
    for n in range(nodes):
        block = planes[:, n].reshape(NZ, EL)
        out[:, n] = dot_of_parts(held, split(block)).reshape(groups, NZ // groups, EL)


def copies(source, target, nodes, done):
    step = -(-nodes // CHUNKS)
    cuts = [(at, min(step, nodes - at)) for at in range(0, nodes, step)]
    return [
        pltpu.make_async_copy(source.at[pl.ds(at, size)], target.at[pl.ds(at, size)], done.at[i])
        for i, (at, size) in enumerate(cuts)
    ]


def enter_kernel(forcing, coef_far, cell_far, planes, order, index, scale, stored, done, small, coef, cell):
    nodes = forcing.shape[0]
    fetched = [pltpu.make_async_copy(coef_far, coef, small.at[0]), pltpu.make_async_copy(cell_far, cell, small.at[1])]
    moved = copies(forcing, planes, nodes, done)
    for copy in fetched + moved:
        copy.start()
    planes[nodes:PADDED] = jnp.zeros((PADDED - nodes, planes.shape[1], EL), F32)
    for copy in fetched:
        copy.wait()
    lane = lax.broadcasted_iota(jnp.int32, (EL, EL), 1)
    elem = lax.broadcasted_iota(jnp.int32, (EL, EL), 0)
    cells = jnp.transpose(jnp.broadcast_to(cell[...], (EL, EL)))
    found = jnp.sum(jnp.where(cells == lane, elem, 0), axis=0, keepdims=True)
    order[...] = jnp.broadcast_to(found, (8, EL))
    index[...] = jnp.broadcast_to(cell[...], (8, EL))
    stored[...] = jnp.broadcast_to(coef[...], (8, EL))
    scale[...] = pick(jnp.broadcast_to(coef[...], (8, EL)), found)
    for copy in moved:
        copy.wait()


def leave_kernel(planes, velocity, done):
    moved = copies(planes, velocity, velocity.shape[0], done)
    for copy in moved:
        copy.start()
    for copy in moved:
        copy.wait()


def flipped(tile):
    back = (8 - lax.broadcasted_iota(jnp.int32, tile.shape, 0)) % 8
    return jnp.take_along_axis(tile, back, axis=0, mode="promise_in_bounds")


def both_ascending(values):
    return jnp.concatenate([values[0:16], flipped(values[16:24]), flipped(values[24:32])], 0)


def condense_kernel(spectral, order, scale, couple, condensed, down, up):
    lane = lax.broadcasted_iota(jnp.int32, (8, EL), 1)
    row, col, slot = lane // ELY, lane % ELY, lane // SLOT
    inner_row, inner_col = (row > 0, row < ELX - 1), (col > 0, col < ELY - 1)

    def messages(t):
        low, high = t[0], t[3]
        for i in (1, 2, 3):
            low = jnp.where(slot == i, pltpu.roll(t[i], SLOT * i, 1), low)
            high = jnp.where(slot == i - 1, pltpu.roll(t[i - 1], SLOT * i, 1), high)
        return low, high

    down[MODES], up[MODES] = messages([scale[...]] * 4)

    def mode(m, _):
        fields = spectral[pl.ds(m, PADDED, stride=MODES), :]
        value = fields[0:NB] - dot_of_parts(split(couple[m]), split(fields[NB:NODES]))
        t = tiles(both_ascending(pick(value, order[0:1])))
        t = add_columns(add_rows(t, ELY, *inner_row), *inner_col)
        condensed[m] = jnp.concatenate(t, 0)
        down[m], up[m] = messages(t)
        return 0

    lax.fori_loop(0, MODES, mode, 0, unroll=UNROLL)


def interior_kernel(spectral, stored, inner, couple, base, turned, wide):
    inverse = 1.0 / stored[0:1]

    def mode(m, _):
        within = spectral[pl.ds(NB * MODES + m, PADDED - NB, stride=MODES), :][0:NI]
        base[m, 0:NI] = dot(inner[pl.ds(m, NI, stride=MODES), :], within) * inverse
        return 0

    lax.fori_loop(0, MODES, mode, 0, unroll=UNROLL)
    wide[...] = jnp.zeros_like(wide)
    for q in range(MODES // QUAD):
        wide[:, 0:NI] = couple[QUAD * q : QUAD * q + QUAD].reshape(QUAD * NB, NI)
        turned[q] = jnp.transpose(wide[...])[0 : turned.shape[1]]


def columns_kernel(condensed, scale, low, high, table, left, right, middle):
    lane = lax.broadcasted_iota(jnp.int32, (8, EL), 1)
    slot = lane // SLOT
    inner, outer = slot == 0, slot == 1
    meets = (lane >= SLOT) & (lane < SLOT + ELY), (lane >= SLOT - ELY) & (lane < SLOT)

    def stack(own, lo, hi):
        first, second = [], []
        for i in range(4):
            moved = pltpu.roll(own[i], SLOT, 1)
            below = lo if i == 0 else pltpu.roll(lo, EL - SLOT * i, 1)
            above = hi if i == 1 else pltpu.roll(hi, (EL + SLOT - SLOT * i) % EL, 1)
            first.append(jnp.where(inner, below, moved))
            second.append(jnp.where(inner, moved, jnp.where(outer, above, 0.0)))
        return first, second

    def put(m, parts):
        for j, part in enumerate(parts):
            middle[m, :, EL * j : EL * j + EL] = jnp.concatenate(part, 0)

    put(MODES, stack([scale[...]] * 4, low[MODES], high[MODES]))

    def mode(m, _):
        parts = stack(tiles(condensed[m]), low[m], high[m])
        put(m, [add_rows(part, ELY, *meets) for part in parts])
        return 0

    lax.fori_loop(0, MODES, mode, 0, unroll=UNROLL)
    total = 0.0
    for i in range(4):
        send = selection(jnp.where(table[5:6] == i, table[2:3], -1), XL)
        total = total + take(middle[:, 8 * i : 8 * i + 8, :].reshape((MODES + 1) * 8, XL), send)
    left[...] = total[:, 0:EL].reshape(MODES + 1, 8, EL)
    right[...] = total[:, EL:XL].reshape(MODES + 1, 8, EL)


def middle_kernel(middle, table, block):
    spread = take(middle[...].reshape((MODES + 1) * NB, XL), selection(table[0:1], XL))
    block[...] = spread.reshape(MODES + 1, NB, XL)


def matrices_kernel(schur, matrix, shift):
    lane = lax.broadcasted_iota(jnp.int32, (NB, NB), 1)
    eye = lax.broadcasted_iota(jnp.int32, (NB, NB), 0) == lane
    across = jnp.where((lane >= 16) & (lane % 8 > 0), lane // 8 * 8 + 8 - lane % 8, lane)

    def mode(m, _):
        trace = jnp.sum(jnp.sum(jnp.where(eye, schur[m], 0.0), axis=0, keepdims=True), axis=1, keepdims=True)
        shift[m] = jnp.broadcast_to((0.5 * NB) / trace, (8, XL))
        rows = both_ascending(schur[m])
        parts = three_parts(jnp.take_along_axis(rows, across, axis=1, mode="promise_in_bounds"))
        for k, (part, _) in enumerate(TERMS):
            matrix[m, :, NB * k : NB * k + NB] = parts[part]
        return 0

    lax.fori_loop(0, MODES, mode, 0, unroll=UNROLL)


def krylov_kernel(
    block, left, right, schur, shift, table, basis, sums, keep_ref, weight_ref, mine_ref, parts, state, applied, spread
):
    sides = jnp.concatenate([left[...].reshape((MODES + 1) * 8, EL), right[...].reshape((MODES + 1) * 8, EL)], 1)
    for i in range(4):
        turn = selection(jnp.where(table[1:2] < 0, -1, table[1:2] + SLOT * i), XL)
        spread[:, 8 * i : 8 * i + 8, :] = take(sides, turn).reshape(MODES + 1, 8, XL)

    row, col = jnp.broadcast_to(table[3:4], (8, XL)), jnp.broadcast_to(table[4:5], (8, XL))
    grid_row = row - DEEP + lax.axis_index("ex") * ELX
    grid_col = col - DEEP + lax.axis_index("ey") * ELY
    last_row, last_col = lax.axis_size("ex") * ELX - 1, lax.axis_size("ey") * ELY - 1
    inside = (grid_row >= 0) & (grid_row <= last_row) & (grid_col >= 0) & (grid_col <= last_col) & (row < XROWS)
    own = (row >= DEEP) & (row < DEEP + ELX) & (col >= DEEP) & (col < DEEP + ELY)
    meets = (col == DEEP) | (col == DEEP + ELY), (col == DEEP - 1) | (col == DEEP + ELY - 1)
    mine_ref[...] = jnp.where(own, 1.0, 0.0).astype(F32)
    corner = lax.broadcasted_iota(jnp.int32, (8, XL), 0) == 0
    low_row, high_row, low_col, high_col = grid_row == 0, grid_row == last_row, grid_col == 0, grid_col == last_col
    for tile, (edge, other) in enumerate(((low_col, low_row), (high_row, low_col), (high_col, high_row), (low_row, high_col))):
        keep = jnp.where(inside & ~(edge | (corner & other)), 1.0, 0.0).astype(F32)
        keep_ref[8 * tile : 8 * tile + 8] = keep
        weight_ref[8 * tile : 8 * tile + 8] = jnp.where(own, keep * jnp.where(corner, 0.25, 0.5), 0.0).astype(F32)
    scale = jnp.where(inside[0:1], block[MODES, 0:1] + spread[MODES, 0:1], 0.0)

    def assemble(values):
        return keep_ref[...] * jnp.concatenate(add_columns(add_rows(tiles(values), PITCH, None, None), None, None), 0)

    def image(m, values):
        parts_of = three_parts(values)
        stacked = jnp.concatenate([parts_of[part] for _, part in TERMS], 0)
        return scale * lax.dot_general(schur[m], stacked, (((1,), (0,)), ((), ())), preferred_element_type=F32)

    def gather_mode(m):
        values = block[m] + spread[m]
        state[0, m] = keep_ref[...] * jnp.concatenate(add_columns(tiles(values), *meets), 0)

    def extend_mode(i):
        def run(m):
            images = image(m, state[i, m])
            applied[i, m] = images
            state[i + 1, m] = assemble(images) * shift[m, 0:1] - state[i, m]

        return run

    def sum_mode(m):
        v = [state[i, m] for i in range(3)]
        w = [applied[0, m], applied[1, m], image(m, v[2])]
        weight, mine = weight_ref[...], mine_ref[0:1]
        weighted = v[1] * weight
        own = [value * mine for value in v]
        k = 0
        for first, second in (
            (v[0], v[0] * weight), (v[0], weighted), (v[1], weighted),
            (own[0], w[0]), (own[1], w[0]), (own[1], w[1]), (own[2], w[1]), (own[2], w[2]),
        ):
            whole = jnp.sum(first * second, axis=0, keepdims=True)
            parts[pl.ds(MODES * k + m, 1), :] = whole[:, 0:EL] + whole[:, EL:XL]
            k += 1
        for i in range(3):
            basis[i, m] = v[i]

    def every(body):
        def step(m, _):
            body(m)
            return 0

        lax.fori_loop(0, MODES, step, 0, unroll=UNROLL)

    every(gather_mode)
    for i in range(2):
        every(extend_mode(i))
    every(sum_mode)
    ones = jnp.ones((8, EL), F32)
    total = lax.dot_general(ones, parts[...], (((1,), (1,)), ((), ())), precision=HIGHEST, preferred_element_type=F32)
    for at in range(0, sums.shape[0], 8):
        sums[at : at + 8] = total


def finish_kernel(gathered, basis, base, couple, cell, out, coefs, mixed, blocks):
    total = jnp.broadcast_to(jnp.sum(gathered[...].reshape(-1, EL), axis=0, keepdims=True), (8, EL))
    b0, b1, b2, h0, h1, h2, h3, h4 = [
        total if k == 0 else pltpu.roll(total, EL - MODES * k, 1) for k in range(8)
    ]
    tiny = 2e-7
    l1, l2 = h1 / h0, h2 / h0
    d1 = h2 - l1 * h1
    ok1 = d1 > tiny * h2
    d1 = jnp.where(ok1, d1, 1.0)
    l12 = jnp.where(ok1, (h3 - l1 * h2) / d1, 0.0)
    d2 = h4 - l2 * h2 - l12 * l12 * d1
    ok2 = d2 > tiny * h4
    y1 = b1 - l1 * b0
    y2 = b2 - l2 * b0 - l12 * y1
    c2 = jnp.where(ok2, y2 / jnp.where(ok2, d2, 1.0), 0.0)
    c1 = jnp.where(ok1, y1 / d1, 0.0) - l12 * c2
    c0 = b0 / h0 - l1 * c1 - l2 * c2
    for i, c in enumerate((c0, c1, c2)):
        coefs[i] = jnp.transpose(jnp.broadcast_to(c[0:1], (EL, EL)))[0:MODES]
    place = (cell[0:1] // ELY + DEEP) * PITCH + cell[0:1] % ELY + DEEP

    chosen = selection(place, XL)
    blocks[...] = jnp.zeros_like(blocks)
    for q in range(MODES // QUAD):
        for r in range(QUAD):
            m = QUAD * q + r
            c = [jnp.concatenate([coefs[i, m : m + 1, :]] * 2, 1) for i in range(3)]
            x = c[0] * basis[0, m] + c[1] * basis[1, m] + c[2] * basis[2, m]
            mixed[m * NB : m * NB + NB, :] = both_ascending(x)
        solved = take(mixed[QUAD * q * NB : QUAD * (q + 1) * NB, :], chosen)
        for r in range(QUAD):
            x = solved[r * NB : r * NB + NB]
            blocks[q, NB * r : NB * r + NB, EL * r : EL * r + EL] = x
            for tile in range(4):
                out[pl.ds(8 * tile * MODES + QUAD * q + r, 8, stride=MODES), :] = x[8 * tile : 8 * tile + 8]
        lifted = dot_of_parts(split(couple[q]), split(blocks[q]))
        for r in range(QUAD):
            m = QUAD * q + r
            within = base[m, 0:NI] - lifted[0:NI, EL * r : EL * r + EL]
            within = jnp.concatenate([within, jnp.zeros((PADDED - NODES, EL), F32)], 0)
            out[pl.ds(NB * MODES + m, PADDED - NB, stride=MODES), :] = within


def call(kernel, shapes=(), scratch=(), far=0, far_out=None):
    def run(*operands):
        many = isinstance(shapes, list)
        outs = [s if isinstance(s, pl.MemoryRef) else pltpu.VMEM(s, F32) for s in (shapes if many else [shapes])]
        whole, away = pl.BlockSpec(memory_space=pltpu.VMEM), pl.BlockSpec(memory_space=pl.ANY)
        near = tuple(pltpu.with_memory_space_constraint(o, pltpu.VMEM) for o in operands[far:])
        if far_out:
            outs = [jax.ShapeDtypeStruct(far_out, F32)]
        specs = [away if far_out else whole] * len(outs)
        return pl.pallas_call(
            kernel,
            out_shape=outs if many else outs[0],
            in_specs=[away] * far + [whole] * len(near),
            out_specs=specs if many else specs[0],
            scratch_shapes=list(scratch),
            compiler_params=pltpu.CompilerParams(vmem_limit_bytes=16 << 20),
            name=kernel.__name__,
        )(*(pltpu.with_memory_space_constraint(o, pltpu.HBM) for o in operands[:far]), *near)

    return run


def swap(array):
    return lax.all_to_all(array, "fourier", split_axis=0, concat_axis=0, tiled=True)


def ring(axis, step):
    count = lax.axis_size(axis)
    return [(i, (i + step) % count) for i in range(count)]


def neighbours(to_low, to_high, axis):
    return lax.ppermute(to_high, axis, ring(axis, 1)), lax.ppermute(to_low, axis, ring(axis, -1))


def on_device(forcing, element_coef, schur, couple, inner_inv, element_cell):
    parts = lax.axis_size("fourier")
    devices = lax.axis_size("ex") * lax.axis_size("ey")
    group = PADDED // parts
    table = jnp.asarray(real_transform())
    exchanged = (parts, group, MODES, EL)
    lanes = (8, EL)
    ints = pltpu.VMEM(lanes, jnp.int32)

    planes, order, index, scale, stored = call(
        enter_kernel, [(PADDED, MODES, EL), ints, ints, lanes, lanes],
        [
            pltpu.SemaphoreType.DMA((CHUNKS,)),
            pltpu.SemaphoreType.DMA((2,)),
            pltpu.VMEM((1, EL), F32),
            pltpu.VMEM((1, EL), jnp.int32),
        ],
        far=3,
    )(jnp.transpose(forcing, (1, 0, 2)), element_coef.reshape(1, EL), element_cell.reshape(1, EL))
    planes = swap(planes).reshape(exchanged)
    spectral = swap(call(transform_kernel, exchanged)(table, planes).reshape(PADDED, MODES, EL))
    spectral = spectral.reshape(PADDED * MODES, EL)

    message, extended = (MODES + 1, 8, EL), (MODES + 1, NB, XL)
    table_of_lanes = jnp.asarray(lane_tables())
    condensed, down, up = call(condense_kernel, [(MODES, NB, EL), message, message])(spectral, order, scale, couple)
    low, high = neighbours(down, up, "ex")
    base, turned = call(
        interior_kernel, [(MODES, 56, EL), (MODES // QUAD, 56, QUAD * NB)], [pltpu.VMEM((QUAD * NB, EL), F32)]
    )(spectral, stored, jnp.transpose(inner_inv, (1, 0, 2)).reshape(NI * MODES, NI), couple)
    low, high, base, turned, schur = lax.optimization_barrier((low, high, base, turned, schur))
    left, right, middle = call(columns_kernel, [message, message, extended])(
        condensed, scale, low, high, table_of_lanes
    )
    left, right = neighbours(left, right, "ey")
    matrix, shift = call(
        matrices_kernel, [pltpu.VMEM((MODES, NB, len(TERMS) * NB), jnp.bfloat16), (MODES, 8, XL)]
    )(schur)
    block = call(middle_kernel, extended)(middle, table_of_lanes)
    basis, sums = call(
        krylov_kernel,
        [(3, MODES, NB, XL), (devices, EL)],
        [
            pltpu.VMEM((NB, XL), F32),
            pltpu.VMEM((NB, XL), F32),
            pltpu.VMEM((8, XL), F32),
            pltpu.VMEM((EL, EL), F32),
            pltpu.VMEM((3, MODES, NB, XL), F32),
            pltpu.VMEM((2, MODES, NB, XL), F32),
            pltpu.VMEM(extended, F32),
        ],
    )(block, left, right, matrix, shift, table_of_lanes)
    gathered = lax.all_to_all(sums.reshape(devices, 1, EL), ("ex", "ey"), split_axis=0, concat_axis=0, tiled=True)
    modal = call(finish_kernel, (PADDED * MODES, EL), [pltpu.VMEM((3, MODES, EL), F32), pltpu.VMEM((MODES * NB, XL), F32), pltpu.VMEM((MODES // QUAD, QUAD * NB, QUAD * EL), F32)])(
        gathered, basis, base, turned, index
    )
    modal = swap(modal.reshape(PADDED, MODES, EL)).reshape(exchanged)
    velocity = swap(call(transform_kernel, exchanged)(table.T, modal).reshape(PADDED, MODES, EL))
    velocity = call(leave_kernel, far_out=(NODES, MODES, EL), scratch=[pltpu.SemaphoreType.DMA((CHUNKS,))])(velocity)
    return jnp.transpose(velocity, (1, 0, 2))


def solution(mesh):
    placed = (
        P("fourier", None, ("ex", "ey")),
        P(("ex", "ey")),
        P("fourier", None, None),
        P("fourier", None, None),
        P("fourier", None, None),
        P(("ex", "ey")),
    )
    return jax.shard_map(
        on_device,
        mesh=mesh,
        in_specs=placed,
        out_specs=P("fourier", None, ("ex", "ey")),
        check_vma=False,
    )
```

```python
import math

import jax
import jax.numpy as jnp
import numpy as np
from jax import lax
from jax.experimental import pallas as pl
from jax.experimental.pallas import tpu as pltpu
from jax.sharding import PartitionSpec as P

P_SIZE = 8
NZ = 128
ELX = 8
ELY = 16
NODES = 81
NB = 32
NI = 49
EL = ELX * ELY
PADDED = 88
MODES = 16
DEEP = 2
XROWS = ELX + 2 * DEEP
XCOLS = ELY + 2 * DEEP
PITCH = XCOLS
XL = 256
SLOT = DEEP * ELY
UNROLL = 16
TERMS = ((0, 0), (0, 1), (1, 0), (1, 1), (0, 2), (2, 0))
QUAD = 4
CHUNKS = 1
HIGHEST = lax.Precision.HIGHEST
F32 = jnp.float32


def real_transform():
    k = np.arange(NZ)[:, None]
    z = np.arange(NZ)[None, :]
    angle = 2.0 * math.pi * (((k + 1) // 2 * z) % NZ) / NZ
    w = np.where(k % 2 == 1, np.cos(angle), np.sin(angle)) * math.sqrt(2.0 / NZ)
    w[0] = 1.0 / math.sqrt(NZ)
    w[NZ - 1] = np.cos(math.pi * np.arange(NZ)) / math.sqrt(NZ)
    return w.astype(np.float32)


def lane_tables():
    lane = np.arange(XL)
    row, col = lane // PITCH, lane % PITCH
    valid = row < XROWS
    middle = valid & (col >= DEEP) & (col < DEEP + ELY)
    spread = np.where(middle, row * ELY + col - DEEP, -1)
    turn = row * DEEP + np.where(col < DEEP, col, EL + col - DEEP - ELY)
    turn = np.where(valid & ~middle, turn, -1)
    at = lane % SLOT
    send = at // DEEP * ELY + at % DEEP + np.where(lane >= EL, ELY - DEEP, 0)
    send = np.where(at < DEEP * XROWS, send, -1)
    return np.stack([spread, turn, send, row, col, lane % EL // SLOT, row, row]).astype(np.int32)


def pick(values, index):
    return jnp.take_along_axis(values, jnp.broadcast_to(index, values.shape), axis=1, mode="promise_in_bounds")


def dot(a, b):
    return lax.dot_general(a, b, (((1,), (0,)), ((), ())), precision=HIGHEST, preferred_element_type=F32)


def selection(index, size):
    return jnp.where(lax.broadcasted_iota(jnp.int32, (size, index.shape[1]), 0) == index, 1.0, 0.0).astype(F32)


def three_parts(values):
    high = values.astype(jnp.bfloat16)
    rest = values - high.astype(F32)
    middle = rest.astype(jnp.bfloat16)
    return high, middle, (rest - middle.astype(F32)).astype(jnp.bfloat16)


def take(values, chosen):
    high, middle, low = three_parts(values)
    chosen = chosen.astype(jnp.bfloat16)

    def product(part):
        return lax.dot_general(part, chosen, (((1,), (0,)), ((), ())), preferred_element_type=F32)

    return (product(high) + product(middle)) + product(low)


def add_rows(t, step, before, behind):
    width = t[0].shape[1]
    zero = lax.broadcasted_iota(jnp.int32, t[0].shape, 0) == 0
    back = width - step

    def masked(mask, values):
        return values if mask is None else jnp.where(mask, values, 0.0)

    from0 = masked(before, pltpu.roll(jnp.where(zero, t[1], 0.0), step, 1))
    from3 = masked(before, pltpu.roll(jnp.where(zero, t[2], t[1]), step, 1))
    from1 = masked(behind, pltpu.roll(jnp.where(zero, t[0], t[3]), back, 1))
    from2 = masked(behind, pltpu.roll(jnp.where(zero, t[3], 0.0), back, 1))
    return [t[0] + from0, t[1] + from1, t[2] + from2, t[3] + from3]


def add_columns(t, before, behind):
    turned = add_rows([t[1], t[2], t[3], t[0]], 1, before, behind)
    return [turned[3], turned[0], turned[1], turned[2]]


def tiles(values):
    return [values[8 * i : 8 * i + 8] for i in range(4)]


def split(values):
    high = values.astype(jnp.bfloat16)
    return high, (values - high.astype(F32)).astype(jnp.bfloat16)


def dot_of_parts(a, b):
    (a_high, a_low), (b_high, b_low) = a, b

    def product(first, second):
        return lax.dot_general(first, second, (((1,), (0,)), ((), ())), preferred_element_type=F32)

    return product(a_high, b_low) + product(a_low, b_high) + product(a_high, b_high)


def transform_kernel(table, planes, out):
    groups, nodes = planes.shape[0], planes.shape[1]
    held = split(table[...])
    for n in range(nodes):
        block = planes[:, n].reshape(NZ, EL)
        out[:, n] = dot_of_parts(held, split(block)).reshape(groups, NZ // groups, EL)


def copies(source, target, nodes, done):
    step = -(-nodes // CHUNKS)
    cuts = [(at, min(step, nodes - at)) for at in range(0, nodes, step)]
    return [
        pltpu.make_async_copy(source.at[pl.ds(at, size)], target.at[pl.ds(at, size)], done.at[i])
        for i, (at, size) in enumerate(cuts)
    ]


def enter_kernel(forcing, coef_far, cell_far, planes, order, index, scale, stored, done, small, coef, cell):
    nodes = forcing.shape[0]
    fetched = [pltpu.make_async_copy(coef_far, coef, small.at[0]), pltpu.make_async_copy(cell_far, cell, small.at[1])]
    moved = copies(forcing, planes, nodes, done)
    for copy in fetched + moved:
        copy.start()
    planes[nodes:PADDED] = jnp.zeros((PADDED - nodes, planes.shape[1], EL), F32)
    for copy in fetched:
        copy.wait()
    lane = lax.broadcasted_iota(jnp.int32, (EL, EL), 1)
    elem = lax.broadcasted_iota(jnp.int32, (EL, EL), 0)
    cells = jnp.transpose(jnp.broadcast_to(cell[...], (EL, EL)))
    found = jnp.sum(jnp.where(cells == lane, elem, 0), axis=0, keepdims=True)
    order[...] = jnp.broadcast_to(found, (8, EL))
    index[...] = jnp.broadcast_to(cell[...], (8, EL))
    stored[...] = jnp.broadcast_to(coef[...], (8, EL))
    scale[...] = pick(jnp.broadcast_to(coef[...], (8, EL)), found)
    for copy in moved:
        copy.wait()


def leave_kernel(planes, velocity, done):
    moved = copies(planes, velocity, velocity.shape[0], done)
    for copy in moved:
        copy.start()
    for copy in moved:
        copy.wait()


def flipped(tile):
    back = (8 - lax.broadcasted_iota(jnp.int32, tile.shape, 0)) % 8
    return jnp.take_along_axis(tile, back, axis=0, mode="promise_in_bounds")


def both_ascending(values):
    return jnp.concatenate([values[0:16], flipped(values[16:24]), flipped(values[24:32])], 0)


def condense_kernel(spectral, order, scale, couple, condensed, down, up):
    lane = lax.broadcasted_iota(jnp.int32, (8, EL), 1)
    row, col, slot = lane // ELY, lane % ELY, lane // SLOT
    inner_row, inner_col = (row > 0, row < ELX - 1), (col > 0, col < ELY - 1)

    def messages(t):
        low, high = t[0], t[3]
        for i in (1, 2, 3):
            low = jnp.where(slot == i, pltpu.roll(t[i], SLOT * i, 1), low)
            high = jnp.where(slot == i - 1, pltpu.roll(t[i - 1], SLOT * i, 1), high)
        return low, high

    down[MODES], up[MODES] = messages([scale[...]] * 4)

    def mode(m, _):
        fields = spectral[pl.ds(m, PADDED, stride=MODES), :]
        value = fields[0:NB] - dot_of_parts(split(couple[m]), split(fields[NB:NODES]))
        t = tiles(both_ascending(pick(value, order[0:1])))
        t = add_columns(add_rows(t, ELY, *inner_row), *inner_col)
        condensed[m] = jnp.concatenate(t, 0)
        down[m], up[m] = messages(t)
        return 0

    lax.fori_loop(0, MODES, mode, 0, unroll=UNROLL)


def interior_kernel(spectral, stored, inner, couple, base, turned, wide):
    inverse = 1.0 / stored[0:1]

    def mode(m, _):
        within = spectral[pl.ds(NB * MODES + m, PADDED - NB, stride=MODES), :][0:NI]
        base[m, 0:NI] = dot(inner[pl.ds(m, NI, stride=MODES), :], within) * inverse
        return 0

    lax.fori_loop(0, MODES, mode, 0, unroll=UNROLL)
    wide[...] = jnp.zeros_like(wide)
    for q in range(MODES // QUAD):
        wide[:, 0:NI] = couple[QUAD * q : QUAD * q + QUAD].reshape(QUAD * NB, NI)
        turned[q] = jnp.transpose(wide[...])[0 : turned.shape[1]]


def columns_kernel(condensed, scale, low, high, table, left, right, middle):
    lane = lax.broadcasted_iota(jnp.int32, (8, EL), 1)
    slot = lane // SLOT
    inner, outer = slot == 0, slot == 1
    meets = (lane >= SLOT) & (lane < SLOT + ELY), (lane >= SLOT - ELY) & (lane < SLOT)

    def stack(own, lo, hi):
        first, second = [], []
        for i in range(4):
            moved = pltpu.roll(own[i], SLOT, 1)
            below = lo if i == 0 else pltpu.roll(lo, EL - SLOT * i, 1)
            above = hi if i == 1 else pltpu.roll(hi, (EL + SLOT - SLOT * i) % EL, 1)
            first.append(jnp.where(inner, below, moved))
            second.append(jnp.where(inner, moved, jnp.where(outer, above, 0.0)))
        return first, second

    def put(m, parts):
        for j, part in enumerate(parts):
            middle[m, :, EL * j : EL * j + EL] = jnp.concatenate(part, 0)

    put(MODES, stack([scale[...]] * 4, low[MODES], high[MODES]))

    def mode(m, _):
        parts = stack(tiles(condensed[m]), low[m], high[m])
        put(m, [add_rows(part, ELY, *meets) for part in parts])
        return 0

    lax.fori_loop(0, MODES, mode, 0, unroll=UNROLL)
    total = 0.0
    for i in range(4):
        send = selection(jnp.where(table[5:6] == i, table[2:3], -1), XL)
        total = total + take(middle[:, 8 * i : 8 * i + 8, :].reshape((MODES + 1) * 8, XL), send)
    left[...] = total[:, 0:EL].reshape(MODES + 1, 8, EL)
    right[...] = total[:, EL:XL].reshape(MODES + 1, 8, EL)


def middle_kernel(middle, table, block):
    spread = take(middle[...].reshape((MODES + 1) * NB, XL), selection(table[0:1], XL))
    block[...] = spread.reshape(MODES + 1, NB, XL)


def matrices_kernel(schur, matrix, shift):
    lane = lax.broadcasted_iota(jnp.int32, (NB, NB), 1)
    eye = lax.broadcasted_iota(jnp.int32, (NB, NB), 0) == lane
    across = jnp.where((lane >= 16) & (lane % 8 > 0), lane // 8 * 8 + 8 - lane % 8, lane)

    def mode(m, _):
        trace = jnp.sum(jnp.sum(jnp.where(eye, schur[m], 0.0), axis=0, keepdims=True), axis=1, keepdims=True)
        shift[m] = jnp.broadcast_to((0.5 * NB) / trace, (8, XL))
        rows = both_ascending(schur[m])
        parts = three_parts(jnp.take_along_axis(rows, across, axis=1, mode="promise_in_bounds"))
        for k, (part, _) in enumerate(TERMS):
            matrix[m, :, NB * k : NB * k + NB] = parts[part]
        return 0

    lax.fori_loop(0, MODES, mode, 0, unroll=UNROLL)


def krylov_kernel(
    block, left, right, schur, shift, table, basis, sums, keep_ref, weight_ref, mine_ref, parts, state, applied, spread
):
    sides = jnp.concatenate([left[...].reshape((MODES + 1) * 8, EL), right[...].reshape((MODES + 1) * 8, EL)], 1)
    for i in range(4):
        turn = selection(jnp.where(table[1:2] < 0, -1, table[1:2] + SLOT * i), XL)
        spread[:, 8 * i : 8 * i + 8, :] = take(sides, turn).reshape(MODES + 1, 8, XL)

    row, col = jnp.broadcast_to(table[3:4], (8, XL)), jnp.broadcast_to(table[4:5], (8, XL))
    grid_row = row - DEEP + lax.axis_index("ex") * ELX
    grid_col = col - DEEP + lax.axis_index("ey") * ELY
    last_row, last_col = lax.axis_size("ex") * ELX - 1, lax.axis_size("ey") * ELY - 1
    inside = (grid_row >= 0) & (grid_row <= last_row) & (grid_col >= 0) & (grid_col <= last_col) & (row < XROWS)
    own = (row >= DEEP) & (row < DEEP + ELX) & (col >= DEEP) & (col < DEEP + ELY)
    meets = (col == DEEP) | (col == DEEP + ELY), (col == DEEP - 1) | (col == DEEP + ELY - 1)
    mine_ref[...] = jnp.where(own, 1.0, 0.0).astype(F32)
    corner = lax.broadcasted_iota(jnp.int32, (8, XL), 0) == 0
    low_row, high_row, low_col, high_col = grid_row == 0, grid_row == last_row, grid_col == 0, grid_col == last_col
    for tile, (edge, other) in enumerate(((low_col, low_row), (high_row, low_col), (high_col, high_row), (low_row, high_col))):
        keep = jnp.where(inside & ~(edge | (corner & other)), 1.0, 0.0).astype(F32)
        keep_ref[8 * tile : 8 * tile + 8] = keep
        weight_ref[8 * tile : 8 * tile + 8] = jnp.where(own, keep * jnp.where(corner, 0.25, 0.5), 0.0).astype(F32)
    scale = jnp.where(inside[0:1], block[MODES, 0:1] + spread[MODES, 0:1], 0.0)

    def assemble(values):
        return keep_ref[...] * jnp.concatenate(add_columns(add_rows(tiles(values), PITCH, None, None), None, None), 0)

    def image(m, values):
        parts_of = three_parts(values)
        stacked = jnp.concatenate([parts_of[part] for _, part in TERMS], 0)
        return scale * lax.dot_general(schur[m], stacked, (((1,), (0,)), ((), ())), preferred_element_type=F32)

    def gather_mode(m):
        values = block[m] + spread[m]
        state[0, m] = keep_ref[...] * jnp.concatenate(add_columns(tiles(values), *meets), 0)

    def extend_mode(i):
        def run(m):
            images = image(m, state[i, m])
            applied[i, m] = images
            state[i + 1, m] = assemble(images) * shift[m, 0:1] - state[i, m]

        return run

    def sum_mode(m):
        v = [state[i, m] for i in range(3)]
        w = [applied[0, m], applied[1, m], image(m, v[2])]
        weight, mine = weight_ref[...], mine_ref[0:1]
        weighted = v[1] * weight
        own = [value * mine for value in v]
        k = 0
        for first, second in (
            (v[0], v[0] * weight), (v[0], weighted), (v[1], weighted),
            (own[0], w[0]), (own[1], w[0]), (own[1], w[1]), (own[2], w[1]), (own[2], w[2]),
        ):
            whole = jnp.sum(first * second, axis=0, keepdims=True)
            parts[pl.ds(MODES * k + m, 1), :] = whole[:, 0:EL] + whole[:, EL:XL]
            k += 1
        for i in range(3):
            basis[i, m] = v[i]

    def every(body):
        def step(m, _):
            body(m)
            return 0

        lax.fori_loop(0, MODES, step, 0, unroll=UNROLL)

    every(gather_mode)
    for i in range(2):
        every(extend_mode(i))
    every(sum_mode)
    ones = jnp.ones((8, EL), F32)
    total = lax.dot_general(ones, parts[...], (((1,), (1,)), ((), ())), precision=HIGHEST, preferred_element_type=F32)
    for at in range(0, sums.shape[0], 8):
        sums[at : at + 8] = total


def finish_kernel(gathered, basis, base, couple, cell, out, coefs, blocks):
    total = jnp.broadcast_to(jnp.sum(gathered[...].reshape(-1, EL), axis=0, keepdims=True), (8, EL))
    b0, b1, b2, h0, h1, h2, h3, h4 = [
        total if k == 0 else pltpu.roll(total, EL - MODES * k, 1) for k in range(8)
    ]
    tiny = 2e-7
    l1, l2 = h1 / h0, h2 / h0
    d1 = h2 - l1 * h1
    ok1 = d1 > tiny * h2
    d1 = jnp.where(ok1, d1, 1.0)
    l12 = jnp.where(ok1, (h3 - l1 * h2) / d1, 0.0)
    d2 = h4 - l2 * h2 - l12 * l12 * d1
    ok2 = d2 > tiny * h4
    y1 = b1 - l1 * b0
    y2 = b2 - l2 * b0 - l12 * y1
    c2 = jnp.where(ok2, y2 / jnp.where(ok2, d2, 1.0), 0.0)
    c1 = jnp.where(ok1, y1 / d1, 0.0) - l12 * c2
    c0 = b0 / h0 - l1 * c1 - l2 * c2
    for i, c in enumerate((c0, c1, c2)):
        coefs[i] = jnp.transpose(jnp.broadcast_to(c[0:1], (EL, EL)))[0:MODES]
    place = (cell[0:1] // ELY + DEEP) * PITCH + cell[0:1] % ELY + DEEP

    chosen = selection(place, XL)
    blocks[...] = jnp.zeros_like(blocks)
    for q in range(MODES // QUAD):
        mixed = []
        for r in range(QUAD):
            m = QUAD * q + r
            c = [jnp.concatenate([coefs[i, m : m + 1, :]] * 2, 1) for i in range(3)]
            x = c[0] * basis[0, m] + c[1] * basis[1, m] + c[2] * basis[2, m]
            mixed.append(both_ascending(x))
        solved = take(jnp.concatenate(mixed, 0), chosen)
        for r in range(QUAD):
            x = solved[r * NB : r * NB + NB]
            blocks[q, NB * r : NB * r + NB, EL * r : EL * r + EL] = x
            for tile in range(4):
                out[pl.ds(8 * tile * MODES + QUAD * q + r, 8, stride=MODES), :] = x[8 * tile : 8 * tile + 8]
        lifted = dot_of_parts(split(couple[q]), split(blocks[q]))
        for r in range(QUAD):
            m = QUAD * q + r
            within = base[m, 0:NI] - lifted[0:NI, EL * r : EL * r + EL]
            within = jnp.concatenate([within, jnp.zeros((PADDED - NODES, EL), F32)], 0)
            out[pl.ds(NB * MODES + m, PADDED - NB, stride=MODES), :] = within


def call(kernel, shapes=(), scratch=(), far=0, far_out=None):
    def run(*operands):
        many = isinstance(shapes, list)
        outs = [s if isinstance(s, pl.MemoryRef) else pltpu.VMEM(s, F32) for s in (shapes if many else [shapes])]
        whole, away = pl.BlockSpec(memory_space=pltpu.VMEM), pl.BlockSpec(memory_space=pl.ANY)
        near = tuple(pltpu.with_memory_space_constraint(o, pltpu.VMEM) for o in operands[far:])
        if far_out:
            outs = [jax.ShapeDtypeStruct(far_out, F32)]
        specs = [away if far_out else whole] * len(outs)
        return pl.pallas_call(
            kernel,
            out_shape=outs if many else outs[0],
            in_specs=[away] * far + [whole] * len(near),
            out_specs=specs if many else specs[0],
            scratch_shapes=list(scratch),
            compiler_params=pltpu.CompilerParams(vmem_limit_bytes=16 << 20),
            name=kernel.__name__,
        )(*(pltpu.with_memory_space_constraint(o, pltpu.HBM) for o in operands[:far]), *near)

    return run


def swap(array):
    return lax.all_to_all(array, "fourier", split_axis=0, concat_axis=0, tiled=True)


def ring(axis, step):
    count = lax.axis_size(axis)
    return [(i, (i + step) % count) for i in range(count)]


def neighbours(to_low, to_high, axis):
    return lax.ppermute(to_high, axis, ring(axis, 1)), lax.ppermute(to_low, axis, ring(axis, -1))


def on_device(forcing, element_coef, schur, couple, inner_inv, element_cell):
    parts = lax.axis_size("fourier")
    devices = lax.axis_size("ex") * lax.axis_size("ey")
    group = PADDED // parts
    table = jnp.asarray(real_transform())
    exchanged = (parts, group, MODES, EL)
    lanes = (8, EL)
    ints = pltpu.VMEM(lanes, jnp.int32)

    planes, order, index, scale, stored = call(
        enter_kernel, [(PADDED, MODES, EL), ints, ints, lanes, lanes],
        [
            pltpu.SemaphoreType.DMA((CHUNKS,)),
            pltpu.SemaphoreType.DMA((2,)),
            pltpu.VMEM((1, EL), F32),
            pltpu.VMEM((1, EL), jnp.int32),
        ],
        far=3,
    )(jnp.transpose(forcing, (1, 0, 2)), element_coef.reshape(1, EL), element_cell.reshape(1, EL))
    planes = swap(planes).reshape(exchanged)
    spectral = swap(call(transform_kernel, exchanged)(table, planes).reshape(PADDED, MODES, EL))
    spectral = spectral.reshape(PADDED * MODES, EL)

    message, extended = (MODES + 1, 8, EL), (MODES + 1, NB, XL)
    table_of_lanes = jnp.asarray(lane_tables())
    condensed, down, up = call(condense_kernel, [(MODES, NB, EL), message, message])(spectral, order, scale, couple)
    low, high = neighbours(down, up, "ex")
    base, turned = call(
        interior_kernel, [(MODES, 56, EL), (MODES // QUAD, 56, QUAD * NB)], [pltpu.VMEM((QUAD * NB, EL), F32)]
    )(spectral, stored, jnp.transpose(inner_inv, (1, 0, 2)).reshape(NI * MODES, NI), couple)
    low, high, base, turned, schur = lax.optimization_barrier((low, high, base, turned, schur))
    left, right, middle = call(columns_kernel, [message, message, extended])(
        condensed, scale, low, high, table_of_lanes
    )
    left, right = neighbours(left, right, "ey")
    matrix, shift = call(
        matrices_kernel, [pltpu.VMEM((MODES, NB, len(TERMS) * NB), jnp.bfloat16), (MODES, 8, XL)]
    )(schur)
    block = call(middle_kernel, extended)(middle, table_of_lanes)
    basis, sums = call(
        krylov_kernel,
        [(3, MODES, NB, XL), (devices, EL)],
        [
            pltpu.VMEM((NB, XL), F32),
            pltpu.VMEM((NB, XL), F32),
            pltpu.VMEM((8, XL), F32),
            pltpu.VMEM((EL, EL), F32),
            pltpu.VMEM((3, MODES, NB, XL), F32),
            pltpu.VMEM((2, MODES, NB, XL), F32),
            pltpu.VMEM(extended, F32),
        ],
    )(block, left, right, matrix, shift, table_of_lanes)
    gathered = lax.all_to_all(sums.reshape(devices, 1, EL), ("ex", "ey"), split_axis=0, concat_axis=0, tiled=True)
    modal = call(finish_kernel, (PADDED * MODES, EL), [pltpu.VMEM((3, MODES, EL), F32), pltpu.VMEM((MODES // QUAD, QUAD * NB, QUAD * EL), F32)])(
        gathered, basis, base, turned, index
    )
    modal = swap(modal.reshape(PADDED, MODES, EL)).reshape(exchanged)
    velocity = swap(call(transform_kernel, exchanged)(table.T, modal).reshape(PADDED, MODES, EL))
    velocity = call(leave_kernel, far_out=(NODES, MODES, EL), scratch=[pltpu.SemaphoreType.DMA((CHUNKS,))])(velocity)
    return jnp.transpose(velocity, (1, 0, 2))


def solution(mesh):
    placed = (
        P("fourier", None, ("ex", "ey")),
        P(("ex", "ey")),
        P("fourier", None, None),
        P("fourier", None, None),
        P("fourier", None, None),
        P(("ex", "ey")),
    )
    return jax.shard_map(
        on_device,
        mesh=mesh,
        in_specs=placed,
        out_specs=P("fourier", None, ("ex", "ey")),
        check_vma=False,
    )
```
